768 devices in a mesh: gx: 32 (over x, z_lo, core), gy: 3 (over z_hi), gz: 8 (over y).
Axes of the slice: x: 4, y: 8, z: 12 (z_hi: 3, z_lo: 4; z = z_hi * 4 + z_lo), core: 2. Of those that a mesh axis runs over, the one named last changes fastest.
Arguments:
- energy: float32 [192, 36, 1536], P('gx', 'gy', 'gz'), may hold values from 0.5 to 18, as said below
- density: float32 [64, 12, 512], P('gx', 'gy', 'gz'), may hold values from 0.125 to 1
- region: int32 [64, 12, 512], P('gx', 'gy', 'gz'), may hold values from 0 to 2
- gamma_table: float32 [3], replicated, may hold values from 1.3 to 1.9
Outputs:
- acceleration: float32 [3, 128, 24, 1024], P(None, 'gx', 'gy', 'gz')
- residual: float32 [3, 128, 24, 1024], P(None, 'gx', 'gy', 'gz')
The draws below stay inside these ranges and needn't reach their ends.
Inputs may be any that keep to these rules, and one draw needn't show every extreme that they name: energy is positive.
All inputs are finite; a program needn't handle non-finite values.
Results may differ from the reference program's by a relative error of at most 0.0001.
Values sent between devices are 32-bit elements; how exact they have to be, the bound alone decides.
No kernel may reach another device: no remote copies, remote signals or barrier semaphores. Data moves between devices by JAX's collectives and lax.ppermute only.
A program may use at most 32 MiB of HBM per device.

```python
import math
import jax
import jax.numpy as jnp
from jax import lax

ITERS = 2
MATERIAL_ZONES = 3
ELEMENTS_X = 64
ELEMENTS_Y = 12
ELEMENTS_Z = 512


def draw_energy(key, part):
    shape_values = (3 * ELEMENTS_X, 3 * ELEMENTS_Y, 3 * ELEMENTS_Z)
    first = jax.random.fold_in(jax.random.fold_in(key, 17), 0)
    along_x = 1.0 + 2.0 * jnp.arange(3 * ELEMENTS_X, dtype=jnp.float32) / (3 * ELEMENTS_X - 1)
    logs = jax.random.uniform(first, shape_values, jnp.float32, jnp.log(0.5), jnp.log(2.0))
    outcome_field = jnp.exp(logs) * along_x[:, None, None]
    return outcome_field.astype(jnp.float32)


def touch_ends(entries, own_key, least, top_value):
    extent = entries.shape
    place = [jax.random.randint(jax.random.fold_in(own_key, axis), (), 0, extent[axis]) for axis in range(len(extent))]
    entries = entries.at[tuple(place)].set(least)
    longest = extent.index(max(extent))
    place[longest] = (place[longest] + 1) % extent[longest]
    return entries.at[tuple(place)].set(top_value)


def steps_of(key, extent, shards, low, top_value):
    gain = 1.0
    for position, blocks in shards:
        steps = jax.random.uniform(jax.random.fold_in(jax.random.fold_in(key, 6), position), (blocks,), jnp.float32, low / len(shards), top_value / len(shards))
        gain = gain * jnp.repeat(jnp.exp(steps), extent[position] // blocks).reshape((-1,) + (1,) * (len(extent) - 1 - position))
    return gain


def setup_inputs(seed: int = 0) -> dict:
    key_list = jax.random.split(jax.random.key(seed), 5)
    energy = draw_energy(jax.random.fold_in(key_list[4], 71), 0)
    density = jnp.clip(jnp.exp(math.log(1.0) - 2.0794415 * jax.random.uniform(key_list[1], (ELEMENTS_X, ELEMENTS_Y, ELEMENTS_Z), jnp.float32) ** steps_of(key_list[1], (ELEMENTS_X, ELEMENTS_Y, ELEMENTS_Z), ((0, 32), (1, 3), (2, 8)), -0.2, 0.2)), 0.125, 1.0)
    region = touch_ends(jax.random.randint(key_list[2], (ELEMENTS_X, ELEMENTS_Y, ELEMENTS_Z), 0, MATERIAL_ZONES), jax.random.fold_in(key_list[2], 1), 0, MATERIAL_ZONES - 1).astype(jnp.int32)
    gamma_table = jnp.clip(jax.random.uniform(key_list[3], (MATERIAL_ZONES,), jnp.float32, 1.3, 1.9), 1.3, 1.9)
    return {"energy": energy, "density": density, "region": region, "gamma_table": gamma_table}


WEIGHTS = [5.0 / 18.0, 8.0 / 18.0, 5.0 / 18.0]

def line_tables():
    root = math.sqrt(0.15)
    spots = [0.5 - root, 0.5, 0.5 + root]
    values = [[2.0 * (spot - 0.5) * (spot - 1.0), -4.0 * spot * (spot - 1.0), 2.0 * spot * (spot - 0.5)] for spot in spots]
    slopes = [[4.0 * spot - 3.0, -8.0 * spot + 4.0, 4.0 * spot - 1.0] for spot in spots]
    return (values, slopes)

def to_points(field, axis, table):
    count = (field.shape[axis] - 1) // 2
    parts = [lax.slice_in_dim(field, offset, offset + 2 * count - 1, 2, axis) for offset in range(3)]
    rows = [table[member][0] * parts[0] + table[member][1] * parts[1] + table[member][2] * parts[2] for member in range(3)]
    joined = jnp.stack(rows, axis=axis + 1)
    shape_values = list(field.shape)
    shape_values[axis] = 3 * count
    return joined.reshape(shape_values)

def to_nodes(points, axis, table):
    count = points.shape[axis] // 3
    shape_values = list(points.shape)
    grouped = points.reshape(shape_values[:axis] + [count, 3] + shape_values[axis + 1:])
    parts = [lax.index_in_dim(grouped, member, axis + 1, keepdims=False) for member in range(3)]
    terms = [table[0][offset] * parts[0] + table[1][offset] * parts[1] + table[2][offset] * parts[2] for offset in range(3)]
    widths_end = [(0, 0)] * len(shape_values)
    widths_end[axis] = (0, 1)
    widths_front = [(0, 0)] * len(shape_values)
    widths_front[axis] = (1, 0)
    evens = jnp.pad(terms[0], widths_end) + jnp.pad(terms[2], widths_front)
    woven = jnp.stack([lax.slice_in_dim(evens, 0, count, 1, axis), terms[1]], axis=axis + 1)
    shape_two = list(terms[1].shape)
    shape_two[axis] = 2 * count
    woven = woven.reshape(shape_two)
    return jnp.concatenate([woven, lax.slice_in_dim(evens, count, count + 1, 1, axis)], axis=axis)

def mass_apply(nodes, coef):
    values, slopes = line_tables()
    points = to_points(to_points(to_points(nodes, 0, values), 1, values), 2, values)
    points = points * coef
    return to_nodes(to_nodes(to_nodes(points, 2, values), 1, values), 0, values)

def force_contributions(pressure_weighted):
    values, slopes = line_tables()
    force_x = to_nodes(to_nodes(to_nodes(pressure_weighted, 0, slopes), 1, values), 2, values)
    force_y = to_nodes(to_nodes(to_nodes(pressure_weighted, 0, values), 1, slopes), 2, values)
    force_z = to_nodes(to_nodes(to_nodes(pressure_weighted, 0, values), 1, values), 2, slopes)
    return jnp.stack([force_x, force_y, force_z])

def expand(values):
    return jnp.repeat(jnp.repeat(jnp.repeat(values, 3, 0), 3, 1), 3, 2)

def lookup(region, gamma_table):
    gamma_elem = jnp.zeros(region.shape, gamma_table.dtype)
    for index in range(MATERIAL_ZONES):
        gamma_elem = gamma_elem + jnp.where(region == index, gamma_table[index], 0.0)
    return gamma_elem

def reference(energy, density, region, gamma_table):
    line_entries = jnp.array(WEIGHTS, energy.dtype)
    quadrature_weights = jnp.tile(line_entries, ELEMENTS_X)[:, None, None] * jnp.tile(line_entries, ELEMENTS_Y)[None, :, None] * jnp.tile(line_entries, ELEMENTS_Z)[None, None, :]
    gamma_elem = lookup(region, gamma_table)
    pressure_weighted = expand((gamma_elem - 1.0) * density) * energy * quadrature_weights
    coef = expand(density) * quadrature_weights
    mask_x = (jnp.arange(2 * ELEMENTS_X) != 0).astype(energy.dtype)
    mask_y = (jnp.arange(2 * ELEMENTS_Y) != 0).astype(energy.dtype)
    depth_mask = (jnp.arange(2 * ELEMENTS_Z) != 0).astype(energy.dtype)
    boundary_mask = (mask_x[:, None, None] * mask_y[None, :, None] * depth_mask[None, None, :])[None]
    corner_force = force_contributions(pressure_weighted)[:, :2 * ELEMENTS_X, :2 * ELEMENTS_Y, :2 * ELEMENTS_Z] * boundary_mask

    def operate(field):
        padded = jnp.pad(field, ((0, 0), (0, 1), (0, 1), (0, 1)))

        def single(nodes):
            return mass_apply(nodes, coef)
        outcome_field = lax.map(single, padded)
        return outcome_field[:, :2 * ELEMENTS_X, :2 * ELEMENTS_Y, :2 * ELEMENTS_Z] * boundary_mask
    solution = jnp.zeros_like(corner_force)
    residual = corner_force
    direction = corner_force
    norm_now = lax.optimization_barrier(jnp.sum(residual * residual, axis=(1, 2, 3)))
    for step in range(ITERS):
        image = operate(direction)
        alpha = norm_now / lax.optimization_barrier(jnp.sum(direction * image, axis=(1, 2, 3)))
        solution = solution + alpha[:, None, None, None] * direction
        residual = residual - alpha[:, None, None, None] * image
        norm_next = lax.optimization_barrier(jnp.sum(residual * residual, axis=(1, 2, 3)))
        direction = residual + (norm_next / norm_now)[:, None, None, None] * direction
        norm_now = norm_next
    return (solution, residual)
```

```python
import functools
import math

import jax
import jax.numpy as jnp
from jax import lax
from jax.experimental import pallas as pl
from jax.experimental.pallas import tpu as pltpu
from jax.sharding import Mesh
from jax.sharding import PartitionSpec as P

LOW, HIGH = 3, 2
PAIRS = 14
ROOT = math.sqrt(0.15)
EDGE_W, MID_W = 5.0 / 18.0, 8.0 / 18.0
EXACT = lax.Precision.HIGHEST
GX = ("gx0", "gx1", "gx2")


def vmem(count):
    return [pl.BlockSpec(memory_space=pltpu.VMEM)] * count


def iota(shape, dim):
    return lax.broadcasted_iota(jnp.int32, shape, dim)


def class_of(q, qz):
    if qz < 2:
        return q, qz
    return (q + 9, 0) if q < 5 else (q + 4, 1)


def prepare(energy, density, region, gamma, rows_out, message_out, spread, lines):
    for point in range(6):
        spread[16 * point : 16 * point + 12, :] = energy[point]
    row, col = iota((192, 256), 0), iota((192, 256), 1)
    pick = (row == 3 * (col % 64) + jnp.minimum(col // 64, 2)).astype(jnp.float32)
    lines[...] = jnp.dot(
        spread[...], pick, precision=EXACT, preferred_element_type=jnp.float32
    )
    rho = density[...]
    zone = region[...]
    table = jnp.zeros_like(rho)
    for index in range(3):
        table = table + jnp.where(zone == index, gamma[index], 0.0)
    scale = (table - 1.0) * rho
    scale = jnp.concatenate([scale, scale], axis=-1)
    rho = jnp.concatenate([rho, rho], axis=-1)
    low_half = iota((1, 128), 1) < 64
    pair, lane = iota((16, 128), 0), iota((16, 128), 1)
    real = pair < PAIRS
    start = (lane + 128 - 3 * pair) % 128
    keep_one = real & ((start >= 125) | ((start >= 64) & (start <= 65)))
    keep_zero = real & (((start >= 61) & (start <= 63)) | (start < 2))
    for x in range(2):
        for y in range(4):
            factor = scale[x, y : y + 1]
            parts = []
            tails = []
            for qx in range(3):
                at = (3 * x + qx) * 16 + 3 * y
                parts.append(lines[at : at + 3, 0:128] * factor)
                tails.append(lines[at : at + 3, 128:256] * factor)
            tail = [tails[q // 3][q % 3 : q % 3 + 1] for q in range(9)] + [rho[x, y : y + 1]]
            for i in range(5):
                parts.append(jnp.where(low_half, tail[i], tail[i + 5]))
            parts.append(jnp.zeros((2, 128), jnp.float32))
            base = 16 * x
            block = jnp.concatenate(parts, axis=0)
            rows_out[y, base : base + 16, :] = block
            turned = pltpu.roll(block, 0, 1, stride=3, stride_axis=0)
            zero = jnp.sum(jnp.where(keep_zero, turned, 0.0), axis=0, keepdims=True)
            one = jnp.sum(jnp.where(keep_one, turned, 0.0), axis=0, keepdims=True)
            place = y * 4 + x * 2
            message_out[place : place + 1, :] = pltpu.roll(zero, 64, 1)
            message_out[place + 1 : place + 2, :] = one


def fill_z(rows, from_low, from_high, rows_out, up_out, down_out):
    lane = iota((16, 128), 1)
    halo = jnp.where((lane < 50) | (lane >= 110), from_low[...], from_high[...])
    for y in range(4):
        for x in range(2):
            base = 16 * x
            place = y * 4 + x * 2
            block = rows[y, base : base + 16, :]
            block = jnp.concatenate([block[:PAIRS], halo[place : place + 2]], axis=0)
            rows_out[y, base : base + 16, :] = block
            if y >= 1:
                up_out[y - 1, base : base + 16, :] = block
            if y < HIGH:
                down_out[y, base : base + 16, :] = block


def fill_y(rows, from_low, from_high, rows_out, last_out):
    for y in range(9):
        if y < LOW:
            block = from_low[y]
        elif y < LOW + 4:
            block = rows[y - LOW]
        else:
            block = from_high[y - LOW - 4]
        rows_out[y] = block
        last_out[y] = block[16:32]


def element_op(v, m, w):
    total, gap = v + w, v - w
    outer = 0.75 * total + m
    inner = 1.25 * gap
    return outer + inner, total + 8.0 * m, outer - inner


def by_values(q0, q1, q2):
    total, gap = q0 + q2, q0 - q2
    outer = (0.3 * EDGE_W) * total
    inner = (ROOT * EDGE_W) * gap
    return outer + inner, (0.4 * EDGE_W) * total + MID_W * q1, outer - inner


def by_slopes(q0, q1, q2):
    total, gap = q0 + q2, q0 - q2
    outer = EDGE_W * total + MID_W * q1
    inner = (4.0 * ROOT * EDGE_W) * gap
    return -outer - inner, 2.0 * inner, outer - inner


def up_z(value):
    return pltpu.roll(value, 1, 1)


def down_z(value):
    return pltpu.roll(value, 127, 1)


def up_x(value):
    return pltpu.roll(value, 1, 0)


def down_x(value):
    return pltpu.roll(value, 7, 0)


def krylov(sizes, own, far, near, above, fields_out, sums_out, points, base, image, second, flat):
    size_x, size_y, size_z = sizes
    index_x = (lax.axis_index(GX[0]) * lax.axis_size(GX[1]) + lax.axis_index(GX[1])) * (
        lax.axis_size(GX[2])
    ) + lax.axis_index(GX[2])
    zeros = jnp.zeros((16, 128), jnp.float32)
    for y in range(9):
        sources = [
            far[y],
            near[y, 0:16],
            near[y, 16:32],
            own[y, 0:16],
            own[y, 16:32],
            above[y, 0:16],
            above[y, 16:32],
            zeros,
        ]
        for s in range(8):
            points[pl.ds(y * 128 + s, 16, stride=8), :] = sources[s]

    sub, lane = iota((8, 128), 0), iota((8, 128), 1)
    at_x = 2 * index_x + sub - LOW
    at_z = 64 * lax.axis_index("gz") + jnp.where(lane < 96, lane, lane - 128)
    inside_x = (at_x > 0) & (at_x < size_x)
    inside_z = (at_z > 0) & (at_z < size_z)
    inside = {
        (0, 0): (inside_x & inside_z).astype(jnp.float32),
        (0, 1): inside_x.astype(jnp.float32),
        (1, 0): inside_z.astype(jnp.float32),
    }
    first_y = 4 * lax.axis_index("gy") - LOW
    mine = lane < 64

    def inside_y(y):
        at = first_y + y
        return ((at > 0) & (at < size_y)).astype(jnp.float32)

    def tile(ref, d, yc, xc, zc, y):
        row = (((d * 2 + yc) * 4 + xc * 2 + zc) * 9 + y) * 8
        return ref.at[pl.ds(pl.multiple_of(row, 8), 8), :]

    def point(y, p, h):
        main = points[pl.ds(pl.multiple_of(y * 128 + p * 8, 8), 8), :]
        side = points[pl.ds(pl.multiple_of(y * 128 + (PAIRS + h) * 8, 8), 8), :]
        if h:
            main = pltpu.roll(main, 64, 1)
        if p:
            side = pltpu.roll(side, 128 - 3 * p, 1)
        return jnp.where(mine, main, side)

    def put(ref, d, xc, zc, y, vertex, middle, wall):
        if (xc, zc) in inside:
            vertex = vertex * inside[xc, zc]
            middle = middle * inside[xc, zc]
        tile(ref, d, 0, xc, zc, y)[...] = vertex * wall
        tile(ref, d, 1, xc, zc, y)[...] = middle

    def force_row(y, carry):
        wall = inside_y(y)
        value_z, slope_z = {}, {}
        for q in range(9):
            q0, q1, q2 = (point(y, *class_of(q, qz)) for qz in range(3))
            n0, n1, n2 = by_values(q0, q1, q2)
            value_z[q, 0], value_z[q, 1] = n0 + up_z(n2), n1
            n0, n1, n2 = by_slopes(q0, q1, q2)
            slope_z[q, 0], slope_z[q, 1] = n0 + up_z(n2), n1
        kept = []
        for d in range(3):
            source = slope_z if d == 2 else value_z
            op_x = by_slopes if d == 0 else by_values
            op_y = by_slopes if d == 1 else by_values
            lines = {}
            for qy in range(3):
                for zc in range(2):
                    n0, n1, n2 = op_x(*(source[3 * qx + qy, zc] for qx in range(3)))
                    lines[qy, 0, zc], lines[qy, 1, zc] = n0 + up_x(n2), n1
            for xc in range(2):
                for zc in range(2):
                    n0, n1, n2 = op_y(*(lines[qy, xc, zc] for qy in range(3)))
                    put(base, d, xc, zc, y, n0 + carry[len(kept)], n1, wall)
                    kept.append(n2)
        return tuple(kept)

    blank = jnp.zeros((8, 128), jnp.float32)
    lax.fori_loop(0, 9, force_row, (blank,) * 12)

    def mass_row(d, y, source, target, carry, rho):
        wall = inside_y(y)
        locals_y = {}
        for xc in range(2):
            for zc in range(2):
                got = element_op(
                    tile(source, d, 0, xc, zc, y)[...],
                    tile(source, d, 1, xc, zc, y)[...],
                    tile(source, d, 0, xc, zc, y + 1)[...],
                )
                for k in range(3):
                    locals_y[k, xc, zc] = got[k]
        kept = [None] * 4
        out = {}
        for k in range(3):
            lines = {}
            for xc in range(2):
                v, m = locals_y[k, xc, 0], locals_y[k, xc, 1]
                got = element_op(v, m, down_z(v))
                for j in range(3):
                    lines[j, xc] = got[j]
            joined = {}
            for j in range(3):
                v, m = lines[j, 0], lines[j, 1]
                n0, n1, n2 = (rho * n for n in element_op(v, m, down_x(v)))
                joined[j, 0], joined[j, 1] = n0 + up_x(n2), n1
            for xc in range(2):
                out[k, xc, 0] = joined[0, xc] + up_z(joined[2, xc])
                out[k, xc, 1] = joined[1, xc]
        for xc in range(2):
            for zc in range(2):
                slot = 2 * xc + zc
                put(target, d, xc, zc, y, out[0, xc, zc] + carry[slot], out[1, xc, zc], wall)
                kept[slot] = out[2, xc, zc]
        return tuple(kept)

    def mass(source, target, start, stop):
        def step(y, carry):
            rho = point(y, 13, 1) * (1.0 / 3375.0)
            kept = ()
            for d in range(3):
                kept += mass_row(d, y, source, target, carry[4 * d : 4 * d + 4], rho)
            return kept

        lax.fori_loop(start, stop, step, (blank,) * 12)

    mass(base, image, 1, 8)
    mass(image, second, 2, 7)

    owned = mine & (sub >= LOW) & (sub < LOW + 2)
    row, col = iota((8, 128), 0), iota((8, 128), 1)
    sums = jnp.zeros((8, 128), jnp.float32)
    for d in range(3):
        totals = [blank] * 4
        for yc in range(2):
            for xc in range(2):
                for zc in range(2):
                    for y in range(LOW, LOW + 4):
                        v0 = tile(base, d, yc, xc, zc, y)[...]
                        v1 = tile(image, d, yc, xc, zc, y)[...]
                        v2 = tile(second, d, yc, xc, zc, y)[...]
                        totals[0] = totals[0] + v0 * v0
                        totals[1] = totals[1] + v0 * v1
                        totals[2] = totals[2] + v1 * v1
                        totals[3] = totals[3] + v1 * v2
        for k in range(4):
            total = jnp.sum(jnp.where(owned, totals[k], 0.0), keepdims=True)
            sums = sums + jnp.where((row == k) & (col == d), total, 0.0)
    sums_out[...] = sums

    mine_row = iota((4, 128), 1) < 64
    for f, ref in enumerate((base, image, second)):
        for d in range(3):
            for yc in range(2):
                for xc in range(2):
                    for x in range(2):
                        got = []
                        for zc in range(2):
                            at = (((d * 2 + yc) * 4 + xc * 2 + zc) * 9 + LOW) * 8 + LOW + x
                            got.append(ref[pl.ds(at, 4, stride=8), :])
                        line = jnp.where(mine_row, got[0], pltpu.roll(got[1], 64, 1))
                        place = ((f * 3 + d) * 4 + 2 * x + xc) * 8 + yc
                        flat[pl.ds(place, 4, stride=2), :] = line
    row, col = iota((128, 128), 0), iota((128, 128), 1)
    weave = (row == (col % 2) * 64 + col // 2).astype(jnp.float32)
    fields_out[...] = jnp.dot(
        flat[...], weave, precision=EXACT, preferred_element_type=jnp.float32
    )


def combine(fields, sums, acceleration_out, residual_out):
    for d in range(3):
        c0, c1, c2, c3 = (sums[k : k + 1, d : d + 1] for k in range(4))
        alpha = c0 / c1
        norm = c0 - 2.0 * alpha * c1 + alpha * alpha * c2
        beta = norm / c0
        grow = 1.0 + beta
        alpha_2 = norm / (grow * grow * c1 - 2.0 * alpha * grow * c2 + alpha * alpha * c3)
        v0, v1, v2 = (fields[96 * f + 32 * d : 96 * f + 32 * d + 32, :] for f in range(3))
        direction = (v0 - alpha * v1) + beta * v0
        image = grow * v1 - alpha * v2
        acceleration_out[32 * d : 32 * d + 32, :] = alpha * v0 + alpha_2 * direction
        residual_out[32 * d : 32 * d + 32, :] = (v0 - alpha * v1) - alpha_2 * image


def moved(value, axis, by):
    count = lax.axis_size(axis)
    pairs = [(i, i + by) for i in range(count) if 0 <= i + by < count]
    return lax.ppermute(value, axis, pairs)


def shape(*dims):
    return jax.ShapeDtypeStruct(dims, jnp.float32)


def call(body, outs, count, scratch=(), specs=None):
    return pl.pallas_call(
        body,
        out_shape=outs,
        in_specs=specs or vmem(count),
        out_specs=tuple(vmem(len(outs))),
        scratch_shapes=[pltpu.VMEM(dims, jnp.float32) for dims in scratch],
    )


def total_over(value):
    for axis in (("gx2",), ("gx1",), ("gx0",), ("gy",), ("gz",)):
        value = lax.psum(value, axis)
    return value


def on_device(sizes, energy, density, region, gamma_table):
    rows, message = call(
        prepare,
        (shape(4, 32, 128), shape(16, 128)),
        4,
        ((96, 192), (96, 256)),
        vmem(3) + [pl.BlockSpec(memory_space=pltpu.SMEM)],
    )(energy, density, region, gamma_table)
    rows, up, down = call(fill_z, (shape(4, 32, 128), shape(3, 32, 128), shape(2, 32, 128)), 3)(
        rows, moved(message, "gz", 1), moved(message, "gz", -1)
    )
    own, last = call(fill_y, (shape(9, 32, 128), shape(9, 16, 128)), 3)(
        rows, moved(up, "gy", 1), moved(down, "gy", -1)
    )
    near, above, far = moved(own, GX, 1), moved(own, GX, -1), moved(last, GX, 2)
    grid = (3 * 2 * 4 * 9 * 8, 128)
    fields, sums = call(
        functools.partial(krylov, sizes),
        (shape(288, 128), shape(8, 128)),
        4,
        ((9 * 128, 128), grid, grid, grid, (288, 128)),
    )(own, far, near, above)
    acceleration, residual = call(combine, (shape(96, 128), shape(96, 128)), 2)(
        fields, total_over(sums)
    )
    return acceleration.reshape(3, 4, 8, 128), residual.reshape(3, 4, 8, 128)


def split(count):
    inner = 2
    middle = math.gcd(4, count // inner)
    return count // (inner * middle), middle, inner


def solution(mesh):
    count = mesh.shape["gx"]
    devices = mesh.devices.reshape(*split(count), mesh.shape["gy"], mesh.shape["gz"])
    finer = Mesh(devices, (*GX, "gy", "gz"))
    sizes = (2 * count, 4 * mesh.shape["gy"], 64 * mesh.shape["gz"])
    place = P(GX, "gy", "gz")
    out = P(None, GX, "gy", "gz")
    return jax.shard_map(
        functools.partial(on_device, sizes),
        mesh=finer,
        in_specs=(place, place, place, P()),
        out_specs=(out, out),
        check_vma=False,
    )
```

```python
import functools
import math

import jax
import jax.numpy as jnp
from jax import lax
from jax.experimental import pallas as pl
from jax.experimental.pallas import tpu as pltpu
from jax.sharding import Mesh
from jax.sharding import PartitionSpec as P

LOW, HIGH = 3, 2
PAIRS = 14
ROOT = math.sqrt(0.15)
EDGE_W, MID_W = 5.0 / 18.0, 8.0 / 18.0
EXACT = lax.Precision.HIGHEST
GX = ("gx0", "gx1", "gx2")


def vmem(count):
    return [pl.BlockSpec(memory_space=pltpu.VMEM)] * count


def iota(shape, dim):
    return lax.broadcasted_iota(jnp.int32, shape, dim)


def class_of(q, qz):
    if qz < 2:
        return q, qz
    return (q + 9, 0) if q < 5 else (q + 4, 1)


def prepare(energy, density, region, gamma, rows_out, message_out, spread, lines):
    for point in range(6):
        spread[16 * point : 16 * point + 12, :] = energy[point]
    row, col = iota((192, 256), 0), iota((192, 256), 1)
    pick = (row == 3 * (col % 64) + jnp.minimum(col // 64, 2)).astype(jnp.float32)
    lines[...] = jnp.dot(
        spread[...], pick, precision=EXACT, preferred_element_type=jnp.float32
    )
    rho = density[...]
    zone = region[...]
    table = jnp.zeros_like(rho)
    for index in range(3):
        table = table + jnp.where(zone == index, gamma[index], 0.0)
    scale = (table - 1.0) * rho
    scale = jnp.concatenate([scale, scale], axis=-1)
    rho = jnp.concatenate([rho, rho], axis=-1)
    low_half = iota((1, 128), 1) < 64
    pair, lane = iota((16, 128), 0), iota((16, 128), 1)
    real = pair < PAIRS
    start = (lane + 128 - 3 * pair) % 128
    keep_one = real & ((start >= 125) | ((start >= 64) & (start <= 65)))
    keep_zero = real & (((start >= 61) & (start <= 63)) | (start < 2))
    for x in range(2):
        for y in range(4):
            factor = scale[x, y : y + 1]
            parts = []
            tails = []
            for qx in range(3):
                at = (3 * x + qx) * 16 + 3 * y
                parts.append(lines[at : at + 3, 0:128] * factor)
                tails.append(lines[at : at + 3, 128:256] * factor)
            tail = [tails[q // 3][q % 3 : q % 3 + 1] for q in range(9)] + [rho[x, y : y + 1]]
            for i in range(5):
                parts.append(jnp.where(low_half, tail[i], tail[i + 5]))
            parts.append(jnp.zeros((2, 128), jnp.float32))
            base = 16 * x
            block = jnp.concatenate(parts, axis=0)
            rows_out[y, base : base + 16, :] = block
            turned = pltpu.roll(block, 0, 1, stride=3, stride_axis=0)
            zero = jnp.sum(jnp.where(keep_zero, turned, 0.0), axis=0, keepdims=True)
            one = jnp.sum(jnp.where(keep_one, turned, 0.0), axis=0, keepdims=True)
            place = y * 4 + x * 2
            message_out[place : place + 1, :] = pltpu.roll(zero, 64, 1)
            message_out[place + 1 : place + 2, :] = one


def fill_z(rows, from_low, from_high, rows_out, up_out, down_out):
    lane = iota((16, 128), 1)
    halo = jnp.where((lane < 50) | (lane >= 110), from_low[...], from_high[...])
    for y in range(4):
        for x in range(2):
            base = 16 * x
            place = y * 4 + x * 2
            block = rows[y, base : base + 16, :]
            block = jnp.concatenate([block[:PAIRS], halo[place : place + 2]], axis=0)
            rows_out[y, base : base + 16, :] = block
            if y >= 1:
                up_out[y - 1, base : base + 16, :] = block
            if y < HIGH:
                down_out[y, base : base + 16, :] = block


def fill_y(rows, from_low, from_high, rows_out, last_out):
    for y in range(9):
        if y < LOW:
            block = from_low[y]
        elif y < LOW + 4:
            block = rows[y - LOW]
        else:
            block = from_high[y - LOW - 4]
        rows_out[y] = block
        last_out[y] = block[16:32]


def element_op(v, m, w):
    total, gap = v + w, v - w
    outer = 0.75 * total + m
    inner = 1.25 * gap
    return outer + inner, total + 8.0 * m, outer - inner


def by_values(q0, q1, q2):
    total, gap = q0 + q2, q0 - q2
    outer = (0.3 * EDGE_W) * total
    inner = (ROOT * EDGE_W) * gap
    return outer + inner, (0.4 * EDGE_W) * total + MID_W * q1, outer - inner


def by_slopes(q0, q1, q2):
    total, gap = q0 + q2, q0 - q2
    outer = EDGE_W * total + MID_W * q1
    inner = (4.0 * ROOT * EDGE_W) * gap
    return -outer - inner, 2.0 * inner, outer - inner


def up_z(value):
    return pltpu.roll(value, 1, 1)


def down_z(value):
    return pltpu.roll(value, 127, 1)


def up_x(value):
    return pltpu.roll(value, 1, 0)


def down_x(value):
    return pltpu.roll(value, 7, 0)


def krylov(sizes, own, far, near, above, fields_out, sums_out, points, base, image, second, flat):
    size_x, size_y, size_z = sizes
    index_x = (lax.axis_index(GX[0]) * lax.axis_size(GX[1]) + lax.axis_index(GX[1])) * (
        lax.axis_size(GX[2])
    ) + lax.axis_index(GX[2])
    zeros = jnp.zeros((16, 128), jnp.float32)
    for y in range(9):
        sources = [
            far[y],
            near[y, 0:16],
            near[y, 16:32],
            own[y, 0:16],
            own[y, 16:32],
            above[y, 0:16],
            above[y, 16:32],
            zeros,
        ]
        for s in range(8):
            points[pl.ds(y * 128 + s, 16, stride=8), :] = sources[s]

    sub, lane = iota((8, 128), 0), iota((8, 128), 1)
    at_x = 2 * index_x + sub - LOW
    at_z = 64 * lax.axis_index("gz") + jnp.where(lane < 96, lane, lane - 128)
    inside_x = (at_x > 0) & (at_x < size_x)
    inside_z = (at_z > 0) & (at_z < size_z)
    inside = {
        (0, 0): (inside_x & inside_z).astype(jnp.float32),
        (0, 1): inside_x.astype(jnp.float32),
        (1, 0): inside_z.astype(jnp.float32),
    }
    first_y = 4 * lax.axis_index("gy") - LOW
    mine = lane < 64

    def inside_y(y):
        at = first_y + y
        return ((at > 0) & (at < size_y)).astype(jnp.float32)

    def tile(ref, d, yc, xc, zc, y):
        row = (((d * 2 + yc) * 4 + xc * 2 + zc) * 9 + y) * 8
        return ref.at[pl.ds(pl.multiple_of(row, 8), 8), :]

    def point(y, p, h):
        main = points[pl.ds(pl.multiple_of(y * 128 + p * 8, 8), 8), :]
        side = points[pl.ds(pl.multiple_of(y * 128 + (PAIRS + h) * 8, 8), 8), :]
        if h:
            main = pltpu.roll(main, 64, 1)
        if p:
            side = pltpu.roll(side, 128 - 3 * p, 1)
        return jnp.where(mine, main, side)

    def put(ref, d, xc, zc, y, vertex, middle, wall):
        if (xc, zc) in inside:
            vertex = vertex * inside[xc, zc]
            middle = middle * inside[xc, zc]
        tile(ref, d, 0, xc, zc, y)[...] = vertex * wall
        tile(ref, d, 1, xc, zc, y)[...] = middle

    def force_row(y, carry):
        wall = inside_y(y)
        value_z, slope_z = {}, {}
        for q in range(9):
            q0, q1, q2 = (point(y, *class_of(q, qz)) for qz in range(3))
            n0, n1, n2 = by_values(q0, q1, q2)
            value_z[q, 0], value_z[q, 1] = n0 + up_z(n2), n1
            n0, n1, n2 = by_slopes(q0, q1, q2)
            slope_z[q, 0], slope_z[q, 1] = n0 + up_z(n2), n1
        kept = []
        for d in range(3):
            source = slope_z if d == 2 else value_z
            op_x = by_slopes if d == 0 else by_values
            op_y = by_slopes if d == 1 else by_values
            lines = {}
            for qy in range(3):
                for zc in range(2):
                    n0, n1, n2 = op_x(*(source[3 * qx + qy, zc] for qx in range(3)))
                    lines[qy, 0, zc], lines[qy, 1, zc] = n0 + up_x(n2), n1
            for xc in range(2):
                for zc in range(2):
                    n0, n1, n2 = op_y(*(lines[qy, xc, zc] for qy in range(3)))
                    put(base, d, xc, zc, y, n0 + carry[len(kept)], n1, wall)
                    kept.append(n2)
        return tuple(kept)

    blank = jnp.zeros((8, 128), jnp.float32)
    lax.fori_loop(0, 9, force_row, (blank,) * 12)

    def mass_row(d, y, source, target, carry, rho):
        wall = inside_y(y)
        locals_y = {}
        for xc in range(2):
            for zc in range(2):
                got = element_op(
                    tile(source, d, 0, xc, zc, y)[...],
                    tile(source, d, 1, xc, zc, y)[...],
                    tile(source, d, 0, xc, zc, y + 1)[...],
                )
                for k in range(3):
                    locals_y[k, xc, zc] = got[k]
        kept = [None] * 4
        out = {}
        for k in range(3):
            lines = {}
            for xc in range(2):
                v, m = locals_y[k, xc, 0], locals_y[k, xc, 1]
                got = element_op(v, m, down_z(v))
                for j in range(3):
                    lines[j, xc] = got[j]
            joined = {}
            for j in range(3):
                v, m = lines[j, 0], lines[j, 1]
                n0, n1, n2 = (rho * n for n in element_op(v, m, down_x(v)))
                joined[j, 0], joined[j, 1] = n0 + up_x(n2), n1
            for xc in range(2):
                out[k, xc, 0] = joined[0, xc] + up_z(joined[2, xc])
                out[k, xc, 1] = joined[1, xc]
        for xc in range(2):
            for zc in range(2):
                slot = 2 * xc + zc
                put(target, d, xc, zc, y, out[0, xc, zc] + carry[slot], out[1, xc, zc], wall)
                kept[slot] = out[2, xc, zc]
        return tuple(kept)

    def mass(source, target, start, stop):
        def step(y, carry):
            rho = point(y, 13, 1) * (1.0 / 3375.0)
            kept = ()
            for d in range(3):
                kept += mass_row(d, y, source, target, carry[4 * d : 4 * d + 4], rho)
            return kept

        lax.fori_loop(start, stop, step, (blank,) * 12)

    mass(base, image, 1, 8)
    mass(image, second, 2, 7)

    owned = mine & (sub >= LOW) & (sub < LOW + 2)
    row, col = iota((8, 128), 0), iota((8, 128), 1)
    sums = jnp.zeros((8, 128), jnp.float32)
    for d in range(3):
        totals = [blank] * 4
        for yc in range(2):
            for xc in range(2):
                for zc in range(2):
                    for y in range(LOW, LOW + 4):
                        v0 = tile(base, d, yc, xc, zc, y)[...]
                        v1 = tile(image, d, yc, xc, zc, y)[...]
                        v2 = tile(second, d, yc, xc, zc, y)[...]
                        totals[0] = totals[0] + v0 * v0
                        totals[1] = totals[1] + v0 * v1
                        totals[2] = totals[2] + v1 * v1
                        totals[3] = totals[3] + v1 * v2
        for k in range(4):
            total = jnp.sum(jnp.where(owned, totals[k], 0.0), keepdims=True)
            sums = sums + jnp.where((row == k) & (col == d), total, 0.0)
    sums_out[...] = sums

    mine_row = iota((4, 128), 1) < 64
    for f, ref in enumerate((base, image, second)):
        for d in range(3):
            for yc in range(2):
                for xc in range(2):
                    for x in range(2):
                        got = []
                        for zc in range(2):
                            at = (((d * 2 + yc) * 4 + xc * 2 + zc) * 9 + LOW) * 8 + LOW + x
                            got.append(ref[pl.ds(at, 4, stride=8), :])
                        line = jnp.where(mine_row, got[0], pltpu.roll(got[1], 64, 1))
                        place = ((f * 3 + d) * 4 + 2 * x + xc) * 8 + yc
                        flat[pl.ds(place, 4, stride=2), :] = line
    row, col = iota((128, 128), 0), iota((128, 128), 1)
    weave = (row == (col % 2) * 64 + col // 2).astype(jnp.float32)
    fields_out[...] = jnp.dot(
        flat[...], weave, precision=EXACT, preferred_element_type=jnp.float32
    )


def combine(fields, sums, acceleration_out, residual_out):
    for d in range(3):
        c0, c1, c2, c3 = (sums[k : k + 1, d : d + 1] for k in range(4))
        alpha = c0 / c1
        norm = c0 - 2.0 * alpha * c1 + alpha * alpha * c2
        beta = norm / c0
        grow = 1.0 + beta
        alpha_2 = norm / (grow * grow * c1 - 2.0 * alpha * grow * c2 + alpha * alpha * c3)
        v0, v1, v2 = (fields[96 * f + 32 * d : 96 * f + 32 * d + 32, :] for f in range(3))
        direction = (v0 - alpha * v1) + beta * v0
        image = grow * v1 - alpha * v2
        acceleration_out[32 * d : 32 * d + 32, :] = alpha * v0 + alpha_2 * direction
        residual_out[32 * d : 32 * d + 32, :] = (v0 - alpha * v1) - alpha_2 * image


def moved(value, axis, by):
    count = lax.axis_size(axis)
    pairs = [(i, i + by) for i in range(count) if 0 <= i + by < count]
    return lax.ppermute(value, axis, pairs)


def shape(*dims):
    return jax.ShapeDtypeStruct(dims, jnp.float32)


def call(body, outs, *operands, scratch=(), last=False, specs=None):
    kept = [pltpu.with_memory_space_constraint(o, pltpu.VMEM) for o in operands]
    place = (lambda o: o) if last else (lambda o: pltpu.VMEM(o.shape, o.dtype))
    return pl.pallas_call(
        body,
        out_shape=tuple(place(o) for o in outs),
        in_specs=vmem(len(operands)),
        out_specs=tuple(vmem(len(outs))),
        scratch_shapes=[pltpu.VMEM(dims, jnp.float32) for dims in scratch],
    )(*kept)


def total_over(value):
    for axis in (("gx2",), ("gx1",), ("gx0",), ("gy",), ("gz",)):
        value = lax.psum(value, axis)
    return value


def on_device(sizes, energy, density, region, gamma_table):
    rows, message = pl.pallas_call(
        prepare,
        out_shape=(pltpu.VMEM((4, 32, 128), jnp.float32), pltpu.VMEM((16, 128), jnp.float32)),
        in_specs=vmem(3) + [pl.BlockSpec(memory_space=pltpu.SMEM)],
        out_specs=tuple(vmem(2)),
        scratch_shapes=[pltpu.VMEM((96, 192), jnp.float32), pltpu.VMEM((96, 256), jnp.float32)],
    )(energy, density, region, gamma_table)
    rows, up, down = call(
        fill_z,
        (shape(4, 32, 128), shape(3, 32, 128), shape(2, 32, 128)),
        rows,
        moved(message, "gz", 1),
        moved(message, "gz", -1),
    )
    own, last = call(
        fill_y,
        (shape(9, 32, 128), shape(9, 16, 128)),
        rows,
        moved(up, "gy", 1),
        moved(down, "gy", -1),
    )
    near, above, far = moved(own, GX, 1), moved(own, GX, -1), moved(last, GX, 2)
    grid = (3 * 2 * 4 * 9 * 8, 128)
    fields, sums = call(
        functools.partial(krylov, sizes),
        (shape(288, 128), shape(8, 128)),
        own,
        far,
        near,
        above,
        scratch=((9 * 128, 128), grid, grid, grid, (288, 128)),
    )
    acceleration, residual = call(
        combine, (shape(96, 128), shape(96, 128)), fields, total_over(sums), last=True
    )
    return acceleration.reshape(3, 4, 8, 128), residual.reshape(3, 4, 8, 128)


def split(count):
    inner = 2
    middle = math.gcd(4, count // inner)
    return count // (inner * middle), middle, inner


def solution(mesh):
    count = mesh.shape["gx"]
    devices = mesh.devices.reshape(*split(count), mesh.shape["gy"], mesh.shape["gz"])
    finer = Mesh(devices, (*GX, "gy", "gz"))
    sizes = (2 * count, 4 * mesh.shape["gy"], 64 * mesh.shape["gz"])
    place = P(GX, "gy", "gz")
    out = P(None, GX, "gy", "gz")
    return jax.shard_map(
        functools.partial(on_device, sizes),
        mesh=finer,
        in_specs=(place, place, place, P()),
        out_specs=(out, out),
        check_vma=False,
    )
```

```python
import functools
import math

import jax
import jax.numpy as jnp
from jax import lax
from jax.experimental import pallas as pl
from jax.experimental.pallas import tpu as pltpu
from jax.sharding import Mesh
from jax.sharding import PartitionSpec as P

LOW, HIGH = 3, 2
PAIRS = 14
ROOT = math.sqrt(0.15)
EDGE_W, MID_W = 5.0 / 18.0, 8.0 / 18.0
EXACT = lax.Precision.HIGHEST
GX = ("gx0", "gx1", "gx2")


def vmem(count):
    return [pl.BlockSpec(memory_space=pltpu.VMEM)] * count


def iota(shape, dim):
    return lax.broadcasted_iota(jnp.int32, shape, dim)


def class_of(q, qz):
    if qz < 2:
        return q, qz
    return (q + 9, 0) if q < 5 else (q + 4, 1)


def prepare(energy, density, region, gamma, rows_out, message_out, spread, lines):
    for point in range(6):
        spread[16 * point : 16 * point + 12, :] = energy[point]
    row, col = iota((192, 256), 0), iota((192, 256), 1)
    pick = (row == 3 * (col % 64) + jnp.minimum(col // 64, 2)).astype(jnp.float32)
    lines[...] = jnp.dot(
        spread[...], pick, precision=EXACT, preferred_element_type=jnp.float32
    )
    rho = density[...]
    zone = region[...]
    table = jnp.zeros_like(rho)
    for index in range(3):
        table = table + jnp.where(zone == index, gamma[index], 0.0)
    scale = (table - 1.0) * rho
    scale = jnp.concatenate([scale, scale], axis=-1)
    rho = jnp.concatenate([rho, rho], axis=-1)
    low_half = iota((1, 128), 1) < 64
    pair, lane = iota((16, 128), 0), iota((16, 128), 1)
    real = pair < PAIRS
    start = (lane + 128 - 3 * pair) % 128
    keep_one = real & ((start >= 125) | ((start >= 64) & (start <= 65)))
    keep_zero = real & (((start >= 61) & (start <= 63)) | (start < 2))
    for x in range(2):
        for y in range(4):
            factor = scale[x, y : y + 1]
            parts = []
            tails = []
            for qx in range(3):
                at = (3 * x + qx) * 16 + 3 * y
                parts.append(lines[at : at + 3, 0:128] * factor)
                tails.append(lines[at : at + 3, 128:256] * factor)
            tail = [tails[q // 3][q % 3 : q % 3 + 1] for q in range(9)] + [rho[x, y : y + 1]]
            for i in range(5):
                parts.append(jnp.where(low_half, tail[i], tail[i + 5]))
            parts.append(jnp.zeros((2, 128), jnp.float32))
            base = 16 * x
            block = jnp.concatenate(parts, axis=0)
            rows_out[y, base : base + 16, :] = block
            turned = pltpu.roll(block, 0, 1, stride=3, stride_axis=0)
            zero = jnp.sum(jnp.where(keep_zero, turned, 0.0), axis=0, keepdims=True)
            one = jnp.sum(jnp.where(keep_one, turned, 0.0), axis=0, keepdims=True)
            place = y * 4 + x * 2
            message_out[place : place + 1, :] = pltpu.roll(zero, 64, 1)
            message_out[place + 1 : place + 2, :] = one


def fill_z(rows, from_low, from_high, rows_out, up_out, down_out):
    lane = iota((16, 128), 1)
    halo = jnp.where((lane < 50) | (lane >= 110), from_low[...], from_high[...])
    for y in range(4):
        for x in range(2):
            base = 16 * x
            place = y * 4 + x * 2
            block = rows[y, base : base + 16, :]
            block = jnp.concatenate([block[:PAIRS], halo[place : place + 2]], axis=0)
            rows_out[y, base : base + 16, :] = block
            if y >= 1:
                up_out[y - 1, base : base + 16, :] = block
            if y < HIGH:
                down_out[y, base : base + 16, :] = block


def fill_y(rows, from_low, from_high, rows_out, last_out):
    for y in range(9):
        if y < LOW:
            block = from_low[y]
        elif y < LOW + 4:
            block = rows[y - LOW]
        else:
            block = from_high[y - LOW - 4]
        rows_out[y] = block
        last_out[y] = block[16:32]


def element_op(v, m, w):
    total, gap = v + w, v - w
    outer = 0.75 * total + m
    inner = 1.25 * gap
    return outer + inner, total + 8.0 * m, outer - inner


def by_values(q0, q1, q2):
    total, gap = q0 + q2, q0 - q2
    outer = (0.3 * EDGE_W) * total
    inner = (ROOT * EDGE_W) * gap
    return outer + inner, (0.4 * EDGE_W) * total + MID_W * q1, outer - inner


def by_slopes(q0, q1, q2):
    total, gap = q0 + q2, q0 - q2
    outer = EDGE_W * total + MID_W * q1
    inner = (4.0 * ROOT * EDGE_W) * gap
    return -outer - inner, 2.0 * inner, outer - inner


def up_z(value):
    return pltpu.roll(value, 1, 1)


def down_z(value):
    return pltpu.roll(value, 127, 1)


def up_x(value):
    return pltpu.roll(value, 1, 0)


def down_x(value):
    return pltpu.roll(value, 7, 0)


def krylov(sizes, own, far, near, above, fields_out, sums_out, points, base, image, second, flat):
    size_x, size_y, size_z = sizes
    index_x = (lax.axis_index(GX[0]) * lax.axis_size(GX[1]) + lax.axis_index(GX[1])) * (
        lax.axis_size(GX[2])
    ) + lax.axis_index(GX[2])
    zeros = jnp.zeros((16, 128), jnp.float32)
    for y in range(9):
        sources = [
            far[y],
            near[y, 0:16],
            near[y, 16:32],
            own[y, 0:16],
            own[y, 16:32],
            above[y, 0:16],
            above[y, 16:32],
            zeros,
        ]
        for s in range(8):
            points[pl.ds(y * 128 + s, 16, stride=8), :] = sources[s]

    sub, lane = iota((8, 128), 0), iota((8, 128), 1)
    at_x = 2 * index_x + sub - LOW
    at_z = 64 * lax.axis_index("gz") + jnp.where(lane < 96, lane, lane - 128)
    inside_x = (at_x > 0) & (at_x < size_x)
    inside_z = (at_z > 0) & (at_z < size_z)
    inside = {
        (0, 0): (inside_x & inside_z).astype(jnp.float32),
        (0, 1): inside_x.astype(jnp.float32),
        (1, 0): inside_z.astype(jnp.float32),
    }
    first_y = 4 * lax.axis_index("gy") - LOW
    mine = lane < 64

    def inside_y(y):
        at = first_y + y
        return ((at > 0) & (at < size_y)).astype(jnp.float32)

    def tile(ref, d, yc, xc, zc, y):
        row = (((d * 2 + yc) * 4 + xc * 2 + zc) * 9 + y) * 8
        return ref.at[pl.ds(pl.multiple_of(row, 8), 8), :]

    def point(y, p, h):
        main = points[pl.ds(pl.multiple_of(y * 128 + p * 8, 8), 8), :]
        side = points[pl.ds(pl.multiple_of(y * 128 + (PAIRS + h) * 8, 8), 8), :]
        if h:
            main = pltpu.roll(main, 64, 1)
        if p:
            side = pltpu.roll(side, 128 - 3 * p, 1)
        return jnp.where(mine, main, side)

    def put(ref, d, xc, zc, y, vertex, middle, wall):
        if (xc, zc) in inside:
            vertex = vertex * inside[xc, zc]
            middle = middle * inside[xc, zc]
        tile(ref, d, 0, xc, zc, y)[...] = vertex * wall
        tile(ref, d, 1, xc, zc, y)[...] = middle

    def force_row(y, carry):
        wall = inside_y(y)
        value_z, slope_z = {}, {}
        for q in range(9):
            q0, q1, q2 = (point(y, *class_of(q, qz)) for qz in range(3))
            n0, n1, n2 = by_values(q0, q1, q2)
            value_z[q, 0], value_z[q, 1] = n0 + up_z(n2), n1
            n0, n1, n2 = by_slopes(q0, q1, q2)
            slope_z[q, 0], slope_z[q, 1] = n0 + up_z(n2), n1
        kept = []
        for d in range(3):
            source = slope_z if d == 2 else value_z
            op_x = by_slopes if d == 0 else by_values
            op_y = by_slopes if d == 1 else by_values
            lines = {}
            for qy in range(3):
                for zc in range(2):
                    n0, n1, n2 = op_x(*(source[3 * qx + qy, zc] for qx in range(3)))
                    lines[qy, 0, zc], lines[qy, 1, zc] = n0 + up_x(n2), n1
            for xc in range(2):
                for zc in range(2):
                    n0, n1, n2 = op_y(*(lines[qy, xc, zc] for qy in range(3)))
                    put(base, d, xc, zc, y, n0 + carry[len(kept)], n1, wall)
                    kept.append(n2)
        return tuple(kept)

    blank = jnp.zeros((8, 128), jnp.float32)
    lax.fori_loop(0, 9, force_row, (blank,) * 12)

    def mass_row(d, y, source, target, carry, rho):
        wall = inside_y(y)
        locals_y = {}
        for xc in range(2):
            for zc in range(2):
                got = element_op(
                    tile(source, d, 0, xc, zc, y)[...],
                    tile(source, d, 1, xc, zc, y)[...],
                    tile(source, d, 0, xc, zc, y + 1)[...],
                )
                for k in range(3):
                    locals_y[k, xc, zc] = got[k]
        kept = [None] * 4
        out = {}
        for k in range(3):
            lines = {}
            for xc in range(2):
                v, m = locals_y[k, xc, 0], locals_y[k, xc, 1]
                got = element_op(v, m, down_z(v))
                for j in range(3):
                    lines[j, xc] = got[j]
            joined = {}
            for j in range(3):
                v, m = lines[j, 0], lines[j, 1]
                n0, n1, n2 = (rho * n for n in element_op(v, m, down_x(v)))
                joined[j, 0], joined[j, 1] = n0 + up_x(n2), n1
            for xc in range(2):
                out[k, xc, 0] = joined[0, xc] + up_z(joined[2, xc])
                out[k, xc, 1] = joined[1, xc]
        for xc in range(2):
            for zc in range(2):
                slot = 2 * xc + zc
                put(target, d, xc, zc, y, out[0, xc, zc] + carry[slot], out[1, xc, zc], wall)
                kept[slot] = out[2, xc, zc]
        return tuple(kept)

    def mass(source, target, start, stop):
        def step(y, carry):
            rho = point(y, 13, 1) * (1.0 / 3375.0)
            kept = ()
            for d in range(3):
                kept += mass_row(d, y, source, target, carry[4 * d : 4 * d + 4], rho)
            return kept

        lax.fori_loop(start, stop, step, (blank,) * 12)

    mass(base, image, 1, 8)
    mass(image, second, 2, 7)

    owned = mine & (sub >= LOW) & (sub < LOW + 2)
    col = iota((1, 128), 1)
    sums = jnp.zeros((1, 128), jnp.float32)
    for d in range(3):
        totals = [blank] * 4
        for yc in range(2):
            for xc in range(2):
                for zc in range(2):
                    for y in range(LOW, LOW + 4):
                        v0 = tile(base, d, yc, xc, zc, y)[...]
                        v1 = tile(image, d, yc, xc, zc, y)[...]
                        v2 = tile(second, d, yc, xc, zc, y)[...]
                        totals[0] = totals[0] + v0 * v0
                        totals[1] = totals[1] + v0 * v1
                        totals[2] = totals[2] + v1 * v1
                        totals[3] = totals[3] + v1 * v2
        for k in range(4):
            total = jnp.sum(jnp.where(owned, totals[k], 0.0), keepdims=True)
            sums = sums + jnp.where(col == 4 * d + k, total, 0.0)
    sums_out[...] = jnp.broadcast_to(sums[None], sums_out.shape)

    mine_row = iota((4, 128), 1) < 64
    for f, ref in enumerate((base, image, second)):
        for d in range(3):
            for yc in range(2):
                for xc in range(2):
                    for x in range(2):
                        got = []
                        for zc in range(2):
                            at = (((d * 2 + yc) * 4 + xc * 2 + zc) * 9 + LOW) * 8 + LOW + x
                            got.append(ref[pl.ds(at, 4, stride=8), :])
                        line = jnp.where(mine_row, got[0], pltpu.roll(got[1], 64, 1))
                        place = ((f * 3 + d) * 4 + 2 * x + xc) * 8 + yc
                        flat[pl.ds(place, 4, stride=2), :] = line
    row, col = iota((128, 128), 0), iota((128, 128), 1)
    weave = (row == (col % 2) * 64 + col // 2).astype(jnp.float32)
    fields_out[...] = jnp.dot(
        flat[...], weave, precision=EXACT, preferred_element_type=jnp.float32
    )


def add_parts(parts):
    total = parts[0]
    for k in range(1, parts.shape[0]):
        total = total + parts[k]
    return total


def relay(parts, sums_out):
    sums_out[...] = jnp.broadcast_to(add_parts(parts)[None], sums_out.shape)


def combine(fields, parts, acceleration_out, residual_out):
    sums = add_parts(parts)
    for d in range(3):
        c0, c1, c2, c3 = (sums[:, 4 * d + k : 4 * d + k + 1] for k in range(4))
        alpha = c0 / c1
        norm = c0 - 2.0 * alpha * c1 + alpha * alpha * c2
        beta = norm / c0
        grow = 1.0 + beta
        alpha_2 = norm / (grow * grow * c1 - 2.0 * alpha * grow * c2 + alpha * alpha * c3)
        v0, v1, v2 = (fields[96 * f + 32 * d : 96 * f + 32 * d + 32, :] for f in range(3))
        direction = (v0 - alpha * v1) + beta * v0
        image = grow * v1 - alpha * v2
        acceleration_out[32 * d : 32 * d + 32, :] = alpha * v0 + alpha_2 * direction
        residual_out[32 * d : 32 * d + 32, :] = (v0 - alpha * v1) - alpha_2 * image


def moved(value, axis, by):
    count = lax.axis_size(axis)
    pairs = [(i, i + by) for i in range(count) if 0 <= i + by < count]
    return lax.ppermute(value, axis, pairs)


def shape(*dims):
    return jax.ShapeDtypeStruct(dims, jnp.float32)


def call(body, outs, *operands, scratch=(), last=False, specs=None):
    kept = [pltpu.with_memory_space_constraint(o, pltpu.VMEM) for o in operands]
    place = (lambda o: o) if last else (lambda o: pltpu.VMEM(o.shape, o.dtype))
    return pl.pallas_call(
        body,
        out_shape=tuple(place(o) for o in outs),
        in_specs=vmem(len(operands)),
        out_specs=tuple(vmem(len(outs))),
        scratch_shapes=[pltpu.VMEM(dims, jnp.float32) for dims in scratch],
    )(*kept)


FIRST, SECOND = ("gx0", "gz", "gx2"), ("gy", "gx1")


def members(axes):
    return math.prod(lax.axis_size(axis) for axis in axes)


def exchange(value, axes):
    return lax.all_to_all(value, axes, 0, 0)


def on_device(sizes, energy, density, region, gamma_table):
    rows, message = pl.pallas_call(
        prepare,
        out_shape=(pltpu.VMEM((4, 32, 128), jnp.float32), pltpu.VMEM((16, 128), jnp.float32)),
        in_specs=vmem(3) + [pl.BlockSpec(memory_space=pltpu.SMEM)],
        out_specs=tuple(vmem(2)),
        scratch_shapes=[pltpu.VMEM((96, 192), jnp.float32), pltpu.VMEM((96, 256), jnp.float32)],
    )(energy, density, region, gamma_table)
    rows, up, down = call(
        fill_z,
        (shape(4, 32, 128), shape(3, 32, 128), shape(2, 32, 128)),
        rows,
        moved(message, "gz", 1),
        moved(message, "gz", -1),
    )
    own, last = call(
        fill_y,
        (shape(9, 32, 128), shape(9, 16, 128)),
        rows,
        moved(up, "gy", 1),
        moved(down, "gy", -1),
    )
    near, above, far = moved(own, GX, 1), moved(own, GX, -1), moved(last, GX, 2)
    grid = (3 * 2 * 4 * 9 * 8, 128)
    fields, sums = call(
        functools.partial(krylov, sizes),
        (shape(288, 128), shape(members(FIRST), 1, 128)),
        own,
        far,
        near,
        above,
        scratch=((9 * 128, 128), grid, grid, grid, (288, 128)),
    )
    (sums,) = call(relay, (shape(members(SECOND), 1, 128),), exchange(sums, FIRST))
    acceleration, residual = call(
        combine,
        (shape(96, 128), shape(96, 128)),
        fields,
        exchange(sums, SECOND),
        last=True,
    )
    return acceleration.reshape(3, 4, 8, 128), residual.reshape(3, 4, 8, 128)


def split(count):
    inner = 2
    middle = math.gcd(4, count // inner)
    return count // (inner * middle), middle, inner


def solution(mesh):
    count = mesh.shape["gx"]
    devices = mesh.devices.reshape(*split(count), mesh.shape["gy"], mesh.shape["gz"])
    finer = Mesh(devices, (*GX, "gy", "gz"))
    sizes = (2 * count, 4 * mesh.shape["gy"], 64 * mesh.shape["gz"])
    place = P(GX, "gy", "gz")
    out = P(None, GX, "gy", "gz")
    return jax.shard_map(
        functools.partial(on_device, sizes),
        mesh=finer,
        in_specs=(place, place, place, P()),
        out_specs=(out, out),
        check_vma=False,
    )
```

```python
import functools
import math

import jax
import jax.numpy as jnp
from jax import lax
from jax.experimental import pallas as pl
from jax.experimental.pallas import tpu as pltpu
from jax.sharding import Mesh
from jax.sharding import PartitionSpec as P

LOW, HIGH = 3, 2
PAIRS = 14
ROOT = math.sqrt(0.15)
EDGE_W, MID_W = 5.0 / 18.0, 8.0 / 18.0
UNROLL = (3, 5, 3)
GX = ("gx0", "gx1", "gx2")


def vmem(count):
    return [pl.BlockSpec(memory_space=pltpu.VMEM)] * count


def selected(value, pick):
    pick = pick.astype(jnp.bfloat16)
    total = None
    for part in range(3):
        piece = value.astype(jnp.bfloat16)
        value = value - piece.astype(jnp.float32)
        got = jnp.dot(piece, pick, preferred_element_type=jnp.float32)
        total = got if total is None else total + got
    return total


def iota(shape, dim):
    return lax.broadcasted_iota(jnp.int32, shape, dim)


def class_of(q, qz):
    if qz < 2:
        return q, qz
    return (q + 9, 0) if q < 5 else (q + 4, 1)


def prepare(energy, density, region, gamma, rows_out, message_out, spread, lines):
    for point in range(6):
        spread[16 * point : 16 * point + 12, :] = energy[point]
    row, col = iota((192, 256), 0), iota((192, 256), 1)
    pick = row == 3 * (col % 64) + jnp.minimum(col // 64, 2)
    lines[...] = selected(spread[...], pick)
    rho = density[...]
    zone = region[...]
    table = jnp.zeros_like(rho)
    for index in range(3):
        table = table + jnp.where(zone == index, gamma[index], 0.0)
    scale = (table - 1.0) * rho
    scale = jnp.concatenate([scale, scale], axis=-1)
    rho = jnp.concatenate([rho, rho], axis=-1)
    low_half = iota((1, 128), 1) < 64
    pair, lane = iota((16, 128), 0), iota((16, 128), 1)
    real = pair < PAIRS
    start = (lane + 128 - 3 * pair) % 128
    keep_one = real & ((start >= 125) | ((start >= 64) & (start <= 65)))
    keep_zero = real & (((start >= 61) & (start <= 63)) | (start < 2))
    middle = iota((3, 128), 0) == 1
    line_w = jnp.where(middle, MID_W, EDGE_W)
    half_w = jnp.where(iota((3, 128), 1) < 64, EDGE_W, MID_W)
    weights = [line_w * half_w * w for w in (EDGE_W, MID_W, EDGE_W)]
    tail_weights = [line_w * EDGE_W * w for w in (EDGE_W, MID_W, EDGE_W)]
    for x in range(2):
        for y in range(4):
            factor = scale[x, y : y + 1]
            parts = []
            tails = []
            for qx in range(3):
                at = (3 * x + qx) * 16 + 3 * y
                parts.append(lines[at : at + 3, 0:128] * (factor * weights[qx]))
                tails.append(lines[at : at + 3, 128:256] * (factor * tail_weights[qx]))
            tail = [tails[q // 3][q % 3 : q % 3 + 1] for q in range(9)] + [rho[x, y : y + 1]]
            for i in range(5):
                parts.append(jnp.where(low_half, tail[i], tail[i + 5]))
            parts.append(jnp.zeros((2, 128), jnp.float32))
            base = 16 * x
            block = jnp.concatenate(parts, axis=0)
            rows_out[y, base : base + 16, :] = block
            turned = pltpu.roll(block, 0, 1, stride=3, stride_axis=0)
            zero = jnp.sum(jnp.where(keep_zero, turned, 0.0), axis=0, keepdims=True)
            one = jnp.sum(jnp.where(keep_one, turned, 0.0), axis=0, keepdims=True)
            place = y * 4 + x * 2
            message_out[place : place + 1, :] = pltpu.roll(zero, 64, 1)
            message_out[place + 1 : place + 2, :] = one


def fill_z(rows, from_low, from_high, rows_out, up_out, down_out):
    lane = iota((16, 128), 1)
    halo = jnp.where((lane < 50) | (lane >= 110), from_low[...], from_high[...])
    for y in range(4):
        for x in range(2):
            base = 16 * x
            place = y * 4 + x * 2
            block = rows[y, base : base + 16, :]
            block = jnp.concatenate([block[:PAIRS], halo[place : place + 2]], axis=0)
            rows_out[y, base : base + 16, :] = block
            if y >= 1:
                up_out[y - 1, base : base + 16, :] = block
            if y < HIGH:
                down_out[y, base : base + 16, :] = block


def fill_y(rows, from_low, from_high, rows_out, last_out):
    for y in range(9):
        if y < LOW:
            block = from_low[y]
        elif y < LOW + 4:
            block = rows[y - LOW]
        else:
            block = from_high[y - LOW - 4]
        rows_out[y] = block
        last_out[y] = block[16:32]


def element_op(v, m, w):
    total, gap = v + w, v - w
    outer = 0.75 * total + m
    inner = 1.25 * gap
    return outer + inner, total + 8.0 * m, outer - inner


def by_values(q0, q1, q2):
    total, gap = q0 + q2, q0 - q2
    outer, inner = 0.3 * total, ROOT * gap
    return outer + inner, 0.4 * total + q1, outer - inner


def by_slopes(q0, q1, q2):
    outer = (q0 + q2) + q1
    inner = (4.0 * ROOT) * (q0 - q2)
    return -outer - inner, 2.0 * inner, outer - inner


def up_z(value):
    return pltpu.roll(value, 1, 1)


def down_z(value):
    return pltpu.roll(value, 127, 1)


def up_x(value):
    return pltpu.roll(value, 1, 0)


def down_x(value):
    return pltpu.roll(value, 7, 0)


def krylov(sizes, own, pair, cross, far, fields_out, sums_out, points, base, image, second, flat):
    size_x, size_y, size_z = sizes
    index_x = (lax.axis_index(GX[0]) * lax.axis_size(GX[1]) + lax.axis_index(GX[1])) * (
        lax.axis_size(GX[2])
    ) + lax.axis_index(GX[2])
    zeros = jnp.zeros((16, 128), jnp.float32)
    core = lax.axis_index(GX[2])
    for y in range(9):
        partner, distant = pair[1 - core, y], cross[y]
        near = jnp.where(core == 1, partner, distant)
        above = jnp.where(core == 1, distant, partner)
        sources = [
            far[y],
            near[0:16],
            near[16:32],
            own[y, 0:16],
            own[y, 16:32],
            above[0:16],
            above[16:32],
            zeros,
        ]
        for s in range(8):
            points[pl.ds(y * 128 + s, 16, stride=8), :] = sources[s]

    sub, lane = iota((8, 128), 0), iota((8, 128), 1)
    at_x = 2 * index_x + sub - LOW
    at_z = 64 * lax.axis_index("gz") + jnp.where(lane < 96, lane, lane - 128)
    inside_x = (at_x > 0) & (at_x < size_x)
    inside_z = (at_z > 0) & (at_z < size_z)
    inside = {
        (0, 0): (inside_x & inside_z).astype(jnp.float32),
        (0, 1): inside_x.astype(jnp.float32),
        (1, 0): inside_z.astype(jnp.float32),
    }
    first_y = 4 * lax.axis_index("gy") - LOW
    mine = lane < 64

    def inside_y(y):
        at = first_y + y
        return ((at > 0) & (at < size_y)).astype(jnp.float32)

    def tile(ref, d, yc, xc, zc, y):
        row = (((d * 2 + yc) * 4 + xc * 2 + zc) * 9 + y) * 8
        return ref.at[pl.ds(pl.multiple_of(row, 8), 8), :]

    def point(y, p, h):
        main = points[pl.ds(pl.multiple_of(y * 128 + p * 8, 8), 8), :]
        side = points[pl.ds(pl.multiple_of(y * 128 + (PAIRS + h) * 8, 8), 8), :]
        if h:
            main = pltpu.roll(main, 64, 1)
        if p:
            side = pltpu.roll(side, 128 - 3 * p, 1)
        return jnp.where(mine, main, side)

    def put(ref, d, xc, zc, y, vertex, middle, wall):
        if (xc, zc) in inside:
            vertex = vertex * inside[xc, zc]
            middle = None if middle is None else middle * inside[xc, zc]
        tile(ref, d, 0, xc, zc, y)[...] = vertex * wall
        if middle is not None:
            tile(ref, d, 1, xc, zc, y)[...] = middle

    def force_row(y, carry):
        wall = inside_y(y)
        lines = {}
        for qy in range(3):
            value_z, slope_z = {}, {}
            for qx in range(3):
                q0, q1, q2 = (point(y, *class_of(3 * qx + qy, qz)) for qz in range(3))
                n0, n1, n2 = by_values(q0, q1, q2)
                value_z[qx, 0], value_z[qx, 1] = n0 + up_z(n2), n1
                n0, n1, n2 = by_slopes(q0, q1, q2)
                slope_z[qx, 0], slope_z[qx, 1] = n0 + up_z(n2), n1
            for d in range(3):
                source = slope_z if d == 2 else value_z
                op_x = by_slopes if d == 0 else by_values
                for zc in range(2):
                    n0, n1, n2 = op_x(*(source[qx, zc] for qx in range(3)))
                    lines[d, qy, 0, zc], lines[d, qy, 1, zc] = n0 + up_x(n2), n1
        kept = []
        for d in range(3):
            op_y = by_slopes if d == 1 else by_values
            for xc in range(2):
                for zc in range(2):
                    n0, n1, n2 = op_y(*(lines[d, qy, xc, zc] for qy in range(3)))
                    put(base, d, xc, zc, y, n0 + carry[len(kept)], n1, wall)
                    kept.append(n2)
        return tuple(kept)

    blank = jnp.zeros((8, 128), jnp.float32)
    lax.fori_loop(0, 9, force_row, (blank,) * 12, unroll=UNROLL[0])

    def mass_row(d, y, source, target, carry, rho, wanted):
        wall = inside_y(y)
        locals_y = {}
        for xc in range(2):
            for zc in range(2):
                got = element_op(
                    tile(source, d, 0, xc, zc, y)[...],
                    tile(source, d, 1, xc, zc, y)[...],
                    tile(source, d, 0, xc, zc, y + 1)[...],
                )
                for k in range(3):
                    locals_y[k, xc, zc] = got[k]
        kept = [None] * 4
        out = {}
        for k in wanted:
            lines = {}
            for xc in range(2):
                v, m = locals_y[k, xc, 0], locals_y[k, xc, 1]
                got = element_op(v, m, down_z(v))
                for j in range(3):
                    lines[j, xc] = got[j]
            joined = {}
            for j in range(3):
                v, m = lines[j, 0], lines[j, 1]
                n0, n1, n2 = (rho * n for n in element_op(v, m, down_x(v)))
                joined[j, 0], joined[j, 1] = n0 + up_x(n2), n1
            for xc in range(2):
                out[k, xc, 0] = joined[0, xc] + up_z(joined[2, xc])
                out[k, xc, 1] = joined[1, xc]
        for xc in range(2):
            for zc in range(2):
                slot = 2 * xc + zc
                if 0 in wanted:
                    middle = out.get((1, xc, zc))
                    put(target, d, xc, zc, y, out[0, xc, zc] + carry[slot], middle, wall)
                kept[slot] = out.get((2, xc, zc), blank)
        return tuple(kept)

    def mass(source, target, start, stop, last, unroll):
        def step(y, carry, wanted=(0, 1, 2)):
            rho = point(y, 13, 1) * (1.0 / 3375.0)
            kept = ()
            for d in range(3):
                kept += mass_row(d, y, source, target, carry[4 * d : 4 * d + 4], rho, wanted)
            return kept

        carry = step(start, (blank,) * 12, (2,))
        carry = lax.fori_loop(start + 1, stop - 1, step, carry, unroll=unroll)
        step(stop - 1, carry, last)

    mass(base, image, 1, 8, (0,), UNROLL[1])
    mass(image, second, 2, 7, (0, 1), UNROLL[2])

    mine_row = iota((4, 128), 1) < 64
    for f, ref in enumerate((base, image, second)):
        for d in range(3):
            for yc in range(2):
                for xc in range(2):
                    for x in range(2):
                        got = []
                        for zc in range(2):
                            at = (((d * 2 + yc) * 4 + xc * 2 + zc) * 9 + LOW) * 8 + LOW + x
                            got.append(ref[pl.ds(at, 4, stride=8), :])
                        line = jnp.where(mine_row, got[0], pltpu.roll(got[1], 64, 1))
                        place = ((f * 3 + d) * 4 + 2 * x + xc) * 8 + yc
                        flat[pl.ds(place, 4, stride=2), :] = line

    lines = []
    for d in range(3):
        v0, v1, v2 = (flat[96 * f + 32 * d : 96 * f + 32 * d + 32, :] for f in range(3))
        for product in (v0 * v0, v0 * v1, v1 * v1, v1 * v2):
            lines.append(jnp.sum(product, axis=0, keepdims=True))
    lines = jnp.sum(jnp.concatenate(lines, axis=0), axis=1, keepdims=True)
    row, col = iota((12, 128), 0), iota((12, 128), 1)
    sums = jnp.sum(jnp.where(row == col, lines, 0.0), axis=0, keepdims=True)
    if sums_out.ndim == 3:
        sums = sums[None]
    sums_out[...] = jnp.broadcast_to(sums, sums_out.shape)

    row, col = iota((128, 128), 0), iota((128, 128), 1)
    weave = row == (col % 2) * 64 + col // 2
    fields_out[...] = jnp.dot(
        flat[...],
        weave.astype(jnp.float32),
        precision=lax.Precision.HIGHEST,
        preferred_element_type=jnp.float32,
    )


def total_of(parts):
    if parts.ndim == 2:
        return jnp.sum(parts[...], axis=0, keepdims=True)
    rows = [parts[k] for k in range(parts.shape[0])]
    while len(rows) > 1:
        rows = [sum(rows[k : k + 2][1:], rows[k]) for k in range(0, len(rows), 2)]
    return rows[0]


def relay(parts, sums_out):
    sums = total_of(parts)
    if sums_out.ndim == 3:
        sums = sums[None]
    sums_out[...] = jnp.broadcast_to(sums, sums_out.shape)


def combine(fields, parts, acceleration_out, residual_out):
    sums = total_of(parts)
    for d in range(3):
        c0, c1, c2, c3 = (sums[:, 4 * d + k : 4 * d + k + 1] for k in range(4))
        alpha = c0 / c1
        norm = c0 - 2.0 * alpha * c1 + alpha * alpha * c2
        beta = norm / c0
        grow = 1.0 + beta
        alpha_2 = norm / (grow * grow * c1 - 2.0 * alpha * grow * c2 + alpha * alpha * c3)
        v0, v1, v2 = (fields[96 * f + 32 * d : 96 * f + 32 * d + 32, :] for f in range(3))
        direction = (v0 - alpha * v1) + beta * v0
        image = grow * v1 - alpha * v2
        acceleration_out[32 * d : 32 * d + 32, :] = alpha * v0 + alpha_2 * direction
        residual_out[32 * d : 32 * d + 32, :] = (v0 - alpha * v1) - alpha_2 * image


def moved(value, axis, by):
    count = lax.axis_size(axis)
    pairs = [(i, i + by) for i in range(count) if 0 <= i + by < count]
    return lax.ppermute(value, axis, pairs)


def shape(*dims):
    return jax.ShapeDtypeStruct(dims, jnp.float32)


def call(body, outs, *operands, scratch=(), last=False, specs=None):
    kept = [pltpu.with_memory_space_constraint(o, pltpu.VMEM) for o in operands]
    place = (lambda o: o) if last else (lambda o: pltpu.VMEM(o.shape, o.dtype))
    return pl.pallas_call(
        body,
        out_shape=tuple(place(o) for o in outs),
        in_specs=vmem(len(operands)),
        out_specs=tuple(vmem(len(outs))),
        scratch_shapes=[pltpu.VMEM(dims, jnp.float32) for dims in scratch],
    )(*kept)


FIRST, SECOND = ("gx0", "gz", "gx2"), ("gy", "gx1")


def members(axes):
    return math.prod(lax.axis_size(axis) for axis in axes)


def parts_shape(axes):
    count = members(axes)
    return shape(count, 128) if count % 8 == 0 else shape(count, 1, 128)


def exchange(value, axes):
    parts = lax.all_to_all(value.reshape(-1, 1, 128), axes, 0, 0)
    return parts.reshape(value.shape)


def on_device(sizes, energy, density, region, gamma_table):
    rows, message = pl.pallas_call(
        prepare,
        out_shape=(pltpu.VMEM((4, 32, 128), jnp.float32), pltpu.VMEM((16, 128), jnp.float32)),
        in_specs=vmem(3) + [pl.BlockSpec(memory_space=pltpu.SMEM)],
        out_specs=tuple(vmem(2)),
        scratch_shapes=[pltpu.VMEM((96, 192), jnp.float32), pltpu.VMEM((96, 256), jnp.float32)],
    )(energy, density, region, gamma_table)
    rows, up, down = call(
        fill_z,
        (shape(4, 32, 128), shape(3, 32, 128), shape(2, 32, 128)),
        rows,
        moved(message, "gz", 1),
        moved(message, "gz", -1),
    )
    own, last = call(
        fill_y,
        (shape(9, 32, 128), shape(9, 16, 128)),
        rows,
        moved(up, "gy", 1),
        moved(down, "gy", -1),
    )
    chips = members(GX) // 2
    links = [(2 * i + 1, 2 * i + 2) for i in range(chips - 1)]
    cross = lax.ppermute(own, GX, links + [(b, a) for a, b in links])
    far = moved(last, GX, 2)
    pair = lax.all_gather(own, GX[2])
    grid = (3 * 2 * 4 * 9 * 8, 128)
    fields, sums = call(
        functools.partial(krylov, sizes),
        (shape(288, 128), parts_shape(FIRST)),
        own,
        pair,
        cross,
        far,
        scratch=((9 * 128, 128), grid, grid, grid, (288, 128)),
    )
    (sums,) = call(relay, (parts_shape(SECOND),), exchange(sums, FIRST))
    acceleration, residual = call(
        combine,
        (shape(96, 128), shape(96, 128)),
        fields,
        exchange(sums, SECOND),
        last=True,
    )
    return acceleration.reshape(3, 4, 8, 128), residual.reshape(3, 4, 8, 128)


def split(count):
    inner = 2
    middle = math.gcd(4, count // inner)
    return count // (inner * middle), middle, inner


def solution(mesh):
    count = mesh.shape["gx"]
    devices = mesh.devices.reshape(*split(count), mesh.shape["gy"], mesh.shape["gz"])
    finer = Mesh(devices, (*GX, "gy", "gz"))
    sizes = (2 * count, 4 * mesh.shape["gy"], 64 * mesh.shape["gz"])
    place = P(GX, "gy", "gz")
    out = P(None, GX, "gy", "gz")
    return jax.shard_map(
        functools.partial(on_device, sizes),
        mesh=finer,
        in_specs=(place, place, place, P()),
        out_specs=(out, out),
        check_vma=False,
    )
```

```python
import functools
import math

import jax
import jax.numpy as jnp
from jax import lax
from jax.experimental import pallas as pl
from jax.experimental.pallas import tpu as pltpu
from jax.sharding import Mesh
from jax.sharding import PartitionSpec as P

LOW, HIGH = 3, 2
PAIRS = 14
ROOT = math.sqrt(0.15)
EDGE_W, MID_W = 5.0 / 18.0, 8.0 / 18.0
UNROLL = (3, 5, 3)
GX = ("gx0", "gx1", "gx2")


def vmem(count):
    return [pl.BlockSpec(memory_space=pltpu.VMEM)] * count


def selected(value, pick):
    pick = pick.astype(jnp.bfloat16)
    total = None
    for part in range(3):
        piece = value.astype(jnp.bfloat16)
        value = value - piece.astype(jnp.float32)
        got = jnp.dot(piece, pick, preferred_element_type=jnp.float32)
        total = got if total is None else total + got
    return total


def iota(shape, dim):
    return lax.broadcasted_iota(jnp.int32, shape, dim)


def class_of(q, qz):
    if qz < 2:
        return q, qz
    return (q + 9, 0) if q < 5 else (q + 4, 1)


def prepare(energy, density, region, gamma, rows_out, message_out, spread, lines):
    for point in range(6):
        spread[16 * point : 16 * point + 12, :] = energy[point]
    row, col = iota((192, 256), 0), iota((192, 256), 1)
    pick = row == 3 * (col % 64) + jnp.minimum(col // 64, 2)
    lines[...] = selected(spread[...], pick)
    rho = density[...]
    zone = region[...]
    table = jnp.zeros_like(rho)
    for index in range(3):
        table = table + jnp.where(zone == index, gamma[index], 0.0)
    scale = (table - 1.0) * rho
    scale = jnp.concatenate([scale, scale], axis=-1)
    rho = jnp.concatenate([rho, rho], axis=-1)
    low_half = iota((1, 128), 1) < 64
    pair, lane = iota((16, 128), 0), iota((16, 128), 1)
    real = pair < PAIRS
    start = (lane + 128 - 3 * pair) % 128
    keep_one = real & ((start >= 125) | ((start >= 64) & (start <= 65)))
    keep_zero = real & (((start >= 61) & (start <= 63)) | (start < 2))
    middle = iota((3, 128), 0) == 1
    line_w = jnp.where(middle, MID_W, EDGE_W)
    half_w = jnp.where(iota((3, 128), 1) < 64, EDGE_W, MID_W)
    weights = [line_w * half_w * w for w in (EDGE_W, MID_W, EDGE_W)]
    tail_weights = [line_w * EDGE_W * w for w in (EDGE_W, MID_W, EDGE_W)]
    for x in range(2):
        for y in range(4):
            factor = scale[x, y : y + 1]
            parts = []
            tails = []
            for qx in range(3):
                at = (3 * x + qx) * 16 + 3 * y
                parts.append(lines[at : at + 3, 0:128] * (factor * weights[qx]))
                tails.append(lines[at : at + 3, 128:256] * (factor * tail_weights[qx]))
            tail = [tails[q // 3][q % 3 : q % 3 + 1] for q in range(9)] + [rho[x, y : y + 1]]
            for i in range(5):
                parts.append(jnp.where(low_half, tail[i], tail[i + 5]))
            parts.append(jnp.zeros((2, 128), jnp.float32))
            base = 16 * x
            block = jnp.concatenate(parts, axis=0)
            rows_out[y, base : base + 16, :] = block
            turned = pltpu.roll(block, 0, 1, stride=3, stride_axis=0)
            zero = jnp.sum(jnp.where(keep_zero, turned, 0.0), axis=0, keepdims=True)
            one = jnp.sum(jnp.where(keep_one, turned, 0.0), axis=0, keepdims=True)
            place = y * 4 + x * 2
            message_out[place : place + 1, :] = pltpu.roll(zero, 64, 1)
            message_out[place + 1 : place + 2, :] = one


def fill_z(rows, even, odd, rows_out, slots_out):
    lane = iota((16, 128), 1)
    place_z = lax.axis_index("gz")
    swapped = place_z % 2 == 1
    from_low = jnp.where(swapped, even[...], odd[...])
    from_high = jnp.where(swapped, odd[...], even[...])
    halo = jnp.where((lane < 50) | (lane >= 110), from_low, from_high)
    me = lax.axis_index("gy")
    for y in range(4):
        blocks = []
        for x in range(2):
            base = 16 * x
            place = y * 4 + x * 2
            block = rows[y, base : base + 16, :]
            blocks.append(jnp.concatenate([block[:PAIRS], halo[place : place + 2]], axis=0))
        rows_out[y] = jnp.concatenate(blocks, axis=0)
    for to in range(slots_out.shape[0]):
        first = jnp.where(to > me, 1, 0)
        for k in range(LOW):
            slots_out[to, 32 * k : 32 * k + 32, :] = rows_out[first + k]


def fill_y(rows, slots, rows_out, last_out):
    me = lax.axis_index("gy")
    count = slots.shape[0]
    below = jnp.maximum(me - 1, 0)
    above = jnp.minimum(me + 1, count - 1)
    for y in range(LOW + 4 + HIGH):
        if y < LOW:
            block = slots[below, 32 * y : 32 * y + 32, :]
            block = jnp.where(me > 0, block, 0.0)
        elif y < LOW + 4:
            block = rows[y - LOW]
        else:
            at = 32 * (y - LOW - 4)
            block = slots[above, at : at + 32, :]
            block = jnp.where(me < count - 1, block, 0.0)
        rows_out[y] = block
        last_out[y] = block[16:32]


def element_op(v, m, w):
    total, gap = v + w, v - w
    outer = 0.75 * total + m
    inner = 1.25 * gap
    return outer + inner, total + 8.0 * m, outer - inner


def by_values(q0, q1, q2):
    total, gap = q0 + q2, q0 - q2
    outer, inner = 0.3 * total, ROOT * gap
    return outer + inner, 0.4 * total + q1, outer - inner


def by_slopes(q0, q1, q2):
    outer = (q0 + q2) + q1
    inner = (4.0 * ROOT) * (q0 - q2)
    return -outer - inner, 2.0 * inner, outer - inner


def up_z(value):
    return pltpu.roll(value, 1, 1)


def down_z(value):
    return pltpu.roll(value, 127, 1)


def up_x(value):
    return pltpu.roll(value, 1, 0)


def down_x(value):
    return pltpu.roll(value, 7, 0)


def krylov(sizes, own, pair, cross, far, fields_out, sums_out, points, base, image, second, flat):
    size_x, size_y, size_z = sizes
    index_x = (lax.axis_index(GX[0]) * lax.axis_size(GX[1]) + lax.axis_index(GX[1])) * (
        lax.axis_size(GX[2])
    ) + lax.axis_index(GX[2])
    zeros = jnp.zeros((16, 128), jnp.float32)
    core = lax.axis_index(GX[2])
    for y in range(9):
        partner, distant = pair[1 - core, y], cross[y]
        near = jnp.where(core == 1, partner, distant)
        above = jnp.where(core == 1, distant, partner)
        sources = [
            far[y],
            near[0:16],
            near[16:32],
            own[y, 0:16],
            own[y, 16:32],
            above[0:16],
            above[16:32],
            zeros,
        ]
        for s in range(8):
            points[pl.ds(y * 128 + s, 16, stride=8), :] = sources[s]

    sub, lane = iota((8, 128), 0), iota((8, 128), 1)
    at_x = 2 * index_x + sub - LOW
    at_z = 64 * lax.axis_index("gz") + jnp.where(lane < 96, lane, lane - 128)
    inside_x = (at_x > 0) & (at_x < size_x)
    inside_z = (at_z > 0) & (at_z < size_z)
    inside = {
        (0, 0): (inside_x & inside_z).astype(jnp.float32),
        (0, 1): inside_x.astype(jnp.float32),
        (1, 0): inside_z.astype(jnp.float32),
    }
    first_y = 4 * lax.axis_index("gy") - LOW
    mine = lane < 64

    def inside_y(y):
        at = first_y + y
        return ((at > 0) & (at < size_y)).astype(jnp.float32)

    def tile(ref, d, yc, xc, zc, y):
        row = (((d * 2 + yc) * 4 + xc * 2 + zc) * 9 + y) * 8
        return ref.at[pl.ds(pl.multiple_of(row, 8), 8), :]

    def point(y, p, h):
        main = points[pl.ds(pl.multiple_of(y * 128 + p * 8, 8), 8), :]
        side = points[pl.ds(pl.multiple_of(y * 128 + (PAIRS + h) * 8, 8), 8), :]
        if h:
            main = pltpu.roll(main, 64, 1)
        if p:
            side = pltpu.roll(side, 128 - 3 * p, 1)
        return jnp.where(mine, main, side)

    def put(ref, d, xc, zc, y, vertex, middle, wall):
        if (xc, zc) in inside:
            vertex = vertex * inside[xc, zc]
            middle = None if middle is None else middle * inside[xc, zc]
        tile(ref, d, 0, xc, zc, y)[...] = vertex * wall
        if middle is not None:
            tile(ref, d, 1, xc, zc, y)[...] = middle

    def force_row(y, carry):
        wall = inside_y(y)
        lines = {}
        for qy in range(3):
            value_z, slope_z = {}, {}
            for qx in range(3):
                q0, q1, q2 = (point(y, *class_of(3 * qx + qy, qz)) for qz in range(3))
                n0, n1, n2 = by_values(q0, q1, q2)
                value_z[qx, 0], value_z[qx, 1] = n0 + up_z(n2), n1
                n0, n1, n2 = by_slopes(q0, q1, q2)
                slope_z[qx, 0], slope_z[qx, 1] = n0 + up_z(n2), n1
            for d in range(3):
                source = slope_z if d == 2 else value_z
                op_x = by_slopes if d == 0 else by_values
                for zc in range(2):
                    n0, n1, n2 = op_x(*(source[qx, zc] for qx in range(3)))
                    lines[d, qy, 0, zc], lines[d, qy, 1, zc] = n0 + up_x(n2), n1
        kept = []
        for d in range(3):
            op_y = by_slopes if d == 1 else by_values
            for xc in range(2):
                for zc in range(2):
                    n0, n1, n2 = op_y(*(lines[d, qy, xc, zc] for qy in range(3)))
                    put(base, d, xc, zc, y, n0 + carry[len(kept)], n1, wall)
                    kept.append(n2)
        return tuple(kept)

    blank = jnp.zeros((8, 128), jnp.float32)
    lax.fori_loop(0, 9, force_row, (blank,) * 12, unroll=UNROLL[0])

    def mass_row(d, y, source, target, carry, rho, wanted):
        wall = inside_y(y)
        locals_y = {}
        for xc in range(2):
            for zc in range(2):
                got = element_op(
                    tile(source, d, 0, xc, zc, y)[...],
                    tile(source, d, 1, xc, zc, y)[...],
                    tile(source, d, 0, xc, zc, y + 1)[...],
                )
                for k in range(3):
                    locals_y[k, xc, zc] = got[k]
        kept = [None] * 4
        out = {}
        for k in wanted:
            lines = {}
            for xc in range(2):
                v, m = locals_y[k, xc, 0], locals_y[k, xc, 1]
                got = element_op(v, m, down_z(v))
                for j in range(3):
                    lines[j, xc] = got[j]
            joined = {}
            for j in range(3):
                v, m = lines[j, 0], lines[j, 1]
                n0, n1, n2 = (rho * n for n in element_op(v, m, down_x(v)))
                joined[j, 0], joined[j, 1] = n0 + up_x(n2), n1
            for xc in range(2):
                out[k, xc, 0] = joined[0, xc] + up_z(joined[2, xc])
                out[k, xc, 1] = joined[1, xc]
        for xc in range(2):
            for zc in range(2):
                slot = 2 * xc + zc
                if 0 in wanted:
                    middle = out.get((1, xc, zc))
                    put(target, d, xc, zc, y, out[0, xc, zc] + carry[slot], middle, wall)
                kept[slot] = out.get((2, xc, zc), blank)
        return tuple(kept)

    def mass(source, target, start, stop, last, unroll):
        def step(y, carry, wanted=(0, 1, 2)):
            rho = point(y, 13, 1) * (1.0 / 3375.0)
            kept = ()
            for d in range(3):
                kept += mass_row(d, y, source, target, carry[4 * d : 4 * d + 4], rho, wanted)
            return kept

        carry = step(start, (blank,) * 12, (2,))
        carry = lax.fori_loop(start + 1, stop - 1, step, carry, unroll=unroll)
        step(stop - 1, carry, last)

    mass(base, image, 1, 8, (0,), UNROLL[1])
    mass(image, second, 2, 7, (0, 1), UNROLL[2])

    mine_row = iota((4, 128), 1) < 64
    for f, ref in enumerate((base, image, second)):
        for d in range(3):
            for yc in range(2):
                for xc in range(2):
                    for x in range(2):
                        got = []
                        for zc in range(2):
                            at = (((d * 2 + yc) * 4 + xc * 2 + zc) * 9 + LOW) * 8 + LOW + x
                            got.append(ref[pl.ds(at, 4, stride=8), :])
                        line = jnp.where(mine_row, got[0], pltpu.roll(got[1], 64, 1))
                        place = ((f * 3 + d) * 4 + 2 * x + xc) * 8 + yc
                        flat[pl.ds(place, 4, stride=2), :] = line

    lines = []
    for d in range(3):
        v0, v1, v2 = (flat[96 * f + 32 * d : 96 * f + 32 * d + 32, :] for f in range(3))
        for product in (v0 * v0, v0 * v1, v1 * v1, v1 * v2):
            lines.append(jnp.sum(product, axis=0, keepdims=True))
    lines = jnp.sum(jnp.concatenate(lines, axis=0), axis=1, keepdims=True)
    row, col = iota((12, 128), 0), iota((12, 128), 1)
    sums = jnp.sum(jnp.where(row == col, lines, 0.0), axis=0, keepdims=True)
    if sums_out.ndim == 3:
        sums = sums[None]
    sums_out[...] = jnp.broadcast_to(sums, sums_out.shape)

    row, col = iota((128, 128), 0), iota((128, 128), 1)
    weave = row == (col % 2) * 64 + col // 2
    fields_out[...] = jnp.dot(
        flat[...],
        weave.astype(jnp.float32),
        precision=lax.Precision.HIGHEST,
        preferred_element_type=jnp.float32,
    )


def total_of(parts):
    if parts.ndim == 2:
        return jnp.sum(parts[...], axis=0, keepdims=True)
    rows = [parts[k] for k in range(parts.shape[0])]
    while len(rows) > 1:
        rows = [sum(rows[k : k + 2][1:], rows[k]) for k in range(0, len(rows), 2)]
    return rows[0]


def relay(parts, sums_out):
    sums = total_of(parts)
    if sums_out.ndim == 3:
        sums = sums[None]
    sums_out[...] = jnp.broadcast_to(sums, sums_out.shape)


def combine(fields, parts, acceleration_out, residual_out):
    sums = total_of(parts)
    for d in range(3):
        c0, c1, c2, c3 = (sums[:, 4 * d + k : 4 * d + k + 1] for k in range(4))
        alpha = c0 / c1
        norm = c0 - 2.0 * alpha * c1 + alpha * alpha * c2
        beta = norm / c0
        grow = 1.0 + beta
        alpha_2 = norm / (grow * grow * c1 - 2.0 * alpha * grow * c2 + alpha * alpha * c3)
        v0, v1, v2 = (fields[96 * f + 32 * d : 96 * f + 32 * d + 32, :] for f in range(3))
        direction = (v0 - alpha * v1) + beta * v0
        image = grow * v1 - alpha * v2
        acceleration_out[32 * d : 32 * d + 32, :] = alpha * v0 + alpha_2 * direction
        residual_out[32 * d : 32 * d + 32, :] = (v0 - alpha * v1) - alpha_2 * image


def moved(value, axis, by):
    count = lax.axis_size(axis)
    pairs = [(i, i + by) for i in range(count) if 0 <= i + by < count]
    return lax.ppermute(value, axis, pairs)


def swapped(value, axis, first):
    links = [(i, i + 1) for i in range(first, lax.axis_size(axis) - 1, 2)]
    return lax.ppermute(value, axis, links + [(b, a) for a, b in links])


def shape(*dims):
    return jax.ShapeDtypeStruct(dims, jnp.float32)


def call(body, outs, *operands, scratch=(), last=False, specs=None):
    kept = [pltpu.with_memory_space_constraint(o, pltpu.VMEM) for o in operands]
    place = (lambda o: o) if last else (lambda o: pltpu.VMEM(o.shape, o.dtype))
    return pl.pallas_call(
        body,
        out_shape=tuple(place(o) for o in outs),
        in_specs=vmem(len(operands)),
        out_specs=tuple(vmem(len(outs))),
        scratch_shapes=[pltpu.VMEM(dims, jnp.float32) for dims in scratch],
    )(*kept)


FIRST, SECOND = ("gx0", "gz", "gx2"), ("gy", "gx1")


def members(axes):
    return math.prod(lax.axis_size(axis) for axis in axes)


def parts_shape(axes):
    count = members(axes)
    return shape(count, 128) if count % 8 == 0 else shape(count, 1, 128)


def exchange(value, axes):
    parts = lax.all_to_all(value.reshape(-1, 1, 128), axes, 0, 0)
    return parts.reshape(value.shape)


def on_device(sizes, energy, density, region, gamma_table):
    rows, message = pl.pallas_call(
        prepare,
        out_shape=(pltpu.VMEM((4, 32, 128), jnp.float32), pltpu.VMEM((16, 128), jnp.float32)),
        in_specs=vmem(3) + [pl.BlockSpec(memory_space=pltpu.SMEM)],
        out_specs=tuple(vmem(2)),
        scratch_shapes=[pltpu.VMEM((96, 192), jnp.float32), pltpu.VMEM((96, 256), jnp.float32)],
    )(energy, density, region, gamma_table)
    rows, slots = call(
        fill_z,
        (shape(4, 32, 128), shape(lax.axis_size("gy"), 32 * LOW, 128)),
        rows,
        swapped(message, "gz", 0),
        swapped(message, "gz", 1),
    )
    own, last = call(
        fill_y,
        (shape(9, 32, 128), shape(9, 16, 128)),
        rows,
        lax.all_to_all(slots, "gy", 0, 0),
    )
    chips = members(GX) // 2
    links = [(2 * i + 1, 2 * i + 2) for i in range(chips - 1)]
    cross = lax.ppermute(own, GX, links + [(b, a) for a, b in links])
    far = moved(last, GX, 2)
    pair = lax.all_gather(own, GX[2])
    grid = (3 * 2 * 4 * 9 * 8, 128)
    fields, sums = call(
        functools.partial(krylov, sizes),
        (shape(288, 128), parts_shape(FIRST)),
        own,
        pair,
        cross,
        far,
        scratch=((9 * 128, 128), grid, grid, grid, (288, 128)),
    )
    (sums,) = call(relay, (parts_shape(SECOND),), exchange(sums, FIRST))
    acceleration, residual = call(
        combine,
        (shape(96, 128), shape(96, 128)),
        fields,
        exchange(sums, SECOND),
        last=True,
    )
    return acceleration.reshape(3, 4, 8, 128), residual.reshape(3, 4, 8, 128)


def split(count):
    inner = 2
    middle = math.gcd(4, count // inner)
    return count // (inner * middle), middle, inner


def solution(mesh):
    count = mesh.shape["gx"]
    devices = mesh.devices.reshape(*split(count), mesh.shape["gy"], mesh.shape["gz"])
    finer = Mesh(devices, (*GX, "gy", "gz"))
    sizes = (2 * count, 4 * mesh.shape["gy"], 64 * mesh.shape["gz"])
    place = P(GX, "gy", "gz")
    out = P(None, GX, "gy", "gz")
    return jax.shard_map(
        functools.partial(on_device, sizes),
        mesh=finer,
        in_specs=(place, place, place, P()),
        out_specs=(out, out),
        check_vma=False,
    )
```

```python
import functools
import math

import jax
import jax.numpy as jnp
from jax import lax
from jax.experimental import pallas as pl
from jax.experimental.pallas import tpu as pltpu
from jax.sharding import Mesh
from jax.sharding import PartitionSpec as P

LOW, HIGH = 3, 2
PAIRS = 14
ROOT = math.sqrt(0.15)
EDGE_W, MID_W = 5.0 / 18.0, 8.0 / 18.0
UNROLL = (3, 5, 3)
GX = ("gx0", "gx1", "gx2")
GZ = ("gz0", "gz1")


def vmem(count):
    return [pl.BlockSpec(memory_space=pltpu.VMEM)] * count


def selected(value, pick):
    pick = pick.astype(jnp.bfloat16)
    total = None
    for part in range(3):
        piece = value.astype(jnp.bfloat16)
        value = value - piece.astype(jnp.float32)
        got = jnp.dot(piece, pick, preferred_element_type=jnp.float32)
        total = got if total is None else total + got
    return total


def iota(shape, dim):
    return lax.broadcasted_iota(jnp.int32, shape, dim)


def class_of(q, qz):
    if qz < 2:
        return q, qz
    return (q + 9, 0) if q < 5 else (q + 4, 1)


def prepare(energy, density, region, gamma, rows_out, message_out, spread, lines):
    for point in range(6):
        spread[16 * point : 16 * point + 12, :] = energy[point]
    row, col = iota((192, 256), 0), iota((192, 256), 1)
    pick = row == 3 * (col % 64) + jnp.minimum(col // 64, 2)
    lines[...] = selected(spread[...], pick)
    rho = density[...]
    zone = region[...]
    table = jnp.zeros_like(rho)
    for index in range(3):
        table = table + jnp.where(zone == index, gamma[index], 0.0)
    scale = (table - 1.0) * rho
    scale = jnp.concatenate([scale, scale], axis=-1)
    rho = jnp.concatenate([rho, rho], axis=-1)
    low_half = iota((1, 128), 1) < 64
    pair, lane = iota((16, 128), 0), iota((16, 128), 1)
    real = pair < PAIRS
    start = (lane + 128 - 3 * pair) % 128
    keep_one = real & ((start >= 125) | ((start >= 64) & (start <= 65)))
    keep_zero = real & (((start >= 61) & (start <= 63)) | (start < 2))
    middle = iota((3, 128), 0) == 1
    line_w = jnp.where(middle, MID_W, EDGE_W)
    half_w = jnp.where(iota((3, 128), 1) < 64, EDGE_W, MID_W)
    weights = [line_w * half_w * w for w in (EDGE_W, MID_W, EDGE_W)]
    tail_weights = [line_w * EDGE_W * w for w in (EDGE_W, MID_W, EDGE_W)]
    for x in range(2):
        for y in range(4):
            factor = scale[x, y : y + 1]
            parts = []
            tails = []
            for qx in range(3):
                at = (3 * x + qx) * 16 + 3 * y
                parts.append(lines[at : at + 3, 0:128] * (factor * weights[qx]))
                tails.append(lines[at : at + 3, 128:256] * (factor * tail_weights[qx]))
            tail = [tails[q // 3][q % 3 : q % 3 + 1] for q in range(9)] + [rho[x, y : y + 1]]
            for i in range(5):
                parts.append(jnp.where(low_half, tail[i], tail[i + 5]))
            parts.append(jnp.zeros((2, 128), jnp.float32))
            base = 16 * x
            block = jnp.concatenate(parts, axis=0)
            rows_out[y, base : base + 16, :] = block
            turned = pltpu.roll(block, 0, 1, stride=3, stride_axis=0)
            zero = jnp.sum(jnp.where(keep_zero, turned, 0.0), axis=0, keepdims=True)
            one = jnp.sum(jnp.where(keep_one, turned, 0.0), axis=0, keepdims=True)
            place = y * 4 + x * 2
            message_out[place : place + 1, :] = pltpu.roll(zero, 64, 1)
            message_out[place + 1 : place + 2, :] = one


def fill_z(rows, even, odd, rows_out, slots_out):
    lane = iota((16, 128), 1)
    second = lax.axis_index(GZ[1]) == 1
    partner = even[1 - lax.axis_index(GZ[1])]
    from_low = jnp.where(second, partner, odd[...])
    from_high = jnp.where(second, odd[...], partner)
    halo = jnp.where((lane < 50) | (lane >= 110), from_low, from_high)
    me = lax.axis_index("gy")
    for y in range(4):
        blocks = []
        for x in range(2):
            base = 16 * x
            place = y * 4 + x * 2
            block = rows[y, base : base + 16, :]
            blocks.append(jnp.concatenate([block[:PAIRS], halo[place : place + 2]], axis=0))
        rows_out[y] = jnp.concatenate(blocks, axis=0)
    for to in range(slots_out.shape[0]):
        first = jnp.where(to > me, 1, 0)
        for k in range(LOW):
            slots_out[to, 32 * k : 32 * k + 32, :] = rows_out[first + k]


def fill_y(rows, slots, rows_out, last_out):
    me = lax.axis_index("gy")
    count = slots.shape[0]
    below = jnp.maximum(me - 1, 0)
    above = jnp.minimum(me + 1, count - 1)
    for y in range(LOW + 4 + HIGH):
        if y < LOW:
            block = slots[below, 32 * y : 32 * y + 32, :]
            block = jnp.where(me > 0, block, 0.0)
        elif y < LOW + 4:
            block = rows[y - LOW]
        else:
            at = 32 * (y - LOW - 4)
            block = slots[above, at : at + 32, :]
            block = jnp.where(me < count - 1, block, 0.0)
        rows_out[y] = block
        last_out[y] = block[16:32]


def element_op(v, m, w):
    total, gap = v + w, v - w
    outer = 0.75 * total + m
    inner = 1.25 * gap
    return outer + inner, total + 8.0 * m, outer - inner


def by_values(q0, q1, q2):
    total, gap = q0 + q2, q0 - q2
    outer, inner = 0.3 * total, ROOT * gap
    return outer + inner, 0.4 * total + q1, outer - inner


def by_slopes(q0, q1, q2):
    outer = (q0 + q2) + q1
    inner = (4.0 * ROOT) * (q0 - q2)
    return -outer - inner, 2.0 * inner, outer - inner


def up_z(value):
    return pltpu.roll(value, 1, 1)


def down_z(value):
    return pltpu.roll(value, 127, 1)


def up_x(value):
    return pltpu.roll(value, 1, 0)


def down_x(value):
    return pltpu.roll(value, 7, 0)


def krylov(sizes, own, pair, cross, far, fields_out, sums_out, points, base, image, second, flat):
    size_x, size_y, size_z = sizes
    index_x = (lax.axis_index(GX[0]) * lax.axis_size(GX[1]) + lax.axis_index(GX[1])) * (
        lax.axis_size(GX[2])
    ) + lax.axis_index(GX[2])
    zeros = jnp.zeros((16, 128), jnp.float32)
    core = lax.axis_index(GX[2])
    for y in range(9):
        partner, distant = pair[1 - core, y], cross[y]
        near = jnp.where(core == 1, partner, distant)
        above = jnp.where(core == 1, distant, partner)
        sources = [
            far[y],
            near[0:16],
            near[16:32],
            own[y, 0:16],
            own[y, 16:32],
            above[0:16],
            above[16:32],
            zeros,
        ]
        for s in range(8):
            points[pl.ds(y * 128 + s, 16, stride=8), :] = sources[s]

    sub, lane = iota((8, 128), 0), iota((8, 128), 1)
    at_x = 2 * index_x + sub - LOW
    index_z = lax.axis_index(GZ[0]) * lax.axis_size(GZ[1]) + lax.axis_index(GZ[1])
    at_z = 64 * index_z + jnp.where(lane < 96, lane, lane - 128)
    inside_x = (at_x > 0) & (at_x < size_x)
    inside_z = (at_z > 0) & (at_z < size_z)
    inside = {
        (0, 0): (inside_x & inside_z).astype(jnp.float32),
        (0, 1): inside_x.astype(jnp.float32),
        (1, 0): inside_z.astype(jnp.float32),
    }
    first_y = 4 * lax.axis_index("gy") - LOW
    mine = lane < 64

    def inside_y(y):
        at = first_y + y
        return ((at > 0) & (at < size_y)).astype(jnp.float32)

    def tile(ref, d, yc, xc, zc, y):
        row = (((d * 2 + yc) * 4 + xc * 2 + zc) * 9 + y) * 8
        return ref.at[pl.ds(pl.multiple_of(row, 8), 8), :]

    def point(y, p, h):
        main = points[pl.ds(pl.multiple_of(y * 128 + p * 8, 8), 8), :]
        side = points[pl.ds(pl.multiple_of(y * 128 + (PAIRS + h) * 8, 8), 8), :]
        if h:
            main = pltpu.roll(main, 64, 1)
        if p:
            side = pltpu.roll(side, 128 - 3 * p, 1)
        return jnp.where(mine, main, side)

    def put(ref, d, xc, zc, y, vertex, middle, wall):
        if (xc, zc) in inside:
            vertex = vertex * inside[xc, zc]
            middle = None if middle is None else middle * inside[xc, zc]
        tile(ref, d, 0, xc, zc, y)[...] = vertex * wall
        if middle is not None:
            tile(ref, d, 1, xc, zc, y)[...] = middle

    def force_row(y, carry):
        wall = inside_y(y)
        lines = {}
        for qy in range(3):
            value_z, slope_z = {}, {}
            for qx in range(3):
                q0, q1, q2 = (point(y, *class_of(3 * qx + qy, qz)) for qz in range(3))
                n0, n1, n2 = by_values(q0, q1, q2)
                value_z[qx, 0], value_z[qx, 1] = n0 + up_z(n2), n1
                n0, n1, n2 = by_slopes(q0, q1, q2)
                slope_z[qx, 0], slope_z[qx, 1] = n0 + up_z(n2), n1
            for d in range(3):
                source = slope_z if d == 2 else value_z
                op_x = by_slopes if d == 0 else by_values
                for zc in range(2):
                    n0, n1, n2 = op_x(*(source[qx, zc] for qx in range(3)))
                    lines[d, qy, 0, zc], lines[d, qy, 1, zc] = n0 + up_x(n2), n1
        kept = []
        for d in range(3):
            op_y = by_slopes if d == 1 else by_values
            for xc in range(2):
                for zc in range(2):
                    n0, n1, n2 = op_y(*(lines[d, qy, xc, zc] for qy in range(3)))
                    put(base, d, xc, zc, y, n0 + carry[len(kept)], n1, wall)
                    kept.append(n2)
        return tuple(kept)

    blank = jnp.zeros((8, 128), jnp.float32)
    lax.fori_loop(0, 9, force_row, (blank,) * 12, unroll=UNROLL[0])

    def mass_row(d, y, source, target, carry, rho, wanted):
        wall = inside_y(y)
        locals_y = {}
        for xc in range(2):
            for zc in range(2):
                got = element_op(
                    tile(source, d, 0, xc, zc, y)[...],
                    tile(source, d, 1, xc, zc, y)[...],
                    tile(source, d, 0, xc, zc, y + 1)[...],
                )
                for k in range(3):
                    locals_y[k, xc, zc] = got[k]
        kept = [None] * 4
        out = {}
        for k in wanted:
            lines = {}
            for xc in range(2):
                v, m = locals_y[k, xc, 0], locals_y[k, xc, 1]
                got = element_op(v, m, down_z(v))
                for j in range(3):
                    lines[j, xc] = got[j]
            joined = {}
            for j in range(3):
                v, m = lines[j, 0], lines[j, 1]
                n0, n1, n2 = (rho * n for n in element_op(v, m, down_x(v)))
                joined[j, 0], joined[j, 1] = n0 + up_x(n2), n1
            for xc in range(2):
                out[k, xc, 0] = joined[0, xc] + up_z(joined[2, xc])
                out[k, xc, 1] = joined[1, xc]
        for xc in range(2):
            for zc in range(2):
                slot = 2 * xc + zc
                if 0 in wanted:
                    middle = out.get((1, xc, zc))
                    put(target, d, xc, zc, y, out[0, xc, zc] + carry[slot], middle, wall)
                kept[slot] = out.get((2, xc, zc), blank)
        return tuple(kept)

    def mass(source, target, start, stop, last, unroll):
        def step(y, carry, wanted=(0, 1, 2)):
            rho = point(y, 13, 1) * (1.0 / 3375.0)
            kept = ()
            for d in range(3):
                kept += mass_row(d, y, source, target, carry[4 * d : 4 * d + 4], rho, wanted)
            return kept

        carry = step(start, (blank,) * 12, (2,))
        carry = lax.fori_loop(start + 1, stop - 1, step, carry, unroll=unroll)
        step(stop - 1, carry, last)

    mass(base, image, 1, 8, (0,), UNROLL[1])
    mass(image, second, 2, 7, (0, 1), UNROLL[2])

    mine_row = iota((4, 128), 1) < 64
    for f, ref in enumerate((base, image, second)):
        for d in range(3):
            for yc in range(2):
                for xc in range(2):
                    for x in range(2):
                        got = []
                        for zc in range(2):
                            at = (((d * 2 + yc) * 4 + xc * 2 + zc) * 9 + LOW) * 8 + LOW + x
                            got.append(ref[pl.ds(at, 4, stride=8), :])
                        line = jnp.where(mine_row, got[0], pltpu.roll(got[1], 64, 1))
                        place = ((f * 3 + d) * 4 + 2 * x + xc) * 8 + yc
                        flat[pl.ds(place, 4, stride=2), :] = line

    lines = []
    for d in range(3):
        v0, v1, v2 = (flat[96 * f + 32 * d : 96 * f + 32 * d + 32, :] for f in range(3))
        for product in (v0 * v0, v0 * v1, v1 * v1, v1 * v2):
            lines.append(jnp.sum(product, axis=0, keepdims=True))
    lines = jnp.sum(jnp.concatenate(lines, axis=0), axis=1, keepdims=True)
    row, col = iota((12, 128), 0), iota((12, 128), 1)
    sums = jnp.sum(jnp.where(row == col, lines, 0.0), axis=0, keepdims=True)
    if sums_out.ndim == 3:
        sums = sums[None]
    sums_out[...] = jnp.broadcast_to(sums, sums_out.shape)

    row, col = iota((128, 128), 0), iota((128, 128), 1)
    weave = row == (col % 2) * 64 + col // 2
    fields_out[...] = jnp.dot(
        flat[...],
        weave.astype(jnp.float32),
        precision=lax.Precision.HIGHEST,
        preferred_element_type=jnp.float32,
    )


def total_of(parts):
    if parts.ndim == 2:
        return jnp.sum(parts[...], axis=0, keepdims=True)
    rows = [parts[k] for k in range(parts.shape[0])]
    while len(rows) > 1:
        rows = [sum(rows[k : k + 2][1:], rows[k]) for k in range(0, len(rows), 2)]
    return rows[0]


def relay(parts, sums_out):
    sums = total_of(parts)
    if sums_out.ndim == 3:
        sums = sums[None]
    sums_out[...] = jnp.broadcast_to(sums, sums_out.shape)


def combine(fields, parts, acceleration_out, residual_out):
    sums = total_of(parts)
    for d in range(3):
        c0, c1, c2, c3 = (sums[:, 4 * d + k : 4 * d + k + 1] for k in range(4))
        alpha = c0 / c1
        norm = c0 - 2.0 * alpha * c1 + alpha * alpha * c2
        beta = norm / c0
        grow = 1.0 + beta
        alpha_2 = norm / (grow * grow * c1 - 2.0 * alpha * grow * c2 + alpha * alpha * c3)
        v0, v1, v2 = (fields[96 * f + 32 * d : 96 * f + 32 * d + 32, :] for f in range(3))
        direction = (v0 - alpha * v1) + beta * v0
        image = grow * v1 - alpha * v2
        acceleration_out[32 * d : 32 * d + 32, :] = alpha * v0 + alpha_2 * direction
        residual_out[32 * d : 32 * d + 32, :] = (v0 - alpha * v1) - alpha_2 * image


def moved(value, axes, by):
    pairs = [(i, i + by) for i in range(members(axes) - by)]
    return lax.ppermute(value, axes, pairs)


def swapped(value, axes):
    links = [(i, i + 1) for i in range(1, members(axes) - 1, 2)]
    return lax.ppermute(value, axes, links + [(b, a) for a, b in links])


def shape(*dims):
    return jax.ShapeDtypeStruct(dims, jnp.float32)


def call(body, outs, *operands, scratch=(), last=False, specs=None):
    kept = [pltpu.with_memory_space_constraint(o, pltpu.VMEM) for o in operands]
    place = (lambda o: o) if last else (lambda o: pltpu.VMEM(o.shape, o.dtype))
    return pl.pallas_call(
        body,
        out_shape=tuple(place(o) for o in outs),
        in_specs=vmem(len(operands)),
        out_specs=tuple(vmem(len(outs))),
        scratch_shapes=[pltpu.VMEM(dims, jnp.float32) for dims in scratch],
    )(*kept)


FIRST, SECOND = ("gx0", *GZ, "gx2"), ("gy", "gx1")


def members(axes):
    return math.prod(lax.axis_size(axis) for axis in axes)


def parts_shape(axes):
    count = members(axes)
    return shape(count, 128) if count % 8 == 0 else shape(count, 1, 128)


def exchange(value, axes):
    parts = lax.all_to_all(value.reshape(-1, 1, 128), axes, 0, 0)
    return parts.reshape(value.shape)


def on_device(sizes, energy, density, region, gamma_table):
    rows, message = pl.pallas_call(
        prepare,
        out_shape=(pltpu.VMEM((4, 32, 128), jnp.float32), pltpu.VMEM((16, 128), jnp.float32)),
        in_specs=vmem(3) + [pl.BlockSpec(memory_space=pltpu.SMEM)],
        out_specs=tuple(vmem(2)),
        scratch_shapes=[pltpu.VMEM((96, 192), jnp.float32), pltpu.VMEM((96, 256), jnp.float32)],
    )(energy, density, region, gamma_table)
    rows, slots = call(
        fill_z,
        (shape(4, 32, 128), shape(lax.axis_size("gy"), 32 * LOW, 128)),
        rows,
        lax.all_gather(message, GZ[1]),
        swapped(message, GZ),
    )
    own, last = call(
        fill_y,
        (shape(9, 32, 128), shape(9, 16, 128)),
        rows,
        lax.all_to_all(slots, "gy", 0, 0),
    )
    cross = swapped(own, GX)
    far = moved(last, GX, 2)
    pair = lax.all_gather(own, GX[2])
    grid = (3 * 2 * 4 * 9 * 8, 128)
    fields, sums = call(
        functools.partial(krylov, sizes),
        (shape(288, 128), parts_shape(FIRST)),
        own,
        pair,
        cross,
        far,
        scratch=((9 * 128, 128), grid, grid, grid, (288, 128)),
    )
    (sums,) = call(relay, (parts_shape(SECOND),), exchange(sums, FIRST))
    acceleration, residual = call(
        combine,
        (shape(96, 128), shape(96, 128)),
        fields,
        exchange(sums, SECOND),
        last=True,
    )
    return acceleration.reshape(3, 4, 8, 128), residual.reshape(3, 4, 8, 128)


def split(count):
    inner = 2
    middle = math.gcd(4, count // inner)
    return count // (inner * middle), middle, inner


def solution(mesh):
    count = mesh.shape["gx"]
    depth = mesh.shape["gz"]
    devices = mesh.devices.reshape(*split(count), mesh.shape["gy"], depth // 2, 2)
    finer = Mesh(devices, (*GX, "gy", *GZ))
    sizes = (2 * count, 4 * mesh.shape["gy"], 64 * depth)
    place = P(GX, "gy", GZ)
    out = P(None, GX, "gy", GZ)
    return jax.shard_map(
        functools.partial(on_device, sizes),
        mesh=finer,
        in_specs=(place, place, place, P()),
        out_specs=(out, out),
        check_vma=False,
    )
```

```python
import functools
import math

import jax
import jax.numpy as jnp
from jax import lax
from jax.experimental import pallas as pl
from jax.experimental.pallas import tpu as pltpu
from jax.sharding import Mesh
from jax.sharding import PartitionSpec as P

LOW, HIGH = 3, 2
PAIRS = 14
CORNERS = ((0, 0), (0, 1), (1, 0), (1, 1))
ROOT = math.sqrt(0.15)
EDGE_W, MID_W = 5.0 / 18.0, 8.0 / 18.0
UNROLL = (9, 5, 3, 9)
GX = ("gx0", "gx1", "gx2")
GZ = ("gz0", "gz1")


def vmem(count):
    return [pl.BlockSpec(memory_space=pltpu.VMEM)] * count


def selected(value, pick):
    pick = pick.astype(jnp.bfloat16)
    total = None
    for part in range(3):
        piece = value.astype(jnp.bfloat16)
        value = value - piece.astype(jnp.float32)
        got = jnp.dot(piece, pick, preferred_element_type=jnp.float32)
        total = got if total is None else total + got
    return total


def iota(shape, dim):
    return lax.broadcasted_iota(jnp.int32, shape, dim)


def class_of(q, qz):
    if qz < 2:
        return q, qz
    return (q + 9, 0) if q < 5 else (q + 4, 1)


def prepare(energy, density, region, gamma, rows_out, message_out, spread, lines):
    for point in range(6):
        spread[16 * point : 16 * point + 12, :] = energy[point]
    row, col = iota((192, 256), 0), iota((192, 256), 1)
    pick = row == 3 * (col % 64) + jnp.minimum(col // 64, 2)
    lines[...] = selected(spread[...], pick)
    rho = density[...]
    zone = region[...]
    table = jnp.zeros_like(rho)
    for index in range(3):
        table = table + jnp.where(zone == index, gamma[index], 0.0)
    scale = (table - 1.0) * rho
    scale = jnp.concatenate([scale, scale], axis=-1)
    rho = jnp.concatenate([rho, rho], axis=-1)
    low_half = iota((1, 128), 1) < 64
    pair, lane = iota((16, 128), 0), iota((16, 128), 1)
    real = pair < PAIRS
    start = (lane + 128 - 3 * pair) % 128
    keep_one = real & ((start >= 125) | ((start >= 64) & (start <= 65)))
    keep_zero = real & (((start >= 61) & (start <= 63)) | (start < 2))
    middle = iota((3, 128), 0) == 1
    line_w = jnp.where(middle, MID_W, EDGE_W)
    half_w = jnp.where(iota((3, 128), 1) < 64, EDGE_W, MID_W)
    weights = [line_w * half_w * w for w in (EDGE_W, MID_W, EDGE_W)]
    tail_weights = [line_w * EDGE_W * w for w in (EDGE_W, MID_W, EDGE_W)]
    for x in range(2):
        for y in range(4):
            factor = scale[x, y : y + 1]
            parts = []
            tails = []
            for qx in range(3):
                at = (3 * x + qx) * 16 + 3 * y
                parts.append(lines[at : at + 3, 0:128] * (factor * weights[qx]))
                tails.append(lines[at : at + 3, 128:256] * (factor * tail_weights[qx]))
            tail = [tails[q // 3][q % 3 : q % 3 + 1] for q in range(9)] + [rho[x, y : y + 1]]
            for i in range(5):
                parts.append(jnp.where(low_half, tail[i], tail[i + 5]))
            parts.append(jnp.zeros((2, 128), jnp.float32))
            base = 16 * x
            block = jnp.concatenate(parts, axis=0)
            rows_out[y, base : base + 16, :] = block
            turned = pltpu.roll(block, 0, 1, stride=3, stride_axis=0)
            zero = jnp.sum(jnp.where(keep_zero, turned, 0.0), axis=0, keepdims=True)
            one = jnp.sum(jnp.where(keep_one, turned, 0.0), axis=0, keepdims=True)
            place = y * 4 + x * 2
            message_out[place : place + 1, :] = pltpu.roll(zero, 64, 1)
            message_out[place + 1 : place + 2, :] = one


def fill_z(rows, even, odd, rows_out, slots_out):
    lane = iota((16, 128), 1)
    second = lax.axis_index(GZ[1]) == 1
    partner = even[1 - lax.axis_index(GZ[1])]
    from_low = jnp.where(second, partner, odd[...])
    from_high = jnp.where(second, odd[...], partner)
    halo = jnp.where((lane < 50) | (lane >= 110), from_low, from_high)
    me = lax.axis_index("gy")
    for y in range(4):
        blocks = []
        for x in range(2):
            base = 16 * x
            place = y * 4 + x * 2
            block = rows[y, base : base + 16, :]
            blocks.append(jnp.concatenate([block[:PAIRS], halo[place : place + 2]], axis=0))
        rows_out[y] = jnp.concatenate(blocks, axis=0)
    for to in range(slots_out.shape[0]):
        first = jnp.where(to > me, 1, 0)
        for k in range(LOW):
            slots_out[to, 32 * k : 32 * k + 32, :] = rows_out[first + k]


def fill_y(rows, slots, rows_out, last_out):
    me = lax.axis_index("gy")
    count = slots.shape[0]
    below = jnp.maximum(me - 1, 0)
    above = jnp.minimum(me + 1, count - 1)
    for y in range(LOW + 4 + HIGH):
        if y < LOW:
            block = slots[below, 32 * y : 32 * y + 32, :]
            block = jnp.where(me > 0, block, 0.0)
        elif y < LOW + 4:
            block = rows[y - LOW]
        else:
            at = 32 * (y - LOW - 4)
            block = slots[above, at : at + 32, :]
            block = jnp.where(me < count - 1, block, 0.0)
        rows_out[y] = block
        last_out[y] = block[16:32]


def element_op(v, m, w):
    total, gap = v + w, v - w
    outer = 0.75 * total + m
    inner = 1.25 * gap
    return outer + inner, total + 8.0 * m, outer - inner


def weighted_op(v, m, w, rhos):
    total, gap = v + w, v - w
    outer = rhos[1] * total + rhos[0] * m
    inner = rhos[2] * gap
    return outer + inner, rhos[0] * total + rhos[3] * m, outer - inner


def by_values(q0, q1, q2):
    total, gap = q0 + q2, q0 - q2
    outer, inner = 0.3 * total, ROOT * gap
    return outer + inner, 0.4 * total + q1, outer - inner


def by_slopes(q0, q1, q2):
    outer = (q0 + q2) + q1
    inner = (4.0 * ROOT) * (q0 - q2)
    return -outer - inner, 2.0 * inner, outer - inner


def up_z(value):
    return pltpu.roll(value, 1, 1)


def down_z(value):
    return pltpu.roll(value, 127, 1)


def up_x(value):
    return pltpu.roll(value, 1, 0)


def down_x(value):
    return pltpu.roll(value, 7, 0)


def krylov(sizes, own, pair, cross, far, fields_out, sums_out, points, ready, base, image, second, flat):
    size_x, size_y, size_z = sizes
    index_x = (lax.axis_index(GX[0]) * lax.axis_size(GX[1]) + lax.axis_index(GX[1])) * (
        lax.axis_size(GX[2])
    ) + lax.axis_index(GX[2])
    zeros = jnp.zeros((16, 128), jnp.float32)
    core = lax.axis_index(GX[2])
    for y in range(9):
        partner, distant = pair[1 - core, y], cross[y]
        near = jnp.where(core == 1, partner, distant)
        above = jnp.where(core == 1, distant, partner)
        sources = [
            far[y],
            near[0:16],
            near[16:32],
            own[y, 0:16],
            own[y, 16:32],
            above[0:16],
            above[16:32],
            zeros,
        ]
        for s in range(8):
            points[pl.ds(y * 128 + s, 16, stride=8), :] = sources[s]

    sub, lane = iota((8, 128), 0), iota((8, 128), 1)
    at_x = 2 * index_x + sub - LOW
    index_z = lax.axis_index(GZ[0]) * lax.axis_size(GZ[1]) + lax.axis_index(GZ[1])
    at_z = 64 * index_z + jnp.where(lane < 96, lane, lane - 128)
    inside_x = (at_x > 0) & (at_x < size_x)
    inside_z = (at_z > 0) & (at_z < size_z)
    inside = {
        (0, 0): (inside_x & inside_z).astype(jnp.float32),
        (0, 1): inside_x.astype(jnp.float32),
        (1, 0): inside_z.astype(jnp.float32),
    }
    first_y = 4 * lax.axis_index("gy") - LOW
    mine = lane < 64

    def inside_y(y):
        at = first_y + y
        return ((at > 0) & (at < size_y)).astype(jnp.float32)

    def tile(ref, d, yc, xc, zc, y):
        row = (((d * 2 + yc) * 4 + xc * 2 + zc) * 9 + y) * 8
        return ref.at[pl.ds(pl.multiple_of(row, 8), 8), :]

    def point(y, p, h):
        main = points[pl.ds(pl.multiple_of(y * 128 + p * 8, 8), 8), :]
        side = points[pl.ds(pl.multiple_of(y * 128 + (PAIRS + h) * 8, 8), 8), :]
        if h:
            main = pltpu.roll(main, 64, 1)
        if p:
            side = pltpu.roll(side, 128 - 3 * p, 1)
        return jnp.where(mine, main, side)

    def walls(y):
        wall = inside_y(y)
        return {at: inside[at] * wall if at in inside else wall for at in CORNERS}

    def put(ref, d, xc, zc, y, vertex, middle, wall):
        if (xc, zc) in inside:
            middle = None if middle is None else middle * inside[xc, zc]
        tile(ref, d, 0, xc, zc, y)[...] = vertex * wall[xc, zc]
        if middle is not None:
            tile(ref, d, 1, xc, zc, y)[...] = middle

    def ready_tile(y, q, qz):
        return ready.at[pl.ds(pl.multiple_of(y * 216 + (3 * q + qz) * 8, 8), 8), :]

    def unpack_row(y, carry):
        for q in range(9):
            for qz in range(3):
                ready_tile(y, q, qz)[...] = point(y, *class_of(q, qz))
        return carry

    lax.fori_loop(0, 9, unpack_row, 0, unroll=UNROLL[3])

    def force_row(y, carry):
        wall = walls(y)
        lines = {}
        for qy in range(3):
            value_z, slope_z = {}, {}
            for qx in range(3):
                q0, q1, q2 = (ready_tile(y, 3 * qx + qy, qz)[...] for qz in range(3))
                n0, n1, n2 = by_values(q0, q1, q2)
                value_z[qx, 0], value_z[qx, 1] = n0 + up_z(n2), n1
                n0, n1, n2 = by_slopes(q0, q1, q2)
                slope_z[qx, 0], slope_z[qx, 1] = n0 + up_z(n2), n1
            for d in range(3):
                source = slope_z if d == 2 else value_z
                op_x = by_slopes if d == 0 else by_values
                for zc in range(2):
                    n0, n1, n2 = op_x(*(source[qx, zc] for qx in range(3)))
                    lines[d, qy, 0, zc], lines[d, qy, 1, zc] = n0 + up_x(n2), n1
        kept = []
        for d in range(3):
            op_y = by_slopes if d == 1 else by_values
            for xc in range(2):
                for zc in range(2):
                    n0, n1, n2 = op_y(*(lines[d, qy, xc, zc] for qy in range(3)))
                    put(base, d, xc, zc, y, n0 + carry[len(kept)], n1, wall)
                    kept.append(n2)
        return tuple(kept)

    blank = jnp.zeros((8, 128), jnp.float32)
    lax.fori_loop(0, 9, force_row, (blank,) * 12, unroll=UNROLL[0])

    def mass_row(d, y, source, target, carry, rhos, wall, wanted):
        locals_y = {}
        for xc in range(2):
            for zc in range(2):
                got = element_op(
                    tile(source, d, 0, xc, zc, y)[...],
                    tile(source, d, 1, xc, zc, y)[...],
                    tile(source, d, 0, xc, zc, y + 1)[...],
                )
                for k in range(3):
                    locals_y[k, xc, zc] = got[k]
        kept = [None] * 4
        out = {}
        for k in wanted:
            lines = {}
            for xc in range(2):
                v, m = locals_y[k, xc, 0], locals_y[k, xc, 1]
                got = element_op(v, m, down_z(v))
                for j in range(3):
                    lines[j, xc] = got[j]
            joined = {}
            for j in range(3):
                v, m = lines[j, 0], lines[j, 1]
                n0, n1, n2 = weighted_op(v, m, down_x(v), rhos)
                joined[j, 0], joined[j, 1] = n0 + up_x(n2), n1
            for xc in range(2):
                out[k, xc, 0] = joined[0, xc] + up_z(joined[2, xc])
                out[k, xc, 1] = joined[1, xc]
        for xc in range(2):
            for zc in range(2):
                slot = 2 * xc + zc
                if 0 in wanted:
                    middle = out.get((1, xc, zc))
                    put(target, d, xc, zc, y, out[0, xc, zc] + carry[slot], middle, wall)
                kept[slot] = out.get((2, xc, zc), blank)
        return tuple(kept)

    def mass(source, target, start, stop, last, unroll):
        def step(y, carry, wanted=(0, 1, 2)):
            rho = point(y, 13, 1)
            rhos = [rho * (k / 3375.0) for k in (1.0, 0.75, 1.25, 8.0)]
            wall = walls(y)
            kept = ()
            for d in range(3):
                kept += mass_row(d, y, source, target, carry[4 * d : 4 * d + 4], rhos, wall, wanted)
            return kept

        carry = step(start, (blank,) * 12, (2,))
        carry = lax.fori_loop(start + 1, stop - 1, step, carry, unroll=unroll)
        step(stop - 1, carry, last)

    mass(base, image, 1, 8, (0,), UNROLL[1])
    mass(image, second, 2, 7, (0, 1), UNROLL[2])

    mine_row = iota((4, 128), 1) < 64
    for f, ref in enumerate((base, image, second)):
        for d in range(3):
            for yc in range(2):
                for xc in range(2):
                    for x in range(2):
                        got = []
                        for zc in range(2):
                            at = (((d * 2 + yc) * 4 + xc * 2 + zc) * 9 + LOW) * 8 + LOW + x
                            got.append(ref[pl.ds(at, 4, stride=8), :])
                        line = jnp.where(mine_row, got[0], pltpu.roll(got[1], 64, 1))
                        place = ((f * 3 + d) * 4 + 2 * x + xc) * 8 + yc
                        flat[pl.ds(place, 4, stride=2), :] = line

    lines = []
    for d in range(3):
        v0, v1, v2 = (flat[96 * f + 32 * d : 96 * f + 32 * d + 32, :] for f in range(3))
        for product in (v0 * v0, v0 * v1, v1 * v1, v1 * v2):
            lines.append(jnp.sum(product, axis=0, keepdims=True))
    lines = jnp.sum(jnp.concatenate(lines, axis=0), axis=1, keepdims=True)
    row, col = iota((12, 128), 0), iota((12, 128), 1)
    sums = jnp.sum(jnp.where(row == col, lines, 0.0), axis=0, keepdims=True)
    if sums_out.ndim == 3:
        sums = sums[None]
    sums_out[...] = jnp.broadcast_to(sums, sums_out.shape)

    row, col = iota((128, 128), 0), iota((128, 128), 1)
    weave = row == (col % 2) * 64 + col // 2
    fields_out[...] = jnp.dot(
        flat[...],
        weave.astype(jnp.float32),
        precision=lax.Precision.HIGHEST,
        preferred_element_type=jnp.float32,
    )


def total_of(parts):
    if parts.ndim == 2:
        return jnp.sum(parts[...], axis=0, keepdims=True)
    rows = [parts[k] for k in range(parts.shape[0])]
    while len(rows) > 1:
        rows = [sum(rows[k : k + 2][1:], rows[k]) for k in range(0, len(rows), 2)]
    return rows[0]


def relay(parts, sums_out):
    sums = total_of(parts)
    if sums_out.ndim == 3:
        sums = sums[None]
    sums_out[...] = jnp.broadcast_to(sums, sums_out.shape)


def combine(fields, parts, acceleration_out, residual_out):
    sums = total_of(parts)
    for d in range(3):
        c0, c1, c2, c3 = (sums[:, 4 * d + k : 4 * d + k + 1] for k in range(4))
        alpha = c0 / c1
        norm = c0 - 2.0 * alpha * c1 + alpha * alpha * c2
        beta = norm / c0
        grow = 1.0 + beta
        alpha_2 = norm / (grow * grow * c1 - 2.0 * alpha * grow * c2 + alpha * alpha * c3)
        v0, v1, v2 = (fields[96 * f + 32 * d : 96 * f + 32 * d + 32, :] for f in range(3))
        direction = (v0 - alpha * v1) + beta * v0
        image = grow * v1 - alpha * v2
        acceleration_out[32 * d : 32 * d + 32, :] = alpha * v0 + alpha_2 * direction
        residual_out[32 * d : 32 * d + 32, :] = (v0 - alpha * v1) - alpha_2 * image


def moved(value, axes, by):
    pairs = [(i, i + by) for i in range(members(axes) - by)]
    return lax.ppermute(value, axes, pairs)


def swapped(value, axes):
    links = [(i, i + 1) for i in range(1, members(axes) - 1, 2)]
    return lax.ppermute(value, axes, links + [(b, a) for a, b in links])


def shape(*dims):
    return jax.ShapeDtypeStruct(dims, jnp.float32)


def call(body, outs, *operands, scratch=(), last=False, specs=None):
    kept = [pltpu.with_memory_space_constraint(o, pltpu.VMEM) for o in operands]
    place = (lambda o: o) if last else (lambda o: pltpu.VMEM(o.shape, o.dtype))
    return pl.pallas_call(
        body,
        out_shape=tuple(place(o) for o in outs),
        in_specs=vmem(len(operands)),
        out_specs=tuple(vmem(len(outs))),
        scratch_shapes=[pltpu.VMEM(dims, jnp.float32) for dims in scratch],
    )(*kept)


FIRST, SECOND = ("gx0", *GZ, "gx2"), ("gy", "gx1")


def members(axes):
    return math.prod(lax.axis_size(axis) for axis in axes)


def parts_shape(axes):
    count = members(axes)
    return shape(count, 128) if count % 8 == 0 else shape(count, 1, 128)


def exchange(value, axes):
    parts = lax.all_to_all(value.reshape(-1, 1, 128), axes, 0, 0)
    return parts.reshape(value.shape)


def on_device(sizes, energy, density, region, gamma_table):
    rows, message = pl.pallas_call(
        prepare,
        out_shape=(pltpu.VMEM((4, 32, 128), jnp.float32), pltpu.VMEM((16, 128), jnp.float32)),
        in_specs=vmem(3) + [pl.BlockSpec(memory_space=pltpu.SMEM)],
        out_specs=tuple(vmem(2)),
        scratch_shapes=[pltpu.VMEM((96, 192), jnp.float32), pltpu.VMEM((96, 256), jnp.float32)],
    )(energy, density, region, gamma_table)
    rows, slots = call(
        fill_z,
        (shape(4, 32, 128), shape(lax.axis_size("gy"), 32 * LOW, 128)),
        rows,
        lax.all_gather(message, GZ[1]),
        swapped(message, GZ),
    )
    own, last = call(
        fill_y,
        (shape(9, 32, 128), shape(9, 16, 128)),
        rows,
        lax.all_to_all(slots, "gy", 0, 0),
    )
    cross = swapped(own, GX)
    far = moved(last, GX, 2)
    pair = lax.all_gather(own, GX[2])
    grid = (3 * 2 * 4 * 9 * 8, 128)
    fields, sums = call(
        functools.partial(krylov, sizes),
        (shape(288, 128), parts_shape(FIRST)),
        own,
        pair,
        cross,
        far,
        scratch=((9 * 128, 128), (9 * 216, 128), grid, grid, grid, (288, 128)),
    )
    (sums,) = call(relay, (parts_shape(SECOND),), exchange(sums, FIRST))
    acceleration, residual = call(
        combine,
        (shape(96, 128), shape(96, 128)),
        fields,
        exchange(sums, SECOND),
        last=True,
    )
    return acceleration.reshape(3, 4, 8, 128), residual.reshape(3, 4, 8, 128)


def split(count):
    inner = 2
    middle = math.gcd(4, count // inner)
    return count // (inner * middle), middle, inner


def solution(mesh):
    count = mesh.shape["gx"]
    depth = mesh.shape["gz"]
    devices = mesh.devices.reshape(*split(count), mesh.shape["gy"], depth // 2, 2)
    finer = Mesh(devices, (*GX, "gy", *GZ))
    sizes = (2 * count, 4 * mesh.shape["gy"], 64 * depth)
    place = P(GX, "gy", GZ)
    out = P(None, GX, "gy", GZ)
    return jax.shard_map(
        functools.partial(on_device, sizes),
        mesh=finer,
        in_specs=(place, place, place, P()),
        out_specs=(out, out),
        check_vma=False,
    )
```

```python
import functools
import math

import jax
import jax.numpy as jnp
from jax import lax
from jax.experimental import pallas as pl
from jax.experimental.pallas import tpu as pltpu
from jax.sharding import Mesh
from jax.sharding import PartitionSpec as P

LOW, HIGH = 3, 2
PAIRS = 14
ROOT = math.sqrt(0.15)
EDGE_W, MID_W = 5.0 / 18.0, 8.0 / 18.0
UNROLL = (3, 5, 3)
GX = ("gx0", "gx1", "gx2")
GZ = ("gz0", "gz1")


def vmem(count):
    return [pl.BlockSpec(memory_space=pltpu.VMEM)] * count


def selected(value, pick):
    pick = pick.astype(jnp.bfloat16)
    total = None
    for part in range(3):
        piece = value.astype(jnp.bfloat16)
        value = value - piece.astype(jnp.float32)
        got = jnp.dot(piece, pick, preferred_element_type=jnp.float32)
        total = got if total is None else total + got
    return total


def iota(shape, dim):
    return lax.broadcasted_iota(jnp.int32, shape, dim)


def class_of(q, qz):
    if qz < 2:
        return q, qz
    return (q + 9, 0) if q < 5 else (q + 4, 1)


def prepare(energy, density, region, gamma, rows_out, message_out, spread, lines):
    for point in range(6):
        spread[16 * point : 16 * point + 12, :] = energy[point]
    row, col = iota((192, 256), 0), iota((192, 256), 1)
    pick = row == 3 * (col % 64) + jnp.minimum(col // 64, 2)
    lines[...] = selected(spread[...], pick)
    rho = density[...]
    zone = region[...]
    table = jnp.zeros_like(rho)
    for index in range(3):
        table = table + jnp.where(zone == index, gamma[index], 0.0)
    scale = (table - 1.0) * rho
    scale = jnp.concatenate([scale, scale], axis=-1)
    rho = jnp.concatenate([rho, rho], axis=-1)
    low_half = iota((1, 128), 1) < 64
    pair, lane = iota((16, 128), 0), iota((16, 128), 1)
    real = pair < PAIRS
    start = (lane + 128 - 3 * pair) % 128
    keep_one = real & ((start >= 125) | ((start >= 64) & (start <= 65)))
    keep_zero = real & (((start >= 61) & (start <= 63)) | (start < 2))
    middle = iota((3, 128), 0) == 1
    line_w = jnp.where(middle, MID_W, EDGE_W)
    half_w = jnp.where(iota((3, 128), 1) < 64, EDGE_W, MID_W)
    weights = [line_w * half_w * w for w in (EDGE_W, MID_W, EDGE_W)]
    tail_weights = [line_w * EDGE_W * w for w in (EDGE_W, MID_W, EDGE_W)]
    for x in range(2):
        for y in range(4):
            factor = scale[x, y : y + 1]
            parts = []
            tails = []
            for qx in range(3):
                at = (3 * x + qx) * 16 + 3 * y
                parts.append(lines[at : at + 3, 0:128] * (factor * weights[qx]))
                tails.append(lines[at : at + 3, 128:256] * (factor * tail_weights[qx]))
            tail = [tails[q // 3][q % 3 : q % 3 + 1] for q in range(9)] + [rho[x, y : y + 1]]
            for i in range(5):
                parts.append(jnp.where(low_half, tail[i], tail[i + 5]))
            parts.append(jnp.zeros((2, 128), jnp.float32))
            base = 16 * x
            block = jnp.concatenate(parts, axis=0)
            rows_out[y, base : base + 16, :] = block
            turned = pltpu.roll(block, 0, 1, stride=3, stride_axis=0)
            zero = jnp.sum(jnp.where(keep_zero, turned, 0.0), axis=0, keepdims=True)
            one = jnp.sum(jnp.where(keep_one, turned, 0.0), axis=0, keepdims=True)
            place = y * 4 + x * 2
            message_out[place : place + 1, :] = pltpu.roll(zero, 64, 1)
            message_out[place + 1 : place + 2, :] = one


def fill_z(rows, even, odd, rows_out, slots_out):
    lane = iota((16, 128), 1)
    second = lax.axis_index(GZ[1]) == 1
    partner = even[1 - lax.axis_index(GZ[1])]
    from_low = jnp.where(second, partner, odd[...])
    from_high = jnp.where(second, odd[...], partner)
    halo = jnp.where((lane < 50) | (lane >= 110), from_low, from_high)
    me = lax.axis_index("gy")
    for y in range(4):
        blocks = []
        for x in range(2):
            base = 16 * x
            place = y * 4 + x * 2
            block = rows[y, base : base + 16, :]
            blocks.append(jnp.concatenate([block[:PAIRS], halo[place : place + 2]], axis=0))
        rows_out[y] = jnp.concatenate(blocks, axis=0)
    for to in range(slots_out.shape[0]):
        first = jnp.where(to > me, 1, 0)
        for k in range(LOW):
            slots_out[to, 32 * k : 32 * k + 32, :] = rows_out[first + k]


def fill_y(rows, slots, rows_out, last_out):
    me = lax.axis_index("gy")
    count = slots.shape[0]
    below = jnp.maximum(me - 1, 0)
    above = jnp.minimum(me + 1, count - 1)
    for y in range(LOW + 4 + HIGH):
        if y < LOW:
            block = slots[below, 32 * y : 32 * y + 32, :]
            block = jnp.where(me > 0, block, 0.0)
        elif y < LOW + 4:
            block = rows[y - LOW]
        else:
            at = 32 * (y - LOW - 4)
            block = slots[above, at : at + 32, :]
            block = jnp.where(me < count - 1, block, 0.0)
        rows_out[y] = block
        last_out[y] = block[16:32]


def element_op(v, m, w):
    total, gap = v + w, v - w
    outer = 0.75 * total + m
    inner = 1.25 * gap
    return outer + inner, total + 8.0 * m, outer - inner


def by_values(q0, q1, q2):
    total, gap = q0 + q2, q0 - q2
    outer, inner = 0.3 * total, ROOT * gap
    return outer + inner, 0.4 * total + q1, outer - inner


def by_slopes(q0, q1, q2):
    outer = (q0 + q2) + q1
    inner = (4.0 * ROOT) * (q0 - q2)
    return -outer - inner, 2.0 * inner, outer - inner


def up_z(value):
    return pltpu.roll(value, 1, 1)


def down_z(value):
    return pltpu.roll(value, 127, 1)


def up_x(value):
    return pltpu.roll(value, 1, 0)


def down_x(value):
    return pltpu.roll(value, 7, 0)


def krylov(sizes, own, pair, cross, far, fields_out, sums_out, points, base, image, second, flat):
    size_x, size_y, size_z = sizes
    index_x = (lax.axis_index(GX[0]) * lax.axis_size(GX[1]) + lax.axis_index(GX[1])) * (
        lax.axis_size(GX[2])
    ) + lax.axis_index(GX[2])
    zeros = jnp.zeros((16, 128), jnp.float32)
    core = lax.axis_index(GX[2])
    for y in range(9):
        partner, distant = pair[1 - core, y], cross[y]
        near = jnp.where(core == 1, partner, distant)
        above = jnp.where(core == 1, distant, partner)
        sources = [
            far[y],
            near[0:16],
            near[16:32],
            own[y, 0:16],
            own[y, 16:32],
            above[0:16],
            above[16:32],
            zeros,
        ]
        for s in range(8):
            points[pl.ds(y * 128 + s, 16, stride=8), :] = sources[s]

    sub, lane = iota((8, 128), 0), iota((8, 128), 1)
    at_x = 2 * index_x + sub - LOW
    index_z = lax.axis_index(GZ[0]) * lax.axis_size(GZ[1]) + lax.axis_index(GZ[1])
    at_z = 64 * index_z + jnp.where(lane < 96, lane, lane - 128)
    inside_x = (at_x > 0) & (at_x < size_x)
    inside_z = (at_z > 0) & (at_z < size_z)
    inside = {
        (0, 0): (inside_x & inside_z).astype(jnp.float32),
        (0, 1): inside_x.astype(jnp.float32),
        (1, 0): inside_z.astype(jnp.float32),
    }
    first_y = 4 * lax.axis_index("gy") - LOW
    mine = lane < 64

    def inside_y(y):
        at = first_y + y
        return ((at > 0) & (at < size_y)).astype(jnp.float32)

    def tile(ref, d, yc, xc, zc, y):
        row = (((d * 2 + yc) * 4 + xc * 2 + zc) * 9 + y) * 8
        return ref.at[pl.ds(pl.multiple_of(row, 8), 8), :]

    def point(y, p, h):
        main = points[pl.ds(pl.multiple_of(y * 128 + p * 8, 8), 8), :]
        side = points[pl.ds(pl.multiple_of(y * 128 + (PAIRS + h) * 8, 8), 8), :]
        if h:
            main = pltpu.roll(main, 64, 1)
        if p:
            side = pltpu.roll(side, 128 - 3 * p, 1)
        return jnp.where(mine, main, side)

    def put(ref, d, xc, zc, y, vertex, middle, wall):
        if (xc, zc) in inside:
            vertex = vertex * inside[xc, zc]
            middle = None if middle is None else middle * inside[xc, zc]
        tile(ref, d, 0, xc, zc, y)[...] = vertex * wall
        if middle is not None:
            tile(ref, d, 1, xc, zc, y)[...] = middle

    def force_row(y, carry):
        wall = inside_y(y)
        lines = {}
        for qy in range(3):
            value_z, slope_z = {}, {}
            for qx in range(3):
                q0, q1, q2 = (point(y, *class_of(3 * qx + qy, qz)) for qz in range(3))
                n0, n1, n2 = by_values(q0, q1, q2)
                value_z[qx, 0], value_z[qx, 1] = n0 + up_z(n2), n1
                n0, n1, n2 = by_slopes(q0, q1, q2)
                slope_z[qx, 0], slope_z[qx, 1] = n0 + up_z(n2), n1
            for d in range(3):
                source = slope_z if d == 2 else value_z
                op_x = by_slopes if d == 0 else by_values
                for zc in range(2):
                    n0, n1, n2 = op_x(*(source[qx, zc] for qx in range(3)))
                    lines[d, qy, 0, zc], lines[d, qy, 1, zc] = n0 + up_x(n2), n1
        kept = []
        for d in range(3):
            op_y = by_slopes if d == 1 else by_values
            for xc in range(2):
                for zc in range(2):
                    n0, n1, n2 = op_y(*(lines[d, qy, xc, zc] for qy in range(3)))
                    put(base, d, xc, zc, y, n0 + carry[len(kept)], n1, wall)
                    kept.append(n2)
        return tuple(kept)

    blank = jnp.zeros((8, 128), jnp.float32)
    lax.fori_loop(0, 9, force_row, (blank,) * 12, unroll=UNROLL[0])

    def mass_row(d, y, source, target, carry, rho, wanted):
        wall = inside_y(y)
        locals_y = {}
        for xc in range(2):
            for zc in range(2):
                got = element_op(
                    tile(source, d, 0, xc, zc, y)[...],
                    tile(source, d, 1, xc, zc, y)[...],
                    tile(source, d, 0, xc, zc, y + 1)[...],
                )
                for k in range(3):
                    locals_y[k, xc, zc] = got[k]
        kept = [None] * 4
        out = {}
        for k in wanted:
            lines = {}
            for xc in range(2):
                v, m = locals_y[k, xc, 0], locals_y[k, xc, 1]
                got = element_op(v, m, down_z(v))
                for j in range(3):
                    lines[j, xc] = got[j]
            joined = {}
            for j in range(3):
                v, m = lines[j, 0], lines[j, 1]
                n0, n1, n2 = (rho * n for n in element_op(v, m, down_x(v)))
                joined[j, 0], joined[j, 1] = n0 + up_x(n2), n1
            for xc in range(2):
                out[k, xc, 0] = joined[0, xc] + up_z(joined[2, xc])
                out[k, xc, 1] = joined[1, xc]
        for xc in range(2):
            for zc in range(2):
                slot = 2 * xc + zc
                if 0 in wanted:
                    middle = out.get((1, xc, zc))
                    put(target, d, xc, zc, y, out[0, xc, zc] + carry[slot], middle, wall)
                kept[slot] = out.get((2, xc, zc), blank)
        return tuple(kept)

    def mass(source, target, start, stop, last, unroll):
        def step(y, carry, wanted=(0, 1, 2)):
            rho = point(y, 13, 1) * (1.0 / 3375.0)
            kept = ()
            for d in range(3):
                kept += mass_row(d, y, source, target, carry[4 * d : 4 * d + 4], rho, wanted)
            return kept

        carry = step(start, (blank,) * 12, (2,))
        carry = lax.fori_loop(start + 1, stop - 1, step, carry, unroll=unroll)
        step(stop - 1, carry, last)

    mass(base, image, 1, 8, (0,), UNROLL[1])
    mass(image, second, 2, 7, (0, 1), UNROLL[2])

    mine_row = iota((4, 128), 1) < 64
    for f, ref in enumerate((base, image, second)):
        for d in range(3):
            for yc in range(2):
                for xc in range(2):
                    for x in range(2):
                        got = []
                        for zc in range(2):
                            at = (((d * 2 + yc) * 4 + xc * 2 + zc) * 9 + LOW) * 8 + LOW + x
                            got.append(ref[pl.ds(at, 4, stride=8), :])
                        line = jnp.where(mine_row, got[0], pltpu.roll(got[1], 64, 1))
                        place = ((f * 3 + d) * 4 + 2 * x + xc) * 8 + yc
                        flat[pl.ds(place, 4, stride=2), :] = line

    lines = []
    for d in range(3):
        v0, v1, v2 = (flat[96 * f + 32 * d : 96 * f + 32 * d + 32, :] for f in range(3))
        for product in (v0 * v0, v0 * v1, v1 * v1, v1 * v2):
            lines.append(jnp.sum(product, axis=0, keepdims=True))
    lines = jnp.sum(jnp.concatenate(lines, axis=0), axis=1, keepdims=True)
    row, col = iota((12, 128), 0), iota((12, 128), 1)
    sums = jnp.sum(jnp.where(row == col, lines, 0.0), axis=0, keepdims=True)
    if sums_out.ndim == 3:
        sums = sums[None]
    sums_out[...] = jnp.broadcast_to(sums, sums_out.shape)

    row, col = iota((128, 128), 0), iota((128, 128), 1)
    weave = row == (col % 2) * 64 + col // 2
    fields_out[...] = jnp.dot(
        flat[...],
        weave.astype(jnp.float32),
        precision=lax.Precision.HIGHEST,
        preferred_element_type=jnp.float32,
    )


def two_sum(a, b):
    total = a + b
    part = total - a
    return total, (a - (total - part)) + (b - part)


def two_product(a, b):
    total = a * b
    a_high, b_high = a * 4097.0, b * 4097.0
    a_high, b_high = a_high - (a_high - a), b_high - (b_high - b)
    a_low, b_low = a - a_high, b - b_high
    rest = ((a_high * b_high - total) + a_high * b_low + a_low * b_high) + a_low * b_low
    return total, rest


def added(a, b):
    total, rest = two_sum(a[0], b[0])
    return total, rest + (a[1] + b[1])


def determinant(a, b, c):
    p, p_rest = two_product(a[0], b[0])
    q, q_rest = two_product(c[0], c[0])
    p_rest = p_rest + (a[0] * b[1] + a[1] * b[0])
    q_rest = q_rest + 2.0 * (c[0] * c[1])
    total, rest = two_sum(p, -q)
    return total + (rest + (p_rest - q_rest))


def total_of(parts, corrected):
    if parts.ndim == 2:
        count = parts.shape[0]
        rows = [parts[k : k + 8, :] for k in range(0, count, 8)]
    else:
        rows = [parts[k] for k in range(parts.shape[0])]
    rows = [(row, pltpu.roll(row, 64, 1) if corrected else jnp.zeros_like(row)) for row in rows]
    while len(rows) > 1:
        ahead = [added(rows[k], rows[k + 1]) for k in range(0, len(rows) - 1, 2)]
        rows = ahead + rows[len(rows) - len(rows) % 2 :]
    total = rows[0]
    while total[0].shape[0] > 1:
        half = total[0].shape[0] // 2
        total = added(
            (total[0][:half], total[1][:half]), (total[0][half:], total[1][half:])
        )
    return total


def relay(parts, sums_out):
    value, rest = total_of(parts, False)
    lane = iota((1, 128), 1)
    sums = jnp.where(lane < 64, value, pltpu.roll(rest, 64, 1))
    if sums_out.ndim == 3:
        sums = sums[None]
    sums_out[...] = jnp.broadcast_to(sums, sums_out.shape)


def combine(fields, parts, acceleration_out, residual_out):
    sums = total_of(parts, True)
    c = [tuple(pltpu.roll(part, (128 - k) % 128, 1) if k else part for part in sums) for k in range(4)]
    upper, lower = determinant(c[0], c[2], c[1]), determinant(c[1], c[3], c[2])
    lane = iota((1, 128), 1)
    used = (lane < 12) & (lane % 4 == 0)
    c0, c1 = (jnp.where(used, c[k][0], 1.0) for k in range(2))
    lower = jnp.where(used, lower, 1.0)
    alphas = c0 / c1
    betas = upper / (c1 * c1)
    alphas_2 = (c1 * upper) / (c0 * lower)
    for d in range(3):
        alpha, beta, alpha_2 = (x[:, 4 * d : 4 * d + 1] for x in (alphas, betas, alphas_2))
        v0, v1, v2 = (fields[96 * f + 32 * d : 96 * f + 32 * d + 32, :] for f in range(3))
        first = v0 - alpha * v1
        direction = first + beta * v0
        image = (v1 + beta * v1) - alpha * v2
        acceleration_out[32 * d : 32 * d + 32, :] = alpha * v0 + alpha_2 * direction
        residual_out[32 * d : 32 * d + 32, :] = first - alpha_2 * image


def moved(value, axes, by):
    pairs = [(i, i + by) for i in range(members(axes) - by)]
    return lax.ppermute(value, axes, pairs)


def swapped(value, axes):
    links = [(i, i + 1) for i in range(1, members(axes) - 1, 2)]
    return lax.ppermute(value, axes, links + [(b, a) for a, b in links])


def shape(*dims):
    return jax.ShapeDtypeStruct(dims, jnp.float32)


def call(body, outs, *operands, scratch=(), last=False, specs=None):
    kept = [pltpu.with_memory_space_constraint(o, pltpu.VMEM) for o in operands]
    place = (lambda o: o) if last else (lambda o: pltpu.VMEM(o.shape, o.dtype))
    return pl.pallas_call(
        body,
        out_shape=tuple(place(o) for o in outs),
        in_specs=vmem(len(operands)),
        out_specs=tuple(vmem(len(outs))),
        scratch_shapes=[pltpu.VMEM(dims, jnp.float32) for dims in scratch],
    )(*kept)


FIRST, SECOND = ("gx0", *GZ, "gx2"), ("gy", "gx1")


def members(axes):
    return math.prod(lax.axis_size(axis) for axis in axes)


def parts_shape(axes):
    count = members(axes)
    return shape(count, 128) if count % 8 == 0 else shape(count, 1, 128)


def exchange(value, axes):
    parts = lax.all_to_all(value.reshape(-1, 1, 128), axes, 0, 0)
    return parts.reshape(value.shape)


def on_device(sizes, energy, density, region, gamma_table):
    rows, message = pl.pallas_call(
        prepare,
        out_shape=(pltpu.VMEM((4, 32, 128), jnp.float32), pltpu.VMEM((16, 128), jnp.float32)),
        in_specs=vmem(3) + [pl.BlockSpec(memory_space=pltpu.SMEM)],
        out_specs=tuple(vmem(2)),
        scratch_shapes=[pltpu.VMEM((96, 192), jnp.float32), pltpu.VMEM((96, 256), jnp.float32)],
    )(energy, density, region, gamma_table)
    rows, slots = call(
        fill_z,
        (shape(4, 32, 128), shape(lax.axis_size("gy"), 32 * LOW, 128)),
        rows,
        lax.all_gather(message, GZ[1]),
        swapped(message, GZ),
    )
    own, last = call(
        fill_y,
        (shape(9, 32, 128), shape(9, 16, 128)),
        rows,
        lax.all_to_all(slots, "gy", 0, 0),
    )
    cross = swapped(own, GX)
    far = moved(last, GX, 2)
    pair = lax.all_gather(own, GX[2])
    grid = (3 * 2 * 4 * 9 * 8, 128)
    fields, sums = call(
        functools.partial(krylov, sizes),
        (shape(288, 128), parts_shape(FIRST)),
        own,
        pair,
        cross,
        far,
        scratch=((9 * 128, 128), grid, grid, grid, (288, 128)),
    )
    (sums,) = call(relay, (parts_shape(SECOND),), exchange(sums, FIRST))
    acceleration, residual = call(
        combine,
        (shape(96, 128), shape(96, 128)),
        fields,
        exchange(sums, SECOND),
        last=True,
    )
    return acceleration.reshape(3, 4, 8, 128), residual.reshape(3, 4, 8, 128)


def split(count):
    inner = 2
    middle = math.gcd(4, count // inner)
    return count // (inner * middle), middle, inner


def solution(mesh):
    count = mesh.shape["gx"]
    depth = mesh.shape["gz"]
    devices = mesh.devices.reshape(*split(count), mesh.shape["gy"], depth // 2, 2)
    finer = Mesh(devices, (*GX, "gy", *GZ))
    sizes = (2 * count, 4 * mesh.shape["gy"], 64 * depth)
    place = P(GX, "gy", GZ)
    out = P(None, GX, "gy", GZ)
    return jax.shard_map(
        functools.partial(on_device, sizes),
        mesh=finer,
        in_specs=(place, place, place, P()),
        out_specs=(out, out),
        check_vma=False,
    )
```

```python
import functools
import math

import jax
import jax.numpy as jnp
from jax import lax
from jax.experimental import pallas as pl
from jax.experimental.pallas import tpu as pltpu
from jax.sharding import Mesh
from jax.sharding import PartitionSpec as P

LOW, HIGH = 3, 2
PAIRS = 14
ROOT = math.sqrt(0.15)
EDGE_W, MID_W = 5.0 / 18.0, 8.0 / 18.0
UNROLL = (3, 5, 3)
GX = ("gx0", "gx1", "gx2")
GZ = ("gz0", "gz1")


def vmem(count):
    return [pl.BlockSpec(memory_space=pltpu.VMEM)] * count


def selected(value, pick):
    pick = pick.astype(jnp.bfloat16)
    total = None
    for part in range(3):
        piece = value.astype(jnp.bfloat16)
        value = value - piece.astype(jnp.float32)
        got = jnp.dot(piece, pick, preferred_element_type=jnp.float32)
        total = got if total is None else total + got
    return total


def iota(shape, dim):
    return lax.broadcasted_iota(jnp.int32, shape, dim)


def class_of(q, qz):
    if qz < 2:
        return q, qz
    return (q + 9, 0) if q < 5 else (q + 4, 1)


def prepare(energy, density, region, gamma, rows_out, message_out, spread, lines):
    for point in range(6):
        spread[16 * point : 16 * point + 12, :] = energy[point]
    row, col = iota((192, 256), 0), iota((192, 256), 1)
    pick = row == 3 * (col % 64) + jnp.minimum(col // 64, 2)
    lines[...] = selected(spread[...], pick)
    rho = density[...]
    zone = region[...]
    table = jnp.zeros_like(rho)
    for index in range(3):
        table = table + jnp.where(zone == index, gamma[index], 0.0)
    scale = (table - 1.0) * rho
    scale = jnp.concatenate([scale, scale], axis=-1)
    rho = jnp.concatenate([rho, rho], axis=-1)
    low_half = iota((1, 128), 1) < 64
    pair, lane = iota((16, 128), 0), iota((16, 128), 1)
    real = pair < PAIRS
    start = (lane + 128 - 3 * pair) % 128
    keep_one = real & ((start >= 125) | ((start >= 64) & (start <= 65)))
    keep_zero = real & (((start >= 61) & (start <= 63)) | (start < 2))
    middle = iota((3, 128), 0) == 1
    line_w = jnp.where(middle, MID_W, EDGE_W)
    half_w = jnp.where(iota((3, 128), 1) < 64, EDGE_W, MID_W)
    weights = [line_w * half_w * w for w in (EDGE_W, MID_W, EDGE_W)]
    tail_weights = [line_w * EDGE_W * w for w in (EDGE_W, MID_W, EDGE_W)]
    for x in range(2):
        for y in range(4):
            factor = scale[x, y : y + 1]
            parts = []
            tails = []
            for qx in range(3):
                at = (3 * x + qx) * 16 + 3 * y
                parts.append(lines[at : at + 3, 0:128] * (factor * weights[qx]))
                tails.append(lines[at : at + 3, 128:256] * (factor * tail_weights[qx]))
            tail = [tails[q // 3][q % 3 : q % 3 + 1] for q in range(9)] + [rho[x, y : y + 1]]
            for i in range(5):
                parts.append(jnp.where(low_half, tail[i], tail[i + 5]))
            parts.append(jnp.zeros((2, 128), jnp.float32))
            base = 16 * x
            block = jnp.concatenate(parts, axis=0)
            rows_out[y, base : base + 16, :] = block
            turned = pltpu.roll(block, 0, 1, stride=3, stride_axis=0)
            zero = jnp.sum(jnp.where(keep_zero, turned, 0.0), axis=0, keepdims=True)
            one = jnp.sum(jnp.where(keep_one, turned, 0.0), axis=0, keepdims=True)
            place = y * 4 + x * 2
            message_out[place : place + 1, :] = pltpu.roll(zero, 64, 1)
            message_out[place + 1 : place + 2, :] = one


def fill_z(rows, even, odd, rows_out, slots_out):
    lane = iota((16, 128), 1)
    second = lax.axis_index(GZ[1]) == 1
    partner = even[1 - lax.axis_index(GZ[1])]
    from_low = jnp.where(second, partner, odd[...])
    from_high = jnp.where(second, odd[...], partner)
    halo = jnp.where((lane < 50) | (lane >= 110), from_low, from_high)
    me = lax.axis_index("gy")
    for y in range(4):
        blocks = []
        for x in range(2):
            base = 16 * x
            place = y * 4 + x * 2
            block = rows[y, base : base + 16, :]
            blocks.append(jnp.concatenate([block[:PAIRS], halo[place : place + 2]], axis=0))
        rows_out[y] = jnp.concatenate(blocks, axis=0)
    for to in range(slots_out.shape[0]):
        first = jnp.where(to > me, 1, 0)
        for k in range(LOW):
            slots_out[to, 32 * k : 32 * k + 32, :] = rows_out[first + k]


def fill_y(rows, slots, rows_out, last_out):
    me = lax.axis_index("gy")
    count = slots.shape[0]
    below = jnp.maximum(me - 1, 0)
    above = jnp.minimum(me + 1, count - 1)
    for y in range(LOW + 4 + HIGH):
        if y < LOW:
            block = slots[below, 32 * y : 32 * y + 32, :]
            block = jnp.where(me > 0, block, 0.0)
        elif y < LOW + 4:
            block = rows[y - LOW]
        else:
            at = 32 * (y - LOW - 4)
            block = slots[above, at : at + 32, :]
            block = jnp.where(me < count - 1, block, 0.0)
        rows_out[y] = block
        last_out[y] = block[16:32]


def element_op(v, m, w):
    total, gap = v + w, v - w
    outer = 0.75 * total + m
    inner = 1.25 * gap
    return outer + inner, total + 8.0 * m, outer - inner


def by_values(q0, q1, q2):
    total, gap = q0 + q2, q0 - q2
    outer, inner = 0.3 * total, ROOT * gap
    return outer + inner, 0.4 * total + q1, outer - inner


def by_slopes(q0, q1, q2):
    outer = (q0 + q2) + q1
    inner = (4.0 * ROOT) * (q0 - q2)
    return -outer - inner, 2.0 * inner, outer - inner


def up_z(value):
    return pltpu.roll(value, 1, 1)


def down_z(value):
    return pltpu.roll(value, 127, 1)


def up_x(value):
    return pltpu.roll(value, 1, 0)


def down_x(value):
    return pltpu.roll(value, 7, 0)


def krylov(sizes, own, pair, cross, far, fields_out, sums_out, points, base, image, second, flat):
    size_x, size_y, size_z = sizes
    index_x = (lax.axis_index(GX[0]) * lax.axis_size(GX[1]) + lax.axis_index(GX[1])) * (
        lax.axis_size(GX[2])
    ) + lax.axis_index(GX[2])
    zeros = jnp.zeros((16, 128), jnp.float32)
    core = lax.axis_index(GX[2])
    for y in range(9):
        partner, distant = pair[1 - core, y], cross[y]
        near = jnp.where(core == 1, partner, distant)
        above = jnp.where(core == 1, distant, partner)
        sources = [
            far[y],
            near[0:16],
            near[16:32],
            own[y, 0:16],
            own[y, 16:32],
            above[0:16],
            above[16:32],
            zeros,
        ]
        for s in range(8):
            points[pl.ds(y * 128 + s, 16, stride=8), :] = sources[s]

    sub, lane = iota((8, 128), 0), iota((8, 128), 1)
    at_x = 2 * index_x + sub - LOW
    index_z = lax.axis_index(GZ[0]) * lax.axis_size(GZ[1]) + lax.axis_index(GZ[1])
    at_z = 64 * index_z + jnp.where(lane < 96, lane, lane - 128)
    inside_x = (at_x > 0) & (at_x < size_x)
    inside_z = (at_z > 0) & (at_z < size_z)
    inside = {
        (0, 0): (inside_x & inside_z).astype(jnp.float32),
        (0, 1): inside_x.astype(jnp.float32),
        (1, 0): inside_z.astype(jnp.float32),
    }
    first_y = 4 * lax.axis_index("gy") - LOW
    mine = lane < 64

    def inside_y(y):
        at = first_y + y
        return ((at > 0) & (at < size_y)).astype(jnp.float32)

    def tile(ref, d, yc, xc, zc, y):
        row = (((d * 2 + yc) * 4 + xc * 2 + zc) * 9 + y) * 8
        return ref.at[pl.ds(pl.multiple_of(row, 8), 8), :]

    def point(y, p, h):
        main = points[pl.ds(pl.multiple_of(y * 128 + p * 8, 8), 8), :]
        side = points[pl.ds(pl.multiple_of(y * 128 + (PAIRS + h) * 8, 8), 8), :]
        if h:
            main = pltpu.roll(main, 64, 1)
        if p:
            side = pltpu.roll(side, 128 - 3 * p, 1)
        return jnp.where(mine, main, side)

    def put(ref, d, xc, zc, y, vertex, middle, wall):
        if (xc, zc) in inside:
            vertex = vertex * inside[xc, zc]
            middle = None if middle is None else middle * inside[xc, zc]
        tile(ref, d, 0, xc, zc, y)[...] = vertex * wall
        if middle is not None:
            tile(ref, d, 1, xc, zc, y)[...] = middle

    def force_row(y, carry):
        wall = inside_y(y)
        lines = {}
        for qy in range(3):
            value_z, slope_z = {}, {}
            for qx in range(3):
                q0, q1, q2 = (point(y, *class_of(3 * qx + qy, qz)) for qz in range(3))
                n0, n1, n2 = by_values(q0, q1, q2)
                value_z[qx, 0], value_z[qx, 1] = n0 + up_z(n2), n1
                n0, n1, n2 = by_slopes(q0, q1, q2)
                slope_z[qx, 0], slope_z[qx, 1] = n0 + up_z(n2), n1
            for d in range(3):
                source = slope_z if d == 2 else value_z
                op_x = by_slopes if d == 0 else by_values
                for zc in range(2):
                    n0, n1, n2 = op_x(*(source[qx, zc] for qx in range(3)))
                    lines[d, qy, 0, zc], lines[d, qy, 1, zc] = n0 + up_x(n2), n1
        kept = []
        for d in range(3):
            op_y = by_slopes if d == 1 else by_values
            for xc in range(2):
                for zc in range(2):
                    n0, n1, n2 = op_y(*(lines[d, qy, xc, zc] for qy in range(3)))
                    put(base, d, xc, zc, y, n0 + carry[len(kept)], n1, wall)
                    kept.append(n2)
        return tuple(kept)

    blank = jnp.zeros((8, 128), jnp.float32)
    lax.fori_loop(0, 9, force_row, (blank,) * 12, unroll=UNROLL[0])

    def mass_row(d, y, source, target, carry, rho, wanted):
        wall = inside_y(y)
        locals_y = {}
        for xc in range(2):
            for zc in range(2):
                got = element_op(
                    tile(source, d, 0, xc, zc, y)[...],
                    tile(source, d, 1, xc, zc, y)[...],
                    tile(source, d, 0, xc, zc, y + 1)[...],
                )
                for k in range(3):
                    locals_y[k, xc, zc] = got[k]
        kept = [None] * 4
        out = {}
        for k in wanted:
            lines = {}
            for xc in range(2):
                v, m = locals_y[k, xc, 0], locals_y[k, xc, 1]
                got = element_op(v, m, down_z(v))
                for j in range(3):
                    lines[j, xc] = got[j]
            joined = {}
            for j in range(3):
                v, m = lines[j, 0], lines[j, 1]
                n0, n1, n2 = (rho * n for n in element_op(v, m, down_x(v)))
                joined[j, 0], joined[j, 1] = n0 + up_x(n2), n1
            for xc in range(2):
                out[k, xc, 0] = joined[0, xc] + up_z(joined[2, xc])
                out[k, xc, 1] = joined[1, xc]
        for xc in range(2):
            for zc in range(2):
                slot = 2 * xc + zc
                if 0 in wanted:
                    middle = out.get((1, xc, zc))
                    put(target, d, xc, zc, y, out[0, xc, zc] + carry[slot], middle, wall)
                kept[slot] = out.get((2, xc, zc), blank)
        return tuple(kept)

    def mass(source, target, start, stop, last, unroll):
        def step(y, carry, wanted=(0, 1, 2)):
            rho = point(y, 13, 1) * (1.0 / 3375.0)
            kept = ()
            for d in range(3):
                kept += mass_row(d, y, source, target, carry[4 * d : 4 * d + 4], rho, wanted)
            return kept

        carry = step(start, (blank,) * 12, (2,))
        carry = lax.fori_loop(start + 1, stop - 1, step, carry, unroll=unroll)
        step(stop - 1, carry, last)

    mass(base, image, 1, 8, (0,), UNROLL[1])
    mass(image, second, 2, 7, (0, 1), UNROLL[2])

    mine_row = iota((4, 128), 1) < 64
    for f, ref in enumerate((base, image, second)):
        for d in range(3):
            for yc in range(2):
                for xc in range(2):
                    for x in range(2):
                        got = []
                        for zc in range(2):
                            at = (((d * 2 + yc) * 4 + xc * 2 + zc) * 9 + LOW) * 8 + LOW + x
                            got.append(ref[pl.ds(at, 4, stride=8), :])
                        line = jnp.where(mine_row, got[0], pltpu.roll(got[1], 64, 1))
                        place = ((f * 3 + d) * 4 + 2 * x + xc) * 8 + yc
                        flat[pl.ds(place, 4, stride=2), :] = line

    lines = []
    for d in range(3):
        v0, v1, v2 = (flat[96 * f + 32 * d : 96 * f + 32 * d + 32, :] for f in range(3))
        for product in (v0 * v0, v0 * v1, v1 * v1, v1 * v2):
            lines.append(jnp.sum(product, axis=0, keepdims=True))
    lines = jnp.sum(jnp.concatenate(lines, axis=0), axis=1, keepdims=True)
    row, col = iota((12, 128), 0), iota((12, 128), 1)
    sums = jnp.sum(jnp.where(row == col, lines, 0.0), axis=0, keepdims=True)
    if sums_out.ndim == 3:
        sums = sums[None]
    sums_out[...] = jnp.broadcast_to(sums, sums_out.shape)

    row, col = iota((128, 128), 0), iota((128, 128), 1)
    weave = row == (col % 2) * 64 + col // 2
    fields_out[...] = jnp.dot(
        flat[...],
        weave.astype(jnp.float32),
        precision=lax.Precision.HIGHEST,
        preferred_element_type=jnp.float32,
    )


def two_sum(a, b):
    total = a + b
    part = total - a
    return total, (a - (total - part)) + (b - part)


def two_product(a, b):
    total = a * b
    a_high, b_high = a * 4097.0, b * 4097.0
    a_high, b_high = a_high - (a_high - a), b_high - (b_high - b)
    a_low, b_low = a - a_high, b - b_high
    rest = ((a_high * b_high - total) + a_high * b_low + a_low * b_high) + a_low * b_low
    return total, rest


def added(a, b):
    total, rest = two_sum(a[0], b[0])
    return total, rest + (a[1] + b[1])


def determinant(a, b, c):
    p, p_rest = two_product(a[0], b[0])
    q, q_rest = two_product(c[0], c[0])
    p_rest = p_rest + (a[0] * b[1] + a[1] * b[0])
    q_rest = q_rest + 2.0 * (c[0] * c[1])
    total, rest = two_sum(p, -q)
    return total + (rest + (p_rest - q_rest))


def total_of(parts, corrected):
    if parts.ndim == 2:
        count = parts.shape[0]
        rows = [parts[k : k + 8, :] for k in range(0, count, 8)]
    else:
        rows = [parts[k] for k in range(parts.shape[0])]
    rows = [(row, pltpu.roll(row, 64, 1) if corrected else jnp.zeros_like(row)) for row in rows]
    while len(rows) > 1:
        ahead = [added(rows[k], rows[k + 1]) for k in range(0, len(rows) - 1, 2)]
        rows = ahead + rows[len(rows) - len(rows) % 2 :]
    total = rows[0]
    while total[0].shape[0] > 1:
        half = total[0].shape[0] // 2
        total = added(
            (total[0][:half], total[1][:half]), (total[0][half:], total[1][half:])
        )
    return total


def relay(parts, sums_out):
    value, rest = total_of(parts, False)
    lane = iota((1, 128), 1)
    sums = jnp.where(lane < 64, value, pltpu.roll(rest, 64, 1))
    if sums_out.ndim == 3:
        sums = sums[None]
    sums_out[...] = jnp.broadcast_to(sums, sums_out.shape)


def combine(fields, parts, acceleration_out, residual_out):
    sums = total_of(parts, True)
    c = [tuple(pltpu.roll(part, (128 - k) % 128, 1) if k else part for part in sums) for k in range(4)]
    upper, lower = determinant(c[0], c[2], c[1]), determinant(c[1], c[3], c[2])
    lane = iota((1, 128), 1)
    used = (lane < 12) & (lane % 4 == 0)
    c0, c1 = (jnp.where(used, c[k][0], 1.0) for k in range(2))
    lower = jnp.where(used, lower, 1.0)
    alphas = c0 / c1
    betas = upper / (c1 * c1)
    alphas_2 = (c1 * upper) / (c0 * lower)
    for d in range(3):
        alpha, beta, alpha_2 = (x[:, 4 * d : 4 * d + 1] for x in (alphas, betas, alphas_2))
        v0, v1, v2 = (fields[96 * f + 32 * d : 96 * f + 32 * d + 32, :] for f in range(3))
        first = v0 - alpha * v1
        direction = first + beta * v0
        image = (v1 + beta * v1) - alpha * v2
        acceleration_out[32 * d : 32 * d + 32, :] = alpha * v0 + alpha_2 * direction
        residual_out[32 * d : 32 * d + 32, :] = first - alpha_2 * image


def moved(value, axes, by):
    pairs = [(i, i + by) for i in range(members(axes) - by)]
    return lax.ppermute(value, axes, pairs)


def swapped(value, axes):
    links = [(i, i + 1) for i in range(1, members(axes) - 1, 2)]
    return lax.ppermute(value, axes, links + [(b, a) for a, b in links])


def shape(*dims):
    return jax.ShapeDtypeStruct(dims, jnp.float32)


def call(body, outs, *operands, scratch=(), last=False, specs=None):
    kept = [pltpu.with_memory_space_constraint(o, pltpu.VMEM) for o in operands]
    place = (lambda o: o) if last else (lambda o: pltpu.VMEM(o.shape, o.dtype))
    return pl.pallas_call(
        body,
        out_shape=tuple(place(o) for o in outs),
        in_specs=vmem(len(operands)),
        out_specs=tuple(vmem(len(outs))),
        scratch_shapes=[pltpu.VMEM(dims, jnp.float32) for dims in scratch],
    )(*kept)


FIRST, SECOND = ("gy", "gx1", "gx2"), ("gx0", *GZ)


def members(axes):
    return math.prod(lax.axis_size(axis) for axis in axes)


def parts_shape(axes):
    count = members(axes)
    return shape(count, 128) if count % 8 == 0 else shape(count, 1, 128)


def exchange(value, axes):
    parts = lax.all_to_all(value.reshape(-1, 1, 128), axes, 0, 0)
    return parts.reshape(value.shape)


def on_device(sizes, energy, density, region, gamma_table):
    rows, message = pl.pallas_call(
        prepare,
        out_shape=(pltpu.VMEM((4, 32, 128), jnp.float32), pltpu.VMEM((16, 128), jnp.float32)),
        in_specs=vmem(3) + [pl.BlockSpec(memory_space=pltpu.SMEM)],
        out_specs=tuple(vmem(2)),
        scratch_shapes=[pltpu.VMEM((96, 192), jnp.float32), pltpu.VMEM((96, 256), jnp.float32)],
    )(energy, density, region, gamma_table)
    rows, slots = call(
        fill_z,
        (shape(4, 32, 128), shape(lax.axis_size("gy"), 32 * LOW, 128)),
        rows,
        lax.all_gather(message, GZ[1]),
        swapped(message, GZ),
    )
    own, last = call(
        fill_y,
        (shape(9, 32, 128), shape(9, 16, 128)),
        rows,
        lax.all_to_all(slots, "gy", 0, 0),
    )
    cross = swapped(own, GX)
    far = moved(last, GX, 2)
    pair = lax.all_gather(own, GX[2])
    grid = (3 * 2 * 4 * 9 * 8, 128)
    fields, sums = call(
        functools.partial(krylov, sizes),
        (shape(288, 128), parts_shape(FIRST)),
        own,
        pair,
        cross,
        far,
        scratch=((9 * 128, 128), grid, grid, grid, (288, 128)),
    )
    (sums,) = call(relay, (parts_shape(SECOND),), exchange(sums, FIRST))
    acceleration, residual = call(
        combine,
        (shape(96, 128), shape(96, 128)),
        fields,
        exchange(sums, SECOND),
        last=True,
    )
    return acceleration.reshape(3, 4, 8, 128), residual.reshape(3, 4, 8, 128)


def split(count):
    inner = 2
    middle = math.gcd(4, count // inner)
    return count // (inner * middle), middle, inner


def solution(mesh):
    count = mesh.shape["gx"]
    depth = mesh.shape["gz"]
    devices = mesh.devices.reshape(*split(count), mesh.shape["gy"], depth // 2, 2)
    finer = Mesh(devices, (*GX, "gy", *GZ))
    sizes = (2 * count, 4 * mesh.shape["gy"], 64 * depth)
    place = P(GX, "gy", GZ)
    out = P(None, GX, "gy", GZ)
    return jax.shard_map(
        functools.partial(on_device, sizes),
        mesh=finer,
        in_specs=(place, place, place, P()),
        out_specs=(out, out),
        check_vma=False,
    )
```

```python
import functools
import math

import jax
import jax.numpy as jnp
from jax import lax
from jax.experimental import pallas as pl
from jax.experimental.pallas import tpu as pltpu
from jax.sharding import Mesh
from jax.sharding import PartitionSpec as P

LOW, HIGH = 3, 2
PAIRS = 14
ROOT = math.sqrt(0.15)
EDGE_W, MID_W = 5.0 / 18.0, 8.0 / 18.0
UNROLL = (3, 1, 3)
GX = ("gx0", "gx1", "gx2")
GZ = ("gz0", "gz1")


def vmem(count):
    return [pl.BlockSpec(memory_space=pltpu.VMEM)] * count


def selected(value, pick):
    pick = pick.astype(jnp.bfloat16)
    total = None
    for part in range(3):
        piece = value.astype(jnp.bfloat16)
        value = value - piece.astype(jnp.float32)
        got = jnp.dot(piece, pick, preferred_element_type=jnp.float32)
        total = got if total is None else total + got
    return total


def iota(shape, dim):
    return lax.broadcasted_iota(jnp.int32, shape, dim)


def class_of(q, qz):
    if qz < 2:
        return q, qz
    return (q + 9, 0) if q < 5 else (q + 4, 1)


def prepare(energy, density, region, gamma, rows_out, message_out, spread, lines):
    for point in range(6):
        spread[16 * point : 16 * point + 12, :] = energy[point]
    row, col = iota((192, 256), 0), iota((192, 256), 1)
    pick = row == 3 * (col % 64) + jnp.minimum(col // 64, 2)
    lines[...] = selected(spread[...], pick)
    rho = density[...]
    zone = region[...]
    table = jnp.zeros_like(rho)
    for index in range(3):
        table = table + jnp.where(zone == index, gamma[index], 0.0)
    scale = (table - 1.0) * rho
    scale = jnp.concatenate([scale, scale], axis=-1)
    rho = jnp.concatenate([rho, rho], axis=-1)
    low_half = iota((1, 128), 1) < 64
    pair, lane = iota((16, 128), 0), iota((16, 128), 1)
    real = pair < PAIRS
    start = (lane + 128 - 3 * pair) % 128
    keep_one = real & ((start >= 125) | ((start >= 64) & (start <= 65)))
    keep_zero = real & (((start >= 61) & (start <= 63)) | (start < 2))
    middle = iota((3, 128), 0) == 1
    line_w = jnp.where(middle, MID_W, EDGE_W)
    half_w = jnp.where(iota((3, 128), 1) < 64, EDGE_W, MID_W)
    weights = [line_w * half_w * w for w in (EDGE_W, MID_W, EDGE_W)]
    tail_weights = [line_w * EDGE_W * w for w in (EDGE_W, MID_W, EDGE_W)]
    for x in range(2):
        for y in range(4):
            factor = scale[x, y : y + 1]
            parts = []
            tails = []
            for qx in range(3):
                at = (3 * x + qx) * 16 + 3 * y
                parts.append(lines[at : at + 3, 0:128] * (factor * weights[qx]))
                tails.append(lines[at : at + 3, 128:256] * (factor * tail_weights[qx]))
            tail = [tails[q // 3][q % 3 : q % 3 + 1] for q in range(9)] + [rho[x, y : y + 1]]
            for i in range(5):
                parts.append(jnp.where(low_half, tail[i], tail[i + 5]))
            parts.append(jnp.zeros((2, 128), jnp.float32))
            base = 16 * x
            block = jnp.concatenate(parts, axis=0)
            rows_out[y, base : base + 16, :] = block
            turned = pltpu.roll(block, 0, 1, stride=3, stride_axis=0)
            zero = jnp.sum(jnp.where(keep_zero, turned, 0.0), axis=0, keepdims=True)
            one = jnp.sum(jnp.where(keep_one, turned, 0.0), axis=0, keepdims=True)
            place = y * 4 + x * 2
            message_out[place : place + 1, :] = pltpu.roll(zero, 64, 1)
            message_out[place + 1 : place + 2, :] = one


def fill_z(rows, even, odd, rows_out, slots_out):
    lane = iota((16, 128), 1)
    second = lax.axis_index(GZ[1]) == 1
    partner = even[1 - lax.axis_index(GZ[1])]
    from_low = jnp.where(second, partner, odd[...])
    from_high = jnp.where(second, odd[...], partner)
    halo = jnp.where((lane < 50) | (lane >= 110), from_low, from_high)
    me = lax.axis_index("gy")
    for y in range(4):
        blocks = []
        for x in range(2):
            base = 16 * x
            place = y * 4 + x * 2
            block = rows[y, base : base + 16, :]
            blocks.append(jnp.concatenate([block[:PAIRS], halo[place : place + 2]], axis=0))
        rows_out[y] = jnp.concatenate(blocks, axis=0)
    for to in range(slots_out.shape[0]):
        first = jnp.where(to > me, 1, 0)
        for k in range(LOW):
            slots_out[to, 32 * k : 32 * k + 32, :] = rows_out[first + k]


def fill_y(rows, slots, rows_out, last_out):
    me = lax.axis_index("gy")
    count = slots.shape[0]
    below = jnp.maximum(me - 1, 0)
    above = jnp.minimum(me + 1, count - 1)
    for y in range(LOW + 4 + HIGH):
        if y < LOW:
            block = slots[below, 32 * y : 32 * y + 32, :]
            block = jnp.where(me > 0, block, 0.0)
        elif y < LOW + 4:
            block = rows[y - LOW]
        else:
            at = 32 * (y - LOW - 4)
            block = slots[above, at : at + 32, :]
            block = jnp.where(me < count - 1, block, 0.0)
        rows_out[y] = block
        last_out[y] = block[16:32]


def element_op(v, m, w):
    total, gap = v + w, v - w
    outer = 0.75 * total + m
    inner = 1.25 * gap
    return outer + inner, total + 8.0 * m, outer - inner


def by_values(q0, q1, q2):
    total, gap = q0 + q2, q0 - q2
    outer, inner = 0.3 * total, ROOT * gap
    return outer + inner, 0.4 * total + q1, outer - inner


def by_slopes(q0, q1, q2):
    outer = (q0 + q2) + q1
    inner = (4.0 * ROOT) * (q0 - q2)
    return -outer - inner, 2.0 * inner, outer - inner


def up_z(value):
    return pltpu.roll(value, 1, 1)


def down_z(value):
    return pltpu.roll(value, 127, 1)


def up_x(value):
    return pltpu.roll(value, 1, 0)


def down_x(value):
    return pltpu.roll(value, 7, 0)


def krylov(sizes, own, pair, cross, far, fields_out, sums_out, points, base, image, second, flat):
    size_x, size_y, size_z = sizes
    index_x = (lax.axis_index(GX[0]) * lax.axis_size(GX[1]) + lax.axis_index(GX[1])) * (
        lax.axis_size(GX[2])
    ) + lax.axis_index(GX[2])
    zeros = jnp.zeros((16, 128), jnp.float32)
    core = lax.axis_index(GX[2])
    for y in range(9):
        partner, distant = pair[1 - core, y], cross[y]
        near = jnp.where(core == 1, partner, distant)
        above = jnp.where(core == 1, distant, partner)
        sources = [
            far[y],
            near[0:16],
            near[16:32],
            own[y, 0:16],
            own[y, 16:32],
            above[0:16],
            above[16:32],
            zeros,
        ]
        for s in range(8):
            points[pl.ds(y * 128 + s, 16, stride=8), :] = sources[s]

    sub, lane = iota((8, 128), 0), iota((8, 128), 1)
    at_x = 2 * index_x + sub - LOW
    index_z = lax.axis_index(GZ[0]) * lax.axis_size(GZ[1]) + lax.axis_index(GZ[1])
    at_z = 64 * index_z + jnp.where(lane < 96, lane, lane - 128)
    inside_x = (at_x > 0) & (at_x < size_x)
    inside_z = (at_z > 0) & (at_z < size_z)
    inside = {
        (0, 0): (inside_x & inside_z).astype(jnp.float32),
        (0, 1): inside_x.astype(jnp.float32),
        (1, 0): inside_z.astype(jnp.float32),
    }
    first_y = 4 * lax.axis_index("gy") - LOW
    mine = lane < 64

    def inside_y(y):
        at = first_y + y
        return ((at > 0) & (at < size_y)).astype(jnp.float32)

    def tile(ref, d, yc, xc, zc, y):
        row = (((d * 2 + yc) * 4 + xc * 2 + zc) * 9 + y) * 8
        return ref.at[pl.ds(pl.multiple_of(row, 8), 8), :]

    def point(y, p, h):
        main = points[pl.ds(pl.multiple_of(y * 128 + p * 8, 8), 8), :]
        side = points[pl.ds(pl.multiple_of(y * 128 + (PAIRS + h) * 8, 8), 8), :]
        if h:
            main = pltpu.roll(main, 64, 1)
        if p:
            side = pltpu.roll(side, 128 - 3 * p, 1)
        return jnp.where(mine, main, side)

    def put(ref, d, xc, zc, y, vertex, middle, wall):
        if (xc, zc) in inside:
            vertex = vertex * inside[xc, zc]
            middle = None if middle is None else middle * inside[xc, zc]
        tile(ref, d, 0, xc, zc, y)[...] = vertex * wall
        if middle is not None:
            tile(ref, d, 1, xc, zc, y)[...] = middle

    def force_row(y, carry):
        wall = inside_y(y)
        lines = {}
        for qy in range(3):
            value_z, slope_z = {}, {}
            for qx in range(3):
                q0, q1, q2 = (point(y, *class_of(3 * qx + qy, qz)) for qz in range(3))
                n0, n1, n2 = by_values(q0, q1, q2)
                value_z[qx, 0], value_z[qx, 1] = n0 + up_z(n2), n1
                n0, n1, n2 = by_slopes(q0, q1, q2)
                slope_z[qx, 0], slope_z[qx, 1] = n0 + up_z(n2), n1
            for d in range(3):
                source = slope_z if d == 2 else value_z
                op_x = by_slopes if d == 0 else by_values
                for zc in range(2):
                    n0, n1, n2 = op_x(*(source[qx, zc] for qx in range(3)))
                    lines[d, qy, 0, zc], lines[d, qy, 1, zc] = n0 + up_x(n2), n1
        kept = []
        for d in range(3):
            op_y = by_slopes if d == 1 else by_values
            for xc in range(2):
                for zc in range(2):
                    n0, n1, n2 = op_y(*(lines[d, qy, xc, zc] for qy in range(3)))
                    put(base, d, xc, zc, y, n0 + carry[len(kept)], n1, wall)
                    kept.append(n2)
        return tuple(kept)

    blank = jnp.zeros((8, 128), jnp.float32)
    lax.fori_loop(0, 9, force_row, (blank,) * 12, unroll=UNROLL[0])

    def mass_row(d, y, source, target, carry, rho, wanted):
        wall = inside_y(y)
        locals_y = {}
        for xc in range(2):
            for zc in range(2):
                got = element_op(
                    tile(source, d, 0, xc, zc, y)[...],
                    tile(source, d, 1, xc, zc, y)[...],
                    tile(source, d, 0, xc, zc, y + 1)[...],
                )
                for k in range(3):
                    locals_y[k, xc, zc] = got[k]
        kept = [None] * 4
        out = {}
        for k in wanted:
            lines = {}
            for xc in range(2):
                v, m = locals_y[k, xc, 0], locals_y[k, xc, 1]
                got = element_op(v, m, down_z(v))
                for j in range(3):
                    lines[j, xc] = got[j]
            joined = {}
            for j in range(3):
                v, m = lines[j, 0], lines[j, 1]
                n0, n1, n2 = (rho * n for n in element_op(v, m, down_x(v)))
                joined[j, 0], joined[j, 1] = n0 + up_x(n2), n1
            for xc in range(2):
                out[k, xc, 0] = joined[0, xc] + up_z(joined[2, xc])
                out[k, xc, 1] = joined[1, xc]
        for xc in range(2):
            for zc in range(2):
                slot = 2 * xc + zc
                if 0 in wanted:
                    middle = out.get((1, xc, zc))
                    put(target, d, xc, zc, y, out[0, xc, zc] + carry[slot], middle, wall)
                kept[slot] = out.get((2, xc, zc), blank)
        return tuple(kept)

    def mass(source, target, start, stop, last, unroll):
        def step(y, carry, wanted=(0, 1, 2)):
            rho = point(y, 13, 1) * (1.0 / 3375.0)
            kept = ()
            for d in range(3):
                kept += mass_row(d, y, source, target, carry[4 * d : 4 * d + 4], rho, wanted)
            return kept

        carry = step(start, (blank,) * 12, (2,))
        carry = lax.fori_loop(start + 1, stop - 1, step, carry, unroll=unroll)
        step(stop - 1, carry, last)

    mass(base, image, 1, 8, (0,), UNROLL[1])
    mass(image, second, 2, 7, (0, 1), UNROLL[2])

    mine_row = iota((4, 128), 1) < 64
    for f, ref in enumerate((base, image, second)):
        for d in range(3):
            for yc in range(2):
                for xc in range(2):
                    for x in range(2):
                        got = []
                        for zc in range(2):
                            at = (((d * 2 + yc) * 4 + xc * 2 + zc) * 9 + LOW) * 8 + LOW + x
                            got.append(ref[pl.ds(at, 4, stride=8), :])
                        line = jnp.where(mine_row, got[0], pltpu.roll(got[1], 64, 1))
                        place = ((f * 3 + d) * 4 + 2 * x + xc) * 8 + yc
                        flat[pl.ds(place, 4, stride=2), :] = line

    lines = []
    for d in range(3):
        v0, v1, v2 = (flat[96 * f + 32 * d : 96 * f + 32 * d + 32, :] for f in range(3))
        for product in (v0 * v0, v0 * v1, v1 * v1, v1 * v2):
            lines.append(jnp.sum(product, axis=0, keepdims=True))
    lines = jnp.sum(jnp.concatenate(lines, axis=0), axis=1, keepdims=True)
    row, col = iota((12, 128), 0), iota((12, 128), 1)
    sums = jnp.sum(jnp.where(row == col, lines, 0.0), axis=0, keepdims=True)
    if sums_out.ndim == 3:
        sums = sums[None]
    sums_out[...] = jnp.broadcast_to(sums, sums_out.shape)

    row, col = iota((128, 128), 0), iota((128, 128), 1)
    weave = row == (col % 2) * 64 + col // 2
    fields_out[...] = jnp.dot(
        flat[...],
        weave.astype(jnp.float32),
        precision=lax.Precision.HIGHEST,
        preferred_element_type=jnp.float32,
    )


def two_sum(a, b):
    total = a + b
    part = total - a
    return total, (a - (total - part)) + (b - part)


def two_product(a, b):
    total = a * b
    a_high, b_high = a * 4097.0, b * 4097.0
    a_high, b_high = a_high - (a_high - a), b_high - (b_high - b)
    a_low, b_low = a - a_high, b - b_high
    rest = ((a_high * b_high - total) + a_high * b_low + a_low * b_high) + a_low * b_low
    return total, rest


def added(a, b):
    total, rest = two_sum(a[0], b[0])
    return total, rest + (a[1] + b[1])


def determinant(a, b, c):
    p, p_rest = two_product(a[0], b[0])
    q, q_rest = two_product(c[0], c[0])
    p_rest = p_rest + (a[0] * b[1] + a[1] * b[0])
    q_rest = q_rest + 2.0 * (c[0] * c[1])
    total, rest = two_sum(p, -q)
    return total + (rest + (p_rest - q_rest))


def total_of(parts, corrected):
    if parts.ndim == 2:
        count = parts.shape[0]
        rows = [parts[k : k + 8, :] for k in range(0, count, 8)]
    else:
        rows = [parts[k] for k in range(parts.shape[0])]
    rows = [(row, pltpu.roll(row, 64, 1) if corrected else jnp.zeros_like(row)) for row in rows]
    while len(rows) > 1:
        ahead = [added(rows[k], rows[k + 1]) for k in range(0, len(rows) - 1, 2)]
        rows = ahead + rows[len(rows) - len(rows) % 2 :]
    total = rows[0]
    while total[0].shape[0] > 1:
        half = total[0].shape[0] // 2
        total = added(
            (total[0][:half], total[1][:half]), (total[0][half:], total[1][half:])
        )
    return total


def relay(parts, sums_out):
    value, rest = total_of(parts, False)
    lane = iota((1, 128), 1)
    sums = jnp.where(lane < 64, value, pltpu.roll(rest, 64, 1))
    if sums_out.ndim == 3:
        sums = sums[None]
    sums_out[...] = jnp.broadcast_to(sums, sums_out.shape)


def combine(fields, parts, acceleration_out, residual_out):
    sums = total_of(parts, True)
    c = [tuple(pltpu.roll(part, (128 - k) % 128, 1) if k else part for part in sums) for k in range(4)]
    upper, lower = determinant(c[0], c[2], c[1]), determinant(c[1], c[3], c[2])
    lane = iota((1, 128), 1)
    used = (lane < 12) & (lane % 4 == 0)
    c0, c1 = (jnp.where(used, c[k][0], 1.0) for k in range(2))
    lower = jnp.where(used, lower, 1.0)
    alphas = c0 / c1
    betas = upper / (c1 * c1)
    alphas_2 = (c1 * upper) / (c0 * lower)
    for d in range(3):
        alpha, beta, alpha_2 = (x[:, 4 * d : 4 * d + 1] for x in (alphas, betas, alphas_2))
        v0, v1, v2 = (fields[96 * f + 32 * d : 96 * f + 32 * d + 32, :] for f in range(3))
        first = v0 - alpha * v1
        direction = first + beta * v0
        image = (v1 + beta * v1) - alpha * v2
        acceleration_out[32 * d : 32 * d + 32, :] = alpha * v0 + alpha_2 * direction
        residual_out[32 * d : 32 * d + 32, :] = first - alpha_2 * image


def moved(value, axes, by):
    pairs = [(i, i + by) for i in range(members(axes) - by)]
    return lax.ppermute(value, axes, pairs)


def swapped(value, axes):
    links = [(i, i + 1) for i in range(1, members(axes) - 1, 2)]
    return lax.ppermute(value, axes, links + [(b, a) for a, b in links])


def shape(*dims):
    return jax.ShapeDtypeStruct(dims, jnp.float32)


def call(body, outs, *operands, scratch=(), last=False, specs=None):
    kept = [pltpu.with_memory_space_constraint(o, pltpu.VMEM) for o in operands]
    place = (lambda o: o) if last else (lambda o: pltpu.VMEM(o.shape, o.dtype))
    return pl.pallas_call(
        body,
        out_shape=tuple(place(o) for o in outs),
        in_specs=vmem(len(operands)),
        out_specs=tuple(vmem(len(outs))),
        scratch_shapes=[pltpu.VMEM(dims, jnp.float32) for dims in scratch],
    )(*kept)


FIRST, SECOND = ("gx0", *GZ, "gx2"), ("gy", "gx1")


def members(axes):
    return math.prod(lax.axis_size(axis) for axis in axes)


def parts_shape(axes):
    count = members(axes)
    return shape(count, 128) if count % 8 == 0 else shape(count, 1, 128)


def exchange(value, axes):
    parts = lax.all_to_all(value.reshape(-1, 1, 128), axes, 0, 0)
    return parts.reshape(value.shape)


def on_device(sizes, energy, density, region, gamma_table):
    rows, message = pl.pallas_call(
        prepare,
        out_shape=(pltpu.VMEM((4, 32, 128), jnp.float32), pltpu.VMEM((16, 128), jnp.float32)),
        in_specs=vmem(3) + [pl.BlockSpec(memory_space=pltpu.SMEM)],
        out_specs=tuple(vmem(2)),
        scratch_shapes=[pltpu.VMEM((96, 192), jnp.float32), pltpu.VMEM((96, 256), jnp.float32)],
    )(energy, density, region, gamma_table)
    rows, slots = call(
        fill_z,
        (shape(4, 32, 128), shape(lax.axis_size("gy"), 32 * LOW, 128)),
        rows,
        lax.all_gather(message, GZ[1]),
        swapped(message, GZ),
    )
    own, last = call(
        fill_y,
        (shape(9, 32, 128), shape(9, 16, 128)),
        rows,
        lax.all_to_all(slots, "gy", 0, 0),
    )
    cross = swapped(own, GX)
    far = moved(last, GX, 2)
    pair = lax.all_gather(own, GX[2])
    grid = (3 * 2 * 4 * 9 * 8, 128)
    fields, sums = call(
        functools.partial(krylov, sizes),
        (shape(288, 128), parts_shape(FIRST)),
        own,
        pair,
        cross,
        far,
        scratch=((9 * 128, 128), grid, grid, grid, (288, 128)),
    )
    (sums,) = call(relay, (parts_shape(SECOND),), exchange(sums, FIRST))
    acceleration, residual = call(
        combine,
        (shape(96, 128), shape(96, 128)),
        fields,
        exchange(sums, SECOND),
        last=True,
    )
    return acceleration.reshape(3, 4, 8, 128), residual.reshape(3, 4, 8, 128)


def split(count):
    inner = 2
    middle = math.gcd(4, count // inner)
    return count // (inner * middle), middle, inner


def solution(mesh):
    count = mesh.shape["gx"]
    depth = mesh.shape["gz"]
    devices = mesh.devices.reshape(*split(count), mesh.shape["gy"], depth // 2, 2)
    finer = Mesh(devices, (*GX, "gy", *GZ))
    sizes = (2 * count, 4 * mesh.shape["gy"], 64 * depth)
    place = P(GX, "gy", GZ)
    out = P(None, GX, "gy", GZ)
    return jax.shard_map(
        functools.partial(on_device, sizes),
        mesh=finer,
        in_specs=(place, place, place, P()),
        out_specs=(out, out),
        check_vma=False,
    )
```

```python
import functools
import math

import jax
import jax.numpy as jnp
from jax import lax
from jax.experimental import pallas as pl
from jax.experimental.pallas import tpu as pltpu
from jax.sharding import Mesh
from jax.sharding import PartitionSpec as P

LOW, HIGH = 3, 2
PAIRS = 14
ROOT = math.sqrt(0.15)
EDGE_W, MID_W = 5.0 / 18.0, 8.0 / 18.0
UNROLL = (3, 5, 3)
GX = ("gx0", "gx1", "gx2")
GZ = ("gz0", "gz1")


def vmem(count):
    return [pl.BlockSpec(memory_space=pltpu.VMEM)] * count


def selected(value, pick):
    pick = pick.astype(jnp.bfloat16)
    total = None
    for part in range(3):
        piece = value.astype(jnp.bfloat16)
        value = value - piece.astype(jnp.float32)
        got = jnp.dot(piece, pick, preferred_element_type=jnp.float32)
        total = got if total is None else total + got
    return total


def iota(shape, dim):
    return lax.broadcasted_iota(jnp.int32, shape, dim)


def class_of(q, qz):
    if qz < 2:
        return q, qz
    return (q + 9, 0) if q < 5 else (q + 4, 1)


def prepare(energy, density, region, gamma, rows_out, message_out, spread, lines):
    for point in range(6):
        spread[16 * point : 16 * point + 12, :] = energy[point]
    row, col = iota((192, 256), 0), iota((192, 256), 1)
    pick = row == 3 * (col % 64) + jnp.minimum(col // 64, 2)
    lines[...] = selected(spread[...], pick)
    rho = density[...]
    zone = region[...]
    table = jnp.zeros_like(rho)
    for index in range(3):
        table = table + jnp.where(zone == index, gamma[index], 0.0)
    scale = (table - 1.0) * rho
    scale = jnp.concatenate([scale, scale], axis=-1)
    rho = jnp.concatenate([rho, rho], axis=-1)
    low_half = iota((1, 128), 1) < 64
    pair, lane = iota((16, 128), 0), iota((16, 128), 1)
    real = pair < PAIRS
    start = (lane + 128 - 3 * pair) % 128
    keep_one = real & ((start >= 125) | ((start >= 64) & (start <= 65)))
    keep_zero = real & (((start >= 61) & (start <= 63)) | (start < 2))
    middle = iota((3, 128), 0) == 1
    line_w = jnp.where(middle, MID_W, EDGE_W)
    half_w = jnp.where(iota((3, 128), 1) < 64, EDGE_W, MID_W)
    weights = [line_w * half_w * w for w in (EDGE_W, MID_W, EDGE_W)]
    tail_weights = [line_w * EDGE_W * w for w in (EDGE_W, MID_W, EDGE_W)]
    for x in range(2):
        for y in range(4):
            factor = scale[x, y : y + 1]
            parts = []
            tails = []
            for qx in range(3):
                at = (3 * x + qx) * 16 + 3 * y
                parts.append(lines[at : at + 3, 0:128] * (factor * weights[qx]))
                tails.append(lines[at : at + 3, 128:256] * (factor * tail_weights[qx]))
            tail = [tails[q // 3][q % 3 : q % 3 + 1] for q in range(9)] + [rho[x, y : y + 1]]
            for i in range(5):
                parts.append(jnp.where(low_half, tail[i], tail[i + 5]))
            parts.append(jnp.zeros((2, 128), jnp.float32))
            base = 16 * x
            block = jnp.concatenate(parts, axis=0)
            rows_out[y, base : base + 16, :] = block
            turned = pltpu.roll(block, 0, 1, stride=3, stride_axis=0)
            zero = jnp.sum(jnp.where(keep_zero, turned, 0.0), axis=0, keepdims=True)
            one = jnp.sum(jnp.where(keep_one, turned, 0.0), axis=0, keepdims=True)
            place = y * 4 + x * 2
            message_out[place : place + 1, :] = pltpu.roll(zero, 64, 1)
            message_out[place + 1 : place + 2, :] = one


def fill_z(rows, even, odd, rows_out, slots_out):
    lane = iota((16, 128), 1)
    second = lax.axis_index(GZ[1]) == 1
    partner = even[1 - lax.axis_index(GZ[1])]
    from_low = jnp.where(second, partner, odd[...])
    from_high = jnp.where(second, odd[...], partner)
    halo = jnp.where((lane < 50) | (lane >= 110), from_low, from_high)
    me = lax.axis_index("gy")
    for y in range(4):
        blocks = []
        for x in range(2):
            base = 16 * x
            place = y * 4 + x * 2
            block = rows[y, base : base + 16, :]
            blocks.append(jnp.concatenate([block[:PAIRS], halo[place : place + 2]], axis=0))
        rows_out[y] = jnp.concatenate(blocks, axis=0)
    for to in range(slots_out.shape[0]):
        first = jnp.where(to > me, 1, 0)
        for k in range(LOW):
            slots_out[to, 32 * k : 32 * k + 32, :] = rows_out[first + k]


def fill_y(rows, slots, rows_out, last_out):
    me = lax.axis_index("gy")
    count = slots.shape[0]
    below = jnp.maximum(me - 1, 0)
    above = jnp.minimum(me + 1, count - 1)
    for y in range(LOW + 4 + HIGH):
        if y < LOW:
            block = slots[below, 32 * y : 32 * y + 32, :]
            block = jnp.where(me > 0, block, 0.0)
        elif y < LOW + 4:
            block = rows[y - LOW]
        else:
            at = 32 * (y - LOW - 4)
            block = slots[above, at : at + 32, :]
            block = jnp.where(me < count - 1, block, 0.0)
        rows_out[y] = block
        last_out[y] = block[16:32]


def element_op(v, m, w):
    total, gap = v + w, v - w
    outer = 0.75 * total + m
    inner = 1.25 * gap
    return outer + inner, total + 8.0 * m, outer - inner


def by_values(q0, q1, q2):
    total, gap = q0 + q2, q0 - q2
    outer, inner = 0.3 * total, ROOT * gap
    return outer + inner, 0.4 * total + q1, outer - inner


def by_slopes(q0, q1, q2):
    outer = (q0 + q2) + q1
    inner = (4.0 * ROOT) * (q0 - q2)
    return -outer - inner, 2.0 * inner, outer - inner


def up_z(value):
    return pltpu.roll(value, 1, 1)


def down_z(value):
    return pltpu.roll(value, 127, 1)


def up_x(value):
    return pltpu.roll(value, 1, 0)


def down_x(value):
    return pltpu.roll(value, 7, 0)


def krylov(sizes, own, pair, cross, far, fields_out, sums_out, points, base, image, second, flat):
    size_x, size_y, size_z = sizes
    index_x = (lax.axis_index(GX[0]) * lax.axis_size(GX[1]) + lax.axis_index(GX[1])) * (
        lax.axis_size(GX[2])
    ) + lax.axis_index(GX[2])
    zeros = jnp.zeros((16, 128), jnp.float32)
    core = lax.axis_index(GX[2])
    for y in range(9):
        partner, distant = pair[1 - core, y], cross[y]
        near = jnp.where(core == 1, partner, distant)
        above = jnp.where(core == 1, distant, partner)
        sources = [
            far[y],
            near[0:16],
            near[16:32],
            own[y, 0:16],
            own[y, 16:32],
            above[0:16],
            above[16:32],
            zeros,
        ]
        for s in range(8):
            points[pl.ds(y * 128 + s, 16, stride=8), :] = sources[s]

    sub, lane = iota((8, 128), 0), iota((8, 128), 1)
    at_x = 2 * index_x + sub - LOW
    index_z = lax.axis_index(GZ[0]) * lax.axis_size(GZ[1]) + lax.axis_index(GZ[1])
    at_z = 64 * index_z + jnp.where(lane < 96, lane, lane - 128)
    inside_x = (at_x > 0) & (at_x < size_x)
    inside_z = (at_z > 0) & (at_z < size_z)
    inside = {
        (0, 0): (inside_x & inside_z).astype(jnp.float32),
        (0, 1): inside_x.astype(jnp.float32),
        (1, 0): inside_z.astype(jnp.float32),
    }
    first_y = 4 * lax.axis_index("gy") - LOW
    mine = lane < 64

    def inside_y(y):
        at = first_y + y
        return ((at > 0) & (at < size_y)).astype(jnp.float32)

    def tile(ref, d, yc, xc, zc, y):
        row = (((d * 2 + yc) * 4 + xc * 2 + zc) * 9 + y) * 8
        return ref.at[pl.ds(pl.multiple_of(row, 8), 8), :]

    def point(y, p, h):
        main = points[pl.ds(pl.multiple_of(y * 128 + p * 8, 8), 8), :]
        side = points[pl.ds(pl.multiple_of(y * 128 + (PAIRS + h) * 8, 8), 8), :]
        if h:
            main = pltpu.roll(main, 64, 1)
        if p:
            side = pltpu.roll(side, 128 - 3 * p, 1)
        return jnp.where(mine, main, side)

    def put(ref, d, xc, zc, y, vertex, middle, wall):
        if (xc, zc) in inside:
            vertex = vertex * inside[xc, zc]
            middle = None if middle is None else middle * inside[xc, zc]
        tile(ref, d, 0, xc, zc, y)[...] = vertex * wall
        if middle is not None:
            tile(ref, d, 1, xc, zc, y)[...] = middle

    def force_row(y, carry):
        wall = inside_y(y)
        lines = {}
        for qy in range(3):
            value_z, slope_z = {}, {}
            for qx in range(3):
                q0, q1, q2 = (point(y, *class_of(3 * qx + qy, qz)) for qz in range(3))
                n0, n1, n2 = by_values(q0, q1, q2)
                value_z[qx, 0], value_z[qx, 1] = n0 + up_z(n2), n1
                n0, n1, n2 = by_slopes(q0, q1, q2)
                slope_z[qx, 0], slope_z[qx, 1] = n0 + up_z(n2), n1
            for d in range(3):
                source = slope_z if d == 2 else value_z
                op_x = by_slopes if d == 0 else by_values
                for zc in range(2):
                    n0, n1, n2 = op_x(*(source[qx, zc] for qx in range(3)))
                    lines[d, qy, 0, zc], lines[d, qy, 1, zc] = n0 + up_x(n2), n1
        kept = []
        for d in range(3):
            op_y = by_slopes if d == 1 else by_values
            for xc in range(2):
                for zc in range(2):
                    n0, n1, n2 = op_y(*(lines[d, qy, xc, zc] for qy in range(3)))
                    put(base, d, xc, zc, y, n0 + carry[len(kept)], n1, wall)
                    kept.append(n2)
        return tuple(kept)

    blank = jnp.zeros((8, 128), jnp.float32)
    lax.fori_loop(0, 9, force_row, (blank,) * 12, unroll=UNROLL[0])

    def mass_row(d, y, source, target, carry, rho, wanted):
        wall = inside_y(y)
        locals_y = {}
        for xc in range(2):
            for zc in range(2):
                got = element_op(
                    tile(source, d, 0, xc, zc, y)[...],
                    tile(source, d, 1, xc, zc, y)[...],
                    tile(source, d, 0, xc, zc, y + 1)[...],
                )
                for k in range(3):
                    locals_y[k, xc, zc] = got[k]
        kept = [None] * 4
        out = {}
        for k in wanted:
            lines = {}
            for xc in range(2):
                v, m = locals_y[k, xc, 0], locals_y[k, xc, 1]
                got = element_op(v, m, down_z(v))
                for j in range(3):
                    lines[j, xc] = got[j]
            joined = {}
            for j in range(3):
                v, m = lines[j, 0], lines[j, 1]
                n0, n1, n2 = (rho * n for n in element_op(v, m, down_x(v)))
                joined[j, 0], joined[j, 1] = n0 + up_x(n2), n1
            for xc in range(2):
                out[k, xc, 0] = joined[0, xc] + up_z(joined[2, xc])
                out[k, xc, 1] = joined[1, xc]
        for xc in range(2):
            for zc in range(2):
                slot = 2 * xc + zc
                if 0 in wanted:
                    middle = out.get((1, xc, zc))
                    put(target, d, xc, zc, y, out[0, xc, zc] + carry[slot], middle, wall)
                kept[slot] = out.get((2, xc, zc), blank)
        return tuple(kept)

    def mass(source, target, start, stop, last, unroll):
        def step(y, carry, wanted=(0, 1, 2)):
            rho = point(y, 13, 1) * (1.0 / 3375.0)
            kept = ()
            for d in range(3):
                kept += mass_row(d, y, source, target, carry[4 * d : 4 * d + 4], rho, wanted)
            return kept

        carry = step(start, (blank,) * 12, (2,))
        carry = lax.fori_loop(start + 1, stop - 1, step, carry, unroll=unroll)
        step(stop - 1, carry, last)

    mass(base, image, 1, 8, (0,), UNROLL[1])
    mass(image, second, 2, 7, (0, 1), UNROLL[2])

    mine_row = iota((4, 128), 1) < 64
    for f, ref in enumerate((base, image, second)):
        for d in range(3):
            for yc in range(2):
                for xc in range(2):
                    for x in range(2):
                        got = []
                        for zc in range(2):
                            at = (((d * 2 + yc) * 4 + xc * 2 + zc) * 9 + LOW) * 8 + LOW + x
                            got.append(ref[pl.ds(at, 4, stride=8), :])
                        line = jnp.where(mine_row, got[0], pltpu.roll(got[1], 64, 1))
                        place = ((f * 3 + d) * 4 + 2 * x + xc) * 8 + yc
                        flat[pl.ds(place, 4, stride=2), :] = line

    lines = []
    for d in range(3):
        v0, v1, v2 = (flat[96 * f + 32 * d : 96 * f + 32 * d + 32, :] for f in range(3))
        for product in (v0 * v0, v0 * v1, v1 * v1, v1 * v2):
            lines.append(jnp.sum(product, axis=0, keepdims=True))
    lines = jnp.sum(jnp.concatenate(lines, axis=0), axis=1, keepdims=True)
    row, col = iota((12, 128), 0), iota((12, 128), 1)
    sums = jnp.sum(jnp.where(row == col, lines, 0.0), axis=0, keepdims=True)
    if sums_out.ndim == 3:
        sums = sums[None]
    sums_out[...] = jnp.broadcast_to(sums, sums_out.shape)

    row, col = iota((128, 128), 0), iota((128, 128), 1)
    weave = row == (col % 2) * 64 + col // 2
    fields_out[...] = jnp.dot(
        flat[...],
        weave.astype(jnp.float32),
        precision=lax.Precision.HIGHEST,
        preferred_element_type=jnp.float32,
    )


def two_sum(a, b):
    total = a + b
    part = total - a
    return total, (a - (total - part)) + (b - part)


def two_product(a, b):
    total = a * b
    a_high, b_high = a * 4097.0, b * 4097.0
    a_high, b_high = a_high - (a_high - a), b_high - (b_high - b)
    a_low, b_low = a - a_high, b - b_high
    rest = ((a_high * b_high - total) + a_high * b_low + a_low * b_high) + a_low * b_low
    return total, rest


def added(a, b):
    total, rest = two_sum(a[0], b[0])
    return total, rest + (a[1] + b[1])


def determinant(a, b, c):
    p, p_rest = two_product(a[0], b[0])
    q, q_rest = two_product(c[0], c[0])
    p_rest = p_rest + (a[0] * b[1] + a[1] * b[0])
    q_rest = q_rest + 2.0 * (c[0] * c[1])
    total, rest = two_sum(p, -q)
    return total + (rest + (p_rest - q_rest))


def total_of(parts, corrected):
    if parts.ndim == 2:
        count = parts.shape[0]
        rows = [parts[k : k + 8, :] for k in range(0, count, 8)]
    else:
        rows = [parts[k] for k in range(parts.shape[0])]
    rows = [(row, pltpu.roll(row, 64, 1) if corrected else jnp.zeros_like(row)) for row in rows]
    while len(rows) > 1:
        ahead = [added(rows[k], rows[k + 1]) for k in range(0, len(rows) - 1, 2)]
        rows = ahead + rows[len(rows) - len(rows) % 2 :]
    total = rows[0]
    while total[0].shape[0] > 1:
        half = total[0].shape[0] // 2
        total = added(
            (total[0][:half], total[1][:half]), (total[0][half:], total[1][half:])
        )
    return total


def relay(parts, sums_out):
    value, rest = total_of(parts, False)
    lane = iota((1, 128), 1)
    sums = jnp.where(lane < 64, value, pltpu.roll(rest, 64, 1))
    if sums_out.ndim == 3:
        sums = sums[None]
    sums_out[...] = jnp.broadcast_to(sums, sums_out.shape)


def combine(fields, parts, acceleration_out, residual_out):
    sums = total_of(parts, True)
    c = [tuple(pltpu.roll(part, (128 - k) % 128, 1) if k else part for part in sums) for k in range(4)]
    upper, lower = determinant(c[0], c[2], c[1]), determinant(c[1], c[3], c[2])
    lane = iota((1, 128), 1)
    used = (lane < 12) & (lane % 4 == 0)
    c0, c1 = (jnp.where(used, c[k][0], 1.0) for k in range(2))
    lower = jnp.where(used, lower, 1.0)
    alphas = c0 / c1
    betas = upper / (c1 * c1)
    alphas_2 = (c1 * upper) / (c0 * lower)
    for d in range(3):
        alpha, beta, alpha_2 = (x[:, 4 * d : 4 * d + 1] for x in (alphas, betas, alphas_2))
        v0, v1, v2 = (fields[96 * f + 32 * d : 96 * f + 32 * d + 32, :] for f in range(3))
        first = v0 - alpha * v1
        direction = first + beta * v0
        image = (v1 + beta * v1) - alpha * v2
        acceleration_out[32 * d : 32 * d + 32, :] = alpha * v0 + alpha_2 * direction
        residual_out[32 * d : 32 * d + 32, :] = first - alpha_2 * image


def moved(value, axes, by):
    pairs = [(i, i + by) for i in range(members(axes) - by)]
    return lax.ppermute(value, axes, pairs)


def swapped(value, axes):
    links = [(i, i + 1) for i in range(1, members(axes) - 1, 2)]
    return lax.ppermute(value, axes, links + [(b, a) for a, b in links])


def shape(*dims):
    return jax.ShapeDtypeStruct(dims, jnp.float32)


def call(body, outs, *operands, scratch=(), last=False, specs=None):
    kept = [pltpu.with_memory_space_constraint(o, pltpu.VMEM) for o in operands]
    place = (lambda o: o) if last else (lambda o: pltpu.VMEM(o.shape, o.dtype))
    return pl.pallas_call(
        body,
        out_shape=tuple(place(o) for o in outs),
        in_specs=vmem(len(operands)),
        out_specs=tuple(vmem(len(outs))),
        scratch_shapes=[pltpu.VMEM(dims, jnp.float32) for dims in scratch],
    )(*kept)


FIRST, SECOND = ("gy", "gx1"), ("gx0", *GZ, "gx2")


def members(axes):
    return math.prod(lax.axis_size(axis) for axis in axes)


def parts_shape(axes):
    count = members(axes)
    return shape(count, 128) if count % 8 == 0 else shape(count, 1, 128)


def exchange(value, axes):
    parts = lax.all_to_all(value.reshape(-1, 1, 128), axes, 0, 0)
    return parts.reshape(value.shape)


def on_device(sizes, energy, density, region, gamma_table):
    rows, message = pl.pallas_call(
        prepare,
        out_shape=(pltpu.VMEM((4, 32, 128), jnp.float32), pltpu.VMEM((16, 128), jnp.float32)),
        in_specs=vmem(3) + [pl.BlockSpec(memory_space=pltpu.SMEM)],
        out_specs=tuple(vmem(2)),
        scratch_shapes=[pltpu.VMEM((96, 192), jnp.float32), pltpu.VMEM((96, 256), jnp.float32)],
    )(energy, density, region, gamma_table)
    rows, slots = call(
        fill_z,
        (shape(4, 32, 128), shape(lax.axis_size("gy"), 32 * LOW, 128)),
        rows,
        lax.all_gather(message, GZ[1]),
        swapped(message, GZ),
    )
    own, last = call(
        fill_y,
        (shape(9, 32, 128), shape(9, 16, 128)),
        rows,
        lax.all_to_all(slots, "gy", 0, 0),
    )
    cross = swapped(own, GX)
    far = moved(last, GX, 2)
    pair = lax.all_gather(own, GX[2])
    grid = (3 * 2 * 4 * 9 * 8, 128)
    fields, sums = call(
        functools.partial(krylov, sizes),
        (shape(288, 128), parts_shape(FIRST)),
        own,
        pair,
        cross,
        far,
        scratch=((9 * 128, 128), grid, grid, grid, (288, 128)),
    )
    (sums,) = call(relay, (parts_shape(SECOND),), exchange(sums, FIRST))
    acceleration, residual = call(
        combine,
        (shape(96, 128), shape(96, 128)),
        fields,
        exchange(sums, SECOND),
        last=True,
    )
    return acceleration.reshape(3, 4, 8, 128), residual.reshape(3, 4, 8, 128)


def split(count):
    inner = 2
    middle = math.gcd(4, count // inner)
    return count // (inner * middle), middle, inner


def solution(mesh):
    count = mesh.shape["gx"]
    depth = mesh.shape["gz"]
    devices = mesh.devices.reshape(*split(count), mesh.shape["gy"], depth // 2, 2)
    finer = Mesh(devices, (*GX, "gy", *GZ))
    sizes = (2 * count, 4 * mesh.shape["gy"], 64 * depth)
    place = P(GX, "gy", GZ)
    out = P(None, GX, "gy", GZ)
    return jax.shard_map(
        functools.partial(on_device, sizes),
        mesh=finer,
        in_specs=(place, place, place, P()),
        out_specs=(out, out),
        check_vma=False,
    )
```

```python
import functools
import math

import jax
import jax.numpy as jnp
from jax import lax
from jax.experimental import pallas as pl
from jax.experimental.pallas import tpu as pltpu
from jax.sharding import Mesh
from jax.sharding import PartitionSpec as P

LOW, HIGH = 3, 2
PAIRS = 14
ROOT = math.sqrt(0.15)
EDGE_W, MID_W = 5.0 / 18.0, 8.0 / 18.0
UNROLL = (9, 5, 3)
GX = ("gx0", "gx1", "gx2")
GZ = ("gz0", "gz1")


def vmem(count):
    return [pl.BlockSpec(memory_space=pltpu.VMEM)] * count


def selected(value, pick):
    pick = pick.astype(jnp.bfloat16)
    total = None
    for part in range(3):
        piece = value.astype(jnp.bfloat16)
        value = value - piece.astype(jnp.float32)
        got = jnp.dot(piece, pick, preferred_element_type=jnp.float32)
        total = got if total is None else total + got
    return total


def iota(shape, dim):
    return lax.broadcasted_iota(jnp.int32, shape, dim)


def class_of(q, qz):
    if qz < 2:
        return q, qz
    return (q + 9, 0) if q < 5 else (q + 4, 1)


def prepare(energy, density, region, gamma, rows_out, message_out, spread, lines):
    for point in range(6):
        spread[16 * point : 16 * point + 12, :] = energy[point]
    row, col = iota((192, 256), 0), iota((192, 256), 1)
    pick = row == 3 * (col % 64) + jnp.minimum(col // 64, 2)
    lines[...] = selected(spread[...], pick)
    rho = density[...]
    zone = region[...]
    table = jnp.zeros_like(rho)
    for index in range(3):
        table = table + jnp.where(zone == index, gamma[index], 0.0)
    scale = (table - 1.0) * rho
    scale = jnp.concatenate([scale, scale], axis=-1)
    rho = jnp.concatenate([rho, rho], axis=-1)
    low_half = iota((1, 128), 1) < 64
    pair, lane = iota((16, 128), 0), iota((16, 128), 1)
    real = pair < PAIRS
    start = (lane + 128 - 3 * pair) % 128
    keep_one = real & ((start >= 125) | ((start >= 64) & (start <= 65)))
    keep_zero = real & (((start >= 61) & (start <= 63)) | (start < 2))
    middle = iota((3, 128), 0) == 1
    line_w = jnp.where(middle, MID_W, EDGE_W)
    half_w = jnp.where(iota((3, 128), 1) < 64, EDGE_W, MID_W)
    weights = [line_w * half_w * w for w in (EDGE_W, MID_W, EDGE_W)]
    tail_weights = [line_w * EDGE_W * w for w in (EDGE_W, MID_W, EDGE_W)]
    for x in range(2):
        for y in range(4):
            factor = scale[x, y : y + 1]
            parts = []
            tails = []
            for qx in range(3):
                at = (3 * x + qx) * 16 + 3 * y
                parts.append(lines[at : at + 3, 0:128] * (factor * weights[qx]))
                tails.append(lines[at : at + 3, 128:256] * (factor * tail_weights[qx]))
            tail = [tails[q // 3][q % 3 : q % 3 + 1] for q in range(9)] + [rho[x, y : y + 1]]
            for i in range(5):
                parts.append(jnp.where(low_half, tail[i], tail[i + 5]))
            parts.append(jnp.zeros((2, 128), jnp.float32))
            base = 16 * x
            block = jnp.concatenate(parts, axis=0)
            rows_out[y, base : base + 16, :] = block
            turned = pltpu.roll(block, 0, 1, stride=3, stride_axis=0)
            zero = jnp.sum(jnp.where(keep_zero, turned, 0.0), axis=0, keepdims=True)
            one = jnp.sum(jnp.where(keep_one, turned, 0.0), axis=0, keepdims=True)
            place = y * 4 + x * 2
            message_out[place : place + 1, :] = pltpu.roll(zero, 64, 1)
            message_out[place + 1 : place + 2, :] = one


def fill_z(rows, even, odd, rows_out, slots_out):
    lane = iota((16, 128), 1)
    second = lax.axis_index(GZ[1]) == 1
    partner = even[1 - lax.axis_index(GZ[1])]
    from_low = jnp.where(second, partner, odd[...])
    from_high = jnp.where(second, odd[...], partner)
    halo = jnp.where((lane < 50) | (lane >= 110), from_low, from_high)
    me = lax.axis_index("gy")
    for y in range(4):
        blocks = []
        for x in range(2):
            base = 16 * x
            place = y * 4 + x * 2
            block = rows[y, base : base + 16, :]
            blocks.append(jnp.concatenate([block[:PAIRS], halo[place : place + 2]], axis=0))
        rows_out[y] = jnp.concatenate(blocks, axis=0)
    for to in range(slots_out.shape[0]):
        first = jnp.where(to > me, 1, 0)
        for k in range(LOW):
            slots_out[to, 32 * k : 32 * k + 32, :] = rows_out[first + k]


def fill_y(rows, slots, rows_out, last_out):
    me = lax.axis_index("gy")
    count = slots.shape[0]
    below = jnp.maximum(me - 1, 0)
    above = jnp.minimum(me + 1, count - 1)
    for y in range(LOW + 4 + HIGH):
        if y < LOW:
            block = slots[below, 32 * y : 32 * y + 32, :]
            block = jnp.where(me > 0, block, 0.0)
        elif y < LOW + 4:
            block = rows[y - LOW]
        else:
            at = 32 * (y - LOW - 4)
            block = slots[above, at : at + 32, :]
            block = jnp.where(me < count - 1, block, 0.0)
        rows_out[y] = block
        last_out[y] = block[16:32]


def element_op(v, m, w):
    total, gap = v + w, v - w
    outer = 0.75 * total + m
    inner = 1.25 * gap
    return outer + inner, total + 8.0 * m, outer - inner


def by_values(q0, q1, q2):
    total, gap = q0 + q2, q0 - q2
    outer, inner = 0.3 * total, ROOT * gap
    return outer + inner, 0.4 * total + q1, outer - inner


def by_slopes(q0, q1, q2):
    outer = (q0 + q2) + q1
    inner = (4.0 * ROOT) * (q0 - q2)
    return -outer - inner, 2.0 * inner, outer - inner


def up_z(value):
    return pltpu.roll(value, 1, 1)


def down_z(value):
    return pltpu.roll(value, 127, 1)


def up_x(value):
    return pltpu.roll(value, 1, 0)


def down_x(value):
    return pltpu.roll(value, 7, 0)


def krylov(sizes, own, pair, cross, far, fields_out, sums_out, points, base, image, second, flat):
    size_x, size_y, size_z = sizes
    index_x = (lax.axis_index(GX[0]) * lax.axis_size(GX[1]) + lax.axis_index(GX[1])) * (
        lax.axis_size(GX[2])
    ) + lax.axis_index(GX[2])
    zeros = jnp.zeros((16, 128), jnp.float32)
    core = lax.axis_index(GX[2])
    for y in range(9):
        partner, distant = pair[1 - core, y], cross[y]
        near = jnp.where(core == 1, partner, distant)
        above = jnp.where(core == 1, distant, partner)
        sources = [
            far[y],
            near[0:16],
            near[16:32],
            own[y, 0:16],
            own[y, 16:32],
            above[0:16],
            above[16:32],
            zeros,
        ]
        for s in range(8):
            points[pl.ds(y * 128 + s, 16, stride=8), :] = sources[s]

    sub, lane = iota((8, 128), 0), iota((8, 128), 1)
    at_x = 2 * index_x + sub - LOW
    index_z = lax.axis_index(GZ[0]) * lax.axis_size(GZ[1]) + lax.axis_index(GZ[1])
    at_z = 64 * index_z + jnp.where(lane < 96, lane, lane - 128)
    inside_x = (at_x > 0) & (at_x < size_x)
    inside_z = (at_z > 0) & (at_z < size_z)
    inside = {
        (0, 0): (inside_x & inside_z).astype(jnp.float32),
        (0, 1): inside_x.astype(jnp.float32),
        (1, 0): inside_z.astype(jnp.float32),
    }
    first_y = 4 * lax.axis_index("gy") - LOW
    mine = lane < 64

    def inside_y(y):
        at = first_y + y
        return ((at > 0) & (at < size_y)).astype(jnp.float32)

    def tile(ref, d, yc, xc, zc, y):
        row = (((d * 2 + yc) * 4 + xc * 2 + zc) * 9 + y) * 8
        return ref.at[pl.ds(pl.multiple_of(row, 8), 8), :]

    def point(y, p, h):
        main = points[pl.ds(pl.multiple_of(y * 128 + p * 8, 8), 8), :]
        side = points[pl.ds(pl.multiple_of(y * 128 + (PAIRS + h) * 8, 8), 8), :]
        if h:
            main = pltpu.roll(main, 64, 1)
        if p:
            side = pltpu.roll(side, 128 - 3 * p, 1)
        return jnp.where(mine, main, side)

    def put(ref, d, xc, zc, y, vertex, middle, wall):
        if (xc, zc) in inside:
            vertex = vertex * inside[xc, zc]
            middle = None if middle is None else middle * inside[xc, zc]
        tile(ref, d, 0, xc, zc, y)[...] = vertex * wall
        if middle is not None:
            tile(ref, d, 1, xc, zc, y)[...] = middle

    def force_row(y, carry):
        wall = inside_y(y)
        lines = {}
        for qy in range(3):
            value_z, slope_z = {}, {}
            for qx in range(3):
                q0, q1, q2 = (point(y, *class_of(3 * qx + qy, qz)) for qz in range(3))
                n0, n1, n2 = by_values(q0, q1, q2)
                value_z[qx, 0], value_z[qx, 1] = n0 + up_z(n2), n1
                n0, n1, n2 = by_slopes(q0, q1, q2)
                slope_z[qx, 0], slope_z[qx, 1] = n0 + up_z(n2), n1
            for d in range(3):
                source = slope_z if d == 2 else value_z
                op_x = by_slopes if d == 0 else by_values
                for zc in range(2):
                    n0, n1, n2 = op_x(*(source[qx, zc] for qx in range(3)))
                    lines[d, qy, 0, zc], lines[d, qy, 1, zc] = n0 + up_x(n2), n1
        kept = []
        for d in range(3):
            op_y = by_slopes if d == 1 else by_values
            for xc in range(2):
                for zc in range(2):
                    n0, n1, n2 = op_y(*(lines[d, qy, xc, zc] for qy in range(3)))
                    put(base, d, xc, zc, y, n0 + carry[len(kept)], n1, wall)
                    kept.append(n2)
        return tuple(kept)

    blank = jnp.zeros((8, 128), jnp.float32)
    lax.fori_loop(0, 9, force_row, (blank,) * 12, unroll=UNROLL[0])

    def mass_row(d, y, source, target, carry, rho, wanted):
        wall = inside_y(y)
        locals_y = {}
        for xc in range(2):
            for zc in range(2):
                got = element_op(
                    tile(source, d, 0, xc, zc, y)[...],
                    tile(source, d, 1, xc, zc, y)[...],
                    tile(source, d, 0, xc, zc, y + 1)[...],
                )
                for k in range(3):
                    locals_y[k, xc, zc] = got[k]
        kept = [None] * 4
        out = {}
        for k in wanted:
            lines = {}
            for xc in range(2):
                v, m = locals_y[k, xc, 0], locals_y[k, xc, 1]
                got = element_op(v, m, down_z(v))
                for j in range(3):
                    lines[j, xc] = got[j]
            joined = {}
            for j in range(3):
                v, m = lines[j, 0], lines[j, 1]
                n0, n1, n2 = (rho * n for n in element_op(v, m, down_x(v)))
                joined[j, 0], joined[j, 1] = n0 + up_x(n2), n1
            for xc in range(2):
                out[k, xc, 0] = joined[0, xc] + up_z(joined[2, xc])
                out[k, xc, 1] = joined[1, xc]
        for xc in range(2):
            for zc in range(2):
                slot = 2 * xc + zc
                if 0 in wanted:
                    middle = out.get((1, xc, zc))
                    put(target, d, xc, zc, y, out[0, xc, zc] + carry[slot], middle, wall)
                kept[slot] = out.get((2, xc, zc), blank)
        return tuple(kept)

    def mass(source, target, start, stop, last, unroll):
        def step(y, carry, wanted=(0, 1, 2)):
            rho = point(y, 13, 1) * (1.0 / 3375.0)
            kept = ()
            for d in range(3):
                kept += mass_row(d, y, source, target, carry[4 * d : 4 * d + 4], rho, wanted)
            return kept

        carry = step(start, (blank,) * 12, (2,))
        carry = lax.fori_loop(start + 1, stop - 1, step, carry, unroll=unroll)
        step(stop - 1, carry, last)

    mass(base, image, 1, 8, (0,), UNROLL[1])
    mass(image, second, 2, 7, (0, 1), UNROLL[2])

    mine_row = iota((4, 128), 1) < 64
    for f, ref in enumerate((base, image, second)):
        for d in range(3):
            for yc in range(2):
                for xc in range(2):
                    for x in range(2):
                        got = []
                        for zc in range(2):
                            at = (((d * 2 + yc) * 4 + xc * 2 + zc) * 9 + LOW) * 8 + LOW + x
                            got.append(ref[pl.ds(at, 4, stride=8), :])
                        line = jnp.where(mine_row, got[0], pltpu.roll(got[1], 64, 1))
                        place = ((f * 3 + d) * 4 + 2 * x + xc) * 8 + yc
                        flat[pl.ds(place, 4, stride=2), :] = line

    lines = []
    for d in range(3):
        v0, v1, v2 = (flat[96 * f + 32 * d : 96 * f + 32 * d + 32, :] for f in range(3))
        for product in (v0 * v0, v0 * v1, v1 * v1, v1 * v2):
            lines.append(jnp.sum(product, axis=0, keepdims=True))
    lines = jnp.sum(jnp.concatenate(lines, axis=0), axis=1, keepdims=True)
    row, col = iota((12, 128), 0), iota((12, 128), 1)
    sums = jnp.sum(jnp.where(row == col, lines, 0.0), axis=0, keepdims=True)
    if sums_out.ndim == 3:
        sums = sums[None]
    sums_out[...] = jnp.broadcast_to(sums, sums_out.shape)

    row, col = iota((128, 128), 0), iota((128, 128), 1)
    weave = row == (col % 2) * 64 + col // 2
    fields_out[...] = jnp.dot(
        flat[...],
        weave.astype(jnp.float32),
        precision=lax.Precision.HIGHEST,
        preferred_element_type=jnp.float32,
    )


def two_sum(a, b):
    total = a + b
    part = total - a
    return total, (a - (total - part)) + (b - part)


def two_product(a, b):
    total = a * b
    a_high, b_high = a * 4097.0, b * 4097.0
    a_high, b_high = a_high - (a_high - a), b_high - (b_high - b)
    a_low, b_low = a - a_high, b - b_high
    rest = ((a_high * b_high - total) + a_high * b_low + a_low * b_high) + a_low * b_low
    return total, rest


def added(a, b):
    total, rest = two_sum(a[0], b[0])
    return total, rest + (a[1] + b[1])


def determinant(a, b, c):
    p, p_rest = two_product(a[0], b[0])
    q, q_rest = two_product(c[0], c[0])
    p_rest = p_rest + (a[0] * b[1] + a[1] * b[0])
    q_rest = q_rest + 2.0 * (c[0] * c[1])
    total, rest = two_sum(p, -q)
    return total + (rest + (p_rest - q_rest))


def total_of(parts, corrected):
    if parts.ndim == 2:
        count = parts.shape[0]
        rows = [parts[k : k + 8, :] for k in range(0, count, 8)]
    else:
        rows = [parts[k] for k in range(parts.shape[0])]
    rows = [(row, pltpu.roll(row, 64, 1) if corrected else jnp.zeros_like(row)) for row in rows]
    while len(rows) > 1:
        ahead = [added(rows[k], rows[k + 1]) for k in range(0, len(rows) - 1, 2)]
        rows = ahead + rows[len(rows) - len(rows) % 2 :]
    total = rows[0]
    while total[0].shape[0] > 1:
        half = total[0].shape[0] // 2
        total = added(
            (total[0][:half], total[1][:half]), (total[0][half:], total[1][half:])
        )
    return total


def relay(parts, sums_out):
    value, rest = total_of(parts, False)
    lane = iota((1, 128), 1)
    sums = jnp.where(lane < 64, value, pltpu.roll(rest, 64, 1))
    if sums_out.ndim == 3:
        sums = sums[None]
    sums_out[...] = jnp.broadcast_to(sums, sums_out.shape)


def combine(fields, parts, acceleration_out, residual_out):
    sums = total_of(parts, True)
    c = [tuple(pltpu.roll(part, (128 - k) % 128, 1) if k else part for part in sums) for k in range(4)]
    upper, lower = determinant(c[0], c[2], c[1]), determinant(c[1], c[3], c[2])
    lane = iota((1, 128), 1)
    used = (lane < 12) & (lane % 4 == 0)
    c0, c1 = (jnp.where(used, c[k][0], 1.0) for k in range(2))
    lower = jnp.where(used, lower, 1.0)
    alphas = c0 / c1
    betas = upper / (c1 * c1)
    alphas_2 = (c1 * upper) / (c0 * lower)
    for d in range(3):
        alpha, beta, alpha_2 = (x[:, 4 * d : 4 * d + 1] for x in (alphas, betas, alphas_2))
        v0, v1, v2 = (fields[96 * f + 32 * d : 96 * f + 32 * d + 32, :] for f in range(3))
        first = v0 - alpha * v1
        direction = first + beta * v0
        image = (v1 + beta * v1) - alpha * v2
        acceleration_out[32 * d : 32 * d + 32, :] = alpha * v0 + alpha_2 * direction
        residual_out[32 * d : 32 * d + 32, :] = first - alpha_2 * image


def moved(value, axes, by):
    pairs = [(i, i + by) for i in range(members(axes) - by)]
    return lax.ppermute(value, axes, pairs)


def swapped(value, axes):
    links = [(i, i + 1) for i in range(1, members(axes) - 1, 2)]
    return lax.ppermute(value, axes, links + [(b, a) for a, b in links])


def shape(*dims):
    return jax.ShapeDtypeStruct(dims, jnp.float32)


def call(body, outs, *operands, scratch=(), last=False, specs=None):
    kept = [pltpu.with_memory_space_constraint(o, pltpu.VMEM) for o in operands]
    place = (lambda o: o) if last else (lambda o: pltpu.VMEM(o.shape, o.dtype))
    return pl.pallas_call(
        body,
        out_shape=tuple(place(o) for o in outs),
        in_specs=vmem(len(operands)),
        out_specs=tuple(vmem(len(outs))),
        scratch_shapes=[pltpu.VMEM(dims, jnp.float32) for dims in scratch],
    )(*kept)


FIRST, SECOND = ("gx0", *GZ, "gx2"), ("gy", "gx1")


def members(axes):
    return math.prod(lax.axis_size(axis) for axis in axes)


def parts_shape(axes):
    count = members(axes)
    return shape(count, 128) if count % 8 == 0 else shape(count, 1, 128)


def exchange(value, axes):
    parts = lax.all_to_all(value.reshape(-1, 1, 128), axes, 0, 0)
    return parts.reshape(value.shape)


def on_device(sizes, energy, density, region, gamma_table):
    rows, message = pl.pallas_call(
        prepare,
        out_shape=(pltpu.VMEM((4, 32, 128), jnp.float32), pltpu.VMEM((16, 128), jnp.float32)),
        in_specs=vmem(3) + [pl.BlockSpec(memory_space=pltpu.SMEM)],
        out_specs=tuple(vmem(2)),
        scratch_shapes=[pltpu.VMEM((96, 192), jnp.float32), pltpu.VMEM((96, 256), jnp.float32)],
    )(energy, density, region, gamma_table)
    rows, slots = call(
        fill_z,
        (shape(4, 32, 128), shape(lax.axis_size("gy"), 32 * LOW, 128)),
        rows,
        lax.all_gather(message, GZ[1]),
        swapped(message, GZ),
    )
    own, last = call(
        fill_y,
        (shape(9, 32, 128), shape(9, 16, 128)),
        rows,
        lax.all_to_all(slots, "gy", 0, 0),
    )
    cross = swapped(own, GX)
    far = moved(last, GX, 2)
    pair = lax.all_gather(own, GX[2])
    grid = (3 * 2 * 4 * 9 * 8, 128)
    fields, sums = call(
        functools.partial(krylov, sizes),
        (shape(288, 128), parts_shape(FIRST)),
        own,
        pair,
        cross,
        far,
        scratch=((9 * 128, 128), grid, grid, grid, (288, 128)),
    )
    (sums,) = call(relay, (parts_shape(SECOND),), exchange(sums, FIRST))
    acceleration, residual = call(
        combine,
        (shape(96, 128), shape(96, 128)),
        fields,
        exchange(sums, SECOND),
        last=True,
    )
    return acceleration.reshape(3, 4, 8, 128), residual.reshape(3, 4, 8, 128)


def split(count):
    inner = 2
    middle = math.gcd(4, count // inner)
    return count // (inner * middle), middle, inner


def solution(mesh):
    count = mesh.shape["gx"]
    depth = mesh.shape["gz"]
    devices = mesh.devices.reshape(*split(count), mesh.shape["gy"], depth // 2, 2)
    finer = Mesh(devices, (*GX, "gy", *GZ))
    sizes = (2 * count, 4 * mesh.shape["gy"], 64 * depth)
    place = P(GX, "gy", GZ)
    out = P(None, GX, "gy", GZ)
    return jax.shard_map(
        functools.partial(on_device, sizes),
        mesh=finer,
        in_specs=(place, place, place, P()),
        out_specs=(out, out),
        check_vma=False,
    )
```
